128 devices in a mesh: req: 16 (over x, z), head: 8 (over y, core).
Axes of the slice: x: 4, y: 4, z: 4, core: 2. Of those that a mesh axis runs over, the one named last changes fastest.
Arguments:
- hidden_in: bfloat16 [16384, 1536], P(('req', 'head')), may hold values from -3 to 3
- attn_gain: float32 [1536], replicated, may hold values from 0.1 to 1.9
- w_query: bfloat16 [1536, 1536], P(None, 'head'), may hold values from -0.15625 to 0.15625
- keyvalue_weight: bfloat16 [1536, 8, 128], P(None, 'head'), may hold values from -0.3125 to 0.3125
- w_out: bfloat16 [1536, 1536], P('head'), may hold values from -0.375 to 0.375
- cache_kv: bfloat16 [64, 2048, 8, 128], P('req', None, 'head'), may hold values from -400 to 400
- ctx_len: int32 [64], replicated, may hold values from 2 to 2048, as said below
- span_len: int32 [16, 4], replicated, may hold values from 1 to 512, 1024 in all within a row
- ffn_gain: float32 [1536], replicated, may hold values from 0.1 to 1.9
- routes: int32 [16384, 8], P(('req', 'head')), may hold values from 0 to 31, all different within a row; in each aligned block of 128 rows (0 to 127, 128 to 255, ...) at most 48 rows name the same one
- gate_weights: bfloat16 [16384, 8], P(('req', 'head')), may hold values from 0.049804688 to 0.29882812
- w_gate_up: bfloat16 [32, 1536, 1024], P('req'), may hold values from -0.15625 to 0.15625
- w_down: bfloat16 [32, 512, 1536], P('req'), may hold values from -0.25 to 0.25
- req_prompt: int32 [288], P('req'), may hold values from 0 to 63
- cache_slot: int32 [288], P('req'), may hold values from 0 to 17, as said below
Outputs:
- layer_out: bfloat16 [16384, 1536], P(('req', 'head'))
- keyvalue_slot_cache: bfloat16 [288, 512, 8, 128], P('req', None, 'head')
The draws below stay inside these ranges and needn't reach their ends.
Inputs may be any that keep to these rules, and one draw needn't show every extreme that they name: `span_len`: each row sums to 1024 and its largest entry is exactly 512. `ctx_len`: some prompt has exactly 2048 cached positions. `cache_slot`: within each block of 18 consecutive requests the entries are a permutation of 0 to 17. `routes`: each row names 8 different experts; within each aligned block of 128 rows no expert is named more than 48 times, and in some block some expert exactly 48 times.
All inputs are finite; a program needn't handle non-finite values.
Results may differ from the reference program's by a relative error of at most 0.0075.
The reference program's roundings to bfloat16 on the way count: a program that leaves them out, or rounds other values in their place, can miss the bound.
Values may be sent and summed in bfloat16 or wider, within the bound.
A program may use at most 128 MiB of HBM per device.

```python
import math
import jax
import jax.numpy as jnp
import numpy as np
from jax import lax

MODEL_WIDTH = 1536
HQ = 24
KEYVALUE_HEADS = 8
HEAD_WIDTH = 64
FF = 512
EXPERTS = 32
TOPK = 8
ROWS_DEV = 128
PR_DEV = 4
CONTEXT_SLOTS = 2048
REQ_DEV = 18
CAP = 48
TOK_DEV = 1024
SPAN_LIMIT = 512
GROUPS = 16
PROMPT_COUNT = 64
TOKEN_COUNT = 16384
REQUEST_COUNT = 288
N_REQ = 16
N_HEAD = 8


def draw_cache_kv(key, part):
    key_layout_dims = (PROMPT_COUNT, CONTEXT_SLOTS, KEYVALUE_HEADS, HEAD_WIDTH)
    keys_part = jnp.clip(2.0 * jax.random.normal(key, key_layout_dims, jnp.float32), -12.0, 12.0)
    vals_part = jnp.clip(jax.random.normal(jax.random.fold_in(key, 5), key_layout_dims, jnp.float32), -6.0, 6.0)
    return jnp.concatenate([keys_part, vals_part], axis=-1).astype(jnp.bfloat16)


def draw_ctx_len(key, part):
    lengths = jax.random.randint(key, (PROMPT_COUNT,), 2, CONTEXT_SLOTS + 1, dtype=jnp.int32)
    longest = jax.random.randint(jax.random.fold_in(key, 3), (), 0, PROMPT_COUNT, dtype=jnp.int32)
    return lengths.at[longest].set(CONTEXT_SLOTS)


def permute_block(subkey):
    return jax.random.permutation(subkey, REQ_DEV)


def draw_cache_slot(key, part):
    subkeys = jax.random.split(key, REQUEST_COUNT // REQ_DEV)
    return jax.vmap(permute_block)(subkeys).reshape(-1).astype(jnp.int32)


def set_ends(result, own_key, least, largest):
    longest = result.shape.index(max(result.shape))
    spots = []
    for shift in (0, 1):
        where = [jax.random.randint(jax.random.fold_in(own_key, axis), (), 0, length) for axis, length in enumerate(result.shape)]
        where[longest] = (where[longest] + shift) % result.shape[longest]
        spots.append(tuple(where))
    return result.at[spots[0]].set(least).at[spots[1]].set(largest)


def shard_levels(rng, dims, pieces, least, largest):
    def one(dim, blocks):
        steps = jax.random.uniform(jax.random.fold_in(jax.random.fold_in(rng, 6), dim), (blocks,), jnp.float32, least / len(pieces), largest / len(pieces))
        return jnp.repeat(jnp.exp(steps), dims[dim] // blocks).reshape((-1,) + (1,) * (len(dims) - dim - 1))

    level = one(*pieces[0])
    for cut in pieces[1:]:
        level = level * one(*cut)
    return level


def profile(count, total, bound, slope):
    weights = [(1 << 20) // math.isqrt(rank ** slope) + 1 for rank in range(2, count + 1)]
    surplus, counts = total - bound - (count - 1), [1] * (count - 1)
    while surplus > 0:
        movable = [i for i in range(count - 1) if counts[i] < bound]
        mass, left = sum([weights[i] for i in movable]), surplus
        for i in movable:
            extra = min(bound - counts[i], max(1, left * weights[i] // mass), surplus)
            counts[i] = counts[i] + extra
            surplus = surplus - extra
    return np.array([bound] + counts)


def ragged_sizes(rng, amount, total, most, skew):
    if amount == 2:
        one = jax.random.randint(rng, (), max(1, total - most), min(most, total - 1) + 1)
        return jnp.stack([one, total - one])
    sizes = jnp.asarray(profile(amount, total, most, skew), jnp.int32)
    couples = (amount - 1) // 2
    donor, taker = sizes[1:1 + 2 * couples:2], sizes[2:2 + 2 * couples:2]
    room = jnp.minimum(donor - 1, most - taker)
    shifted = jax.random.randint(jax.random.fold_in(rng, 1), (couples,), 0, 1 << 20) % (room + 1)
    sizes = sizes.at[1:1 + 2 * couples:2].set(donor - shifted).at[2:2 + 2 * couples:2].set(taker + shifted)
    return sizes[jax.random.permutation(jax.random.fold_in(rng, 2), amount)]


def assign_block(rng, own, number, rows, number_of, top, reach, lean):
    sequence = jax.random.permutation(rng, number_of)
    heavy_load, common = shares(number_of, rows * top, reach, lean, True), shares(number_of, rows * top, reach, lean, False)
    places = jnp.arange(number_of)

    def named(tallies, rotation):
        used = int((tallies > 0).sum())
        fixed = max(1, used // 4)
        shifted = fixed + (places - fixed + rotation * (used - fixed)) % max(1, number_of - fixed)
        return jnp.zeros((number_of,), jnp.int32).at[sequence[jnp.where(places < fixed, places, shifted)]].set(jnp.asarray(tallies, jnp.int32))

    tallies = jnp.where(number % 4 == 0, named(heavy_load, number // 4), named(common, number - number // 4 - 1))
    mixed = jax.random.permutation(jax.random.fold_in(own, 3), number_of)
    giver, taker = mixed[0:number_of // 2 * 2:2], mixed[1:number_of // 2 * 2:2]
    room = jnp.minimum(tallies[giver] - 1, reach - tallies[taker]) // 2
    room = jnp.where((giver == sequence[0]) | (taker == sequence[0]) | (tallies[taker] == 0), 0, jnp.maximum(room, 0))
    shifted = jax.random.randint(jax.random.fold_in(own, 4), (number_of // 2,), 0, 1 << 20) % (room + 1)
    tallies = tallies.at[giver].add(-shifted).at[taker].add(shifted)
    members = jnp.searchsorted(jnp.cumsum(tallies), jnp.arange(rows * top), side="right").astype(jnp.int32)
    table = members.reshape(top, rows).T
    table = table[jax.random.permutation(jax.random.fold_in(own, 1), rows)]
    rotation = jax.random.randint(jax.random.fold_in(own, 2), (rows, 1), 0, top)
    return jnp.take_along_axis(table, (jnp.arange(top)[None, :] + rotation) % top, axis=1)


def shares(count, total, bound, slope, full):
    loads = [(1 << 20) // math.isqrt(rank ** slope) + 1 for rank in range(1, count + 1)]
    largest = bound if full else min(bound, max(-(-total // count), total * loads[0] // sum(loads)))
    least = 1 if total - largest >= count - 1 else 0
    given, surplus = [largest] + [least] * (count - 1), total - largest - least * (count - 1)
    while surplus > 0:
        free = [i for i in range(1, count) if given[i] < largest] or [i for i in range(1, count) if given[i] < bound]
        mass, left = sum([loads[i] for i in free]), surplus
        for i in free:
            more = min(bound - given[i], max(1, left * loads[i] // mass), surplus)
            given[i] = given[i] + more
            surplus = surplus - more
    return np.array(given)


def bell_draw(own_key, shape, scale, most, pieces=(), kind=jnp.bfloat16):
    result = jax.random.normal(own_key, shape, jnp.float32) * scale
    if len(pieces) > 0:
        result = shard_levels(own_key, shape, pieces, -0.22, 0.18) * result
    return jnp.clip(result, min=-most, max=most).astype(kind)


def setup_inputs(seed: int = 0) -> dict:
    seeds = jax.random.split(jax.random.key(seed), 16)
    hidden_in = bell_draw(seeds[0], (TOKEN_COUNT, MODEL_WIDTH), 0.5, 3.0, ((0, 128),))
    attn_gain = jnp.clip(1.0 + 0.18 * jax.random.normal(seeds[1], (MODEL_WIDTH,), jnp.float32), 0.1, 1.9)
    w_query = bell_draw(seeds[2], (MODEL_WIDTH, HQ * HEAD_WIDTH), MODEL_WIDTH ** -0.5, 0.15625, ((1, 8),))
    keyvalue_weight = bell_draw(seeds[3], (MODEL_WIDTH, KEYVALUE_HEADS, 2 * HEAD_WIDTH), (MODEL_WIDTH // 4) ** -0.5, 0.3125, ((1, 8),))
    w_out = bell_draw(seeds[4], (HQ * HEAD_WIDTH, MODEL_WIDTH), (4 * HEAD_WIDTH) ** -0.5, 0.375, ((0, 8),))
    cache_kv = draw_cache_kv(jax.random.fold_in(seeds[15], 71), 0)
    ctx_len = draw_ctx_len(jax.random.fold_in(seeds[15], 71), 0)
    span_len = jax.vmap(lambda own: ragged_sizes(own, PR_DEV, TOK_DEV, SPAN_LIMIT, 2))(jax.random.split(seeds[7], GROUPS)).reshape((GROUPS, PR_DEV)).astype(jnp.int32)
    ffn_gain = jnp.clip(1.0 + 0.18 * jax.random.normal(seeds[8], (MODEL_WIDTH,), jnp.float32), 0.1, 1.9)
    routes_keys = jax.random.split(jax.random.fold_in(seeds[9], 1), TOKEN_COUNT // ROWS_DEV)
    routes_turns = jax.random.permutation(jax.random.fold_in(seeds[9], 3), TOKEN_COUNT // ROWS_DEV)
    routes = jax.vmap(lambda own, number: assign_block(jax.random.fold_in(seeds[9], 2), own, number, ROWS_DEV, EXPERTS, TOPK, CAP, 2))(routes_keys, routes_turns).reshape((TOKEN_COUNT, TOPK))
    gate_weights = jnp.clip(0.049804688 + 0.24902344 * jax.random.uniform(seeds[10], (TOKEN_COUNT, TOPK), jnp.float32) ** shard_levels(seeds[10], (TOKEN_COUNT, TOPK), ((0, 128),), -0.2, 0.2), 0.049804688, 0.29882812).astype(jnp.bfloat16)
    w_gate_up = bell_draw(seeds[11], (EXPERTS, MODEL_WIDTH, 2 * FF), MODEL_WIDTH ** -0.5, 0.15625, ((0, 16),))
    w_down = bell_draw(seeds[12], (EXPERTS, FF, MODEL_WIDTH), FF ** -0.5, 0.25, ((0, 16),))
    req_prompt = set_ends(jax.random.randint(seeds[13], (REQUEST_COUNT,), 0, PROMPT_COUNT), jax.random.fold_in(seeds[13], 1), 0, PROMPT_COUNT - 1).astype(jnp.int32)
    cache_slot = draw_cache_slot(jax.random.fold_in(seeds[15], 71), 0)
    return dict(hidden_in=hidden_in, attn_gain=attn_gain, w_query=w_query, keyvalue_weight=keyvalue_weight, w_out=w_out, cache_kv=cache_kv, ctx_len=ctx_len, span_len=span_len, ffn_gain=ffn_gain, routes=routes, gate_weights=gate_weights, w_gate_up=w_gate_up, w_down=w_down, req_prompt=req_prompt, cache_slot=cache_slot)


epsilon = 1e-05
rope_base = 10000.0

def rms_norm(values, gain):
    values = values.astype(jnp.float32)
    mean_sq = lax.optimization_barrier(jnp.mean(values * values, axis=-1, keepdims=True))
    return values * lax.rsqrt(mean_sq + epsilon) * gain.astype(jnp.float32)

def rotate(heads, position):
    half_dim = heads.shape[-1] // 2
    frequency = rope_base ** (-2.0 * jnp.arange(half_dim).astype(jnp.float32) / heads.shape[-1])
    angles = position[:, None] * frequency[None, :]
    cosine = jnp.cos(angles)[:, None, :]
    sine = jnp.sin(angles)[:, None, :]
    first_half = heads[..., :half_dim]
    second_half = heads[..., half_dim:]
    return jnp.concatenate([first_half * cosine - second_half * sine, second_half * cosine + first_half * sine], axis=-1)

def attend_prompt(queries, keyval, cached, ctx_length, seg_start, seg_length, window_first):
    most = queries.shape[0]
    heads_kv = keyval.shape[1]
    head_size = keyval.shape[2] // 2
    groups = queries.shape[1] // (heads_kv * head_size)
    query_four = queries.reshape(most, heads_kv, groups, head_size).astype(jnp.float32)
    new_keys = keyval[..., :head_size].astype(jnp.float32)
    new_vals = keyval[..., head_size:].astype(jnp.float32)
    old_keys = cached[..., :head_size].astype(jnp.float32)
    old_vals = cached[..., head_size:].astype(jnp.float32)
    row_pos = window_first + jnp.arange(most).astype(jnp.int32)
    row_ok = (row_pos >= seg_start) & (row_pos < seg_start + seg_length)
    scale = 1.0 / head_size ** 0.5
    score_old = jnp.einsum('mhgd,chd->hgmc', query_four, old_keys) * scale
    score_new = jnp.einsum('mhgd,nhd->hgmn', query_four, new_keys) * scale
    old_ok = jnp.arange(cached.shape[0]).astype(jnp.int32) < ctx_length
    index_rows = jnp.arange(most).astype(jnp.int32)
    new_ok = row_ok[None, :] & (index_rows[None, :] <= index_rows[:, None])
    score_old = jnp.where(old_ok[None, None, None, :], score_old, -1e+30)
    score_new = jnp.where(new_ok[None, None], score_new, -1e+30)
    top_score = jnp.maximum(lax.optimization_barrier(jnp.max(score_old, axis=-1)), lax.optimization_barrier(jnp.max(score_new, axis=-1)))
    exp_old = jnp.exp(score_old - top_score[..., None])
    exp_new = jnp.exp(score_new - top_score[..., None])
    denom = lax.optimization_barrier(jnp.sum(exp_old, axis=-1)) + lax.optimization_barrier(jnp.sum(exp_new, axis=-1))
    weight_old = (exp_old / denom[..., None]).astype(jnp.bfloat16).astype(jnp.float32)
    weight_new = (exp_new / denom[..., None]).astype(jnp.bfloat16).astype(jnp.float32)
    mixed = jnp.einsum('hgmc,chd->mhgd', weight_old, old_vals) + jnp.einsum('hgmn,nhd->mhgd', weight_new, new_vals)
    return (mixed.reshape(most, -1).astype(jnp.bfloat16), row_ok)

def reference(hidden_in, attn_gain, w_query, keyvalue_weight, w_out, cache_kv, ctx_len, span_len, ffn_gain, routes, gate_weights, w_gate_up, w_down, req_prompt, cache_slot):
    seg_ends = jnp.cumsum(span_len, axis=1).astype(jnp.int32)
    seg_starts = (seg_ends - span_len).astype(jnp.int32)
    all_rows = jnp.arange(TOKEN_COUNT).astype(jnp.int32)
    group_of = all_rows // TOK_DEV
    within = all_rows % TOK_DEV
    local_prompt = lax.optimization_barrier(jnp.sum((seg_ends[group_of] <= within[:, None]).astype(jnp.int32), axis=1)).astype(jnp.int32)
    start_rows = jnp.take_along_axis(seg_starts[group_of], local_prompt[:, None], axis=1)[:, 0]
    prompt_of = group_of * PR_DEV + local_prompt
    position = (ctx_len[prompt_of] + within - start_rows).astype(jnp.float32)
    scaled_hidden = rms_norm(hidden_in, attn_gain).astype(jnp.bfloat16)
    query_all = jnp.dot(scaled_hidden, w_query, preferred_element_type=jnp.float32).reshape(TOKEN_COUNT, HQ, HEAD_WIDTH)
    query_all = rotate(query_all, position).reshape(TOKEN_COUNT, HQ * HEAD_WIDTH).astype(jnp.bfloat16)
    every_keyval_row = jnp.dot(scaled_hidden, keyvalue_weight.reshape(MODEL_WIDTH, KEYVALUE_HEADS * 2 * HEAD_WIDTH), preferred_element_type=jnp.float32).reshape(TOKEN_COUNT, KEYVALUE_HEADS, 2 * HEAD_WIDTH)
    every_keyval_row = jnp.concatenate([rotate(every_keyval_row[..., :HEAD_WIDTH], position), every_keyval_row[..., HEAD_WIDTH:]], axis=-1).astype(jnp.bfloat16)

    def one_prompt(result_rows, prompt_idx):
        group_idx = prompt_idx // PR_DEV
        member = prompt_idx % PR_DEV
        seg_start = seg_starts[group_idx, member]
        seg_length = span_len[group_idx, member]
        window_first = jnp.minimum(seg_start, TOK_DEV - SPAN_LIMIT).astype(jnp.int32)
        first_row = (group_idx * TOK_DEV + window_first).astype(jnp.int32)
        queries = lax.dynamic_slice_in_dim(query_all, first_row, SPAN_LIMIT, 0)
        keyval = lax.dynamic_slice_in_dim(every_keyval_row, first_row, SPAN_LIMIT, 0)
        mixed, row_ok = attend_prompt(queries, keyval, cache_kv[prompt_idx], ctx_len[prompt_idx], seg_start, seg_length, window_first)
        previous = lax.dynamic_slice_in_dim(result_rows, first_row, SPAN_LIMIT, 0)
        merged = jnp.where(row_ok[:, None], mixed, previous)
        return (lax.dynamic_update_slice_in_dim(result_rows, merged, first_row, 0), None)
    attn = lax.scan(one_prompt, jnp.zeros((TOKEN_COUNT, HQ * HEAD_WIDTH), jnp.bfloat16), jnp.arange(PROMPT_COUNT).astype(jnp.int32))[0]
    resid = hidden_in.astype(jnp.float32) + jnp.dot(attn, w_out, preferred_element_type=jnp.float32)
    expert_in = rms_norm(resid, ffn_gain).astype(jnp.bfloat16)
    pair_expert = routes.reshape(-1)
    pair_gate = gate_weights.reshape(-1).astype(jnp.float32)
    limit = N_REQ * N_HEAD * CAP

    def one_expert(running, expert):
        flags = jnp.where(pair_expert == expert, 0, 1).astype(jnp.int32)
        order = jnp.argsort(flags, stable=True)[:limit].astype(jnp.int32)
        chosen = flags[order] == 0
        token_ids = (order // TOPK).astype(jnp.int32)
        picked = expert_in[token_ids]
        both = jnp.dot(picked, w_gate_up[expert], preferred_element_type=jnp.float32)
        act = (jax.nn.silu(both[:, :FF]) * both[:, FF:]).astype(jnp.bfloat16)
        outputs = jnp.dot(act, w_down[expert], preferred_element_type=jnp.float32).astype(jnp.bfloat16)
        weight_col = jnp.where(chosen, pair_gate[order], 0.0)
        return (running.at[token_ids].add(weight_col[:, None] * outputs.astype(jnp.float32)), None)
    moe_sum = lax.scan(one_expert, jnp.zeros((TOKEN_COUNT, MODEL_WIDTH), jnp.float32), jnp.arange(EXPERTS).astype(jnp.int32))[0]
    layer_out = (resid + moe_sum).astype(jnp.bfloat16)
    prompt_ids = jnp.arange(PROMPT_COUNT).astype(jnp.int32)
    global_start = (prompt_ids // PR_DEV * TOK_DEV + seg_starts.reshape(-1)).astype(jnp.int32)
    flat_lengths = span_len.reshape(-1)
    offsets = jnp.arange(SPAN_LIMIT).astype(jnp.int32)
    req_start = global_start[req_prompt]
    req_length = flat_lengths[req_prompt]
    row_ok = offsets[None, :] < req_length[:, None]
    row_ids = jnp.where(row_ok, req_start[:, None] + offsets[None, :], 0).astype(jnp.int32)
    selected_rows = jnp.where(row_ok[:, :, None, None], every_keyval_row[row_ids], jnp.zeros((), jnp.bfloat16))
    target_slots = (jnp.arange(REQUEST_COUNT).astype(jnp.int32) // REQ_DEV * REQ_DEV + cache_slot).astype(jnp.int32)
    keyvalue_slot_cache = jnp.zeros((REQUEST_COUNT, SPAN_LIMIT, KEYVALUE_HEADS, 2 * HEAD_WIDTH), jnp.bfloat16).at[target_slots].set(selected_rows)
    return (layer_out, keyvalue_slot_cache)
```

```python
import functools

import jax
import jax.numpy as jnp
from jax import lax
from jax.experimental import pallas as pl
from jax.experimental.pallas import tpu as pltpu
from jax.sharding import PartitionSpec as P

CAP = 48
EPSILON = 1e-05
ROPE_BASE = 10000.0
LOG2E = 1.4426950408889634
MESH = pl.DeviceIdType.MESH
F32 = jnp.float32
BF16 = jnp.bfloat16
VMEM_BYTES = 60 * 1024 * 1024


def vmem():
    return pl.BlockSpec(memory_space=pltpu.VMEM)


def smem():
    return pl.BlockSpec(memory_space=pltpu.SMEM)


def anyspace():
    return pl.BlockSpec(memory_space=pl.ANY)


def rms(values, gain):
    mean_sq = jnp.mean(values * values, axis=-1, keepdims=True)
    return values * lax.rsqrt(mean_sq + EPSILON) * gain


def head_neighbours():
    hd = lax.axis_index("head")
    y, c = hd // 2, hd % 2
    partner = y * 2 + (1 - c)
    up = ((y + 1) % 4) * 2 + c
    down = ((y + 3) % 4) * 2 + c
    return y, c, partner, up, down


def greet(neighbours):
    barrier = pltpu.get_barrier_semaphore()
    for axis, where in neighbours:
        pl.semaphore_signal(barrier, inc=1, device_id={axis: where}, device_id_type=MESH)
    return lambda: pl.semaphore_wait(barrier, len(neighbours))


def project_kernel(
    hidden_ref, gain_ref, wq_ref, wkv_ref, freq_ref, span_ref, ctx_ref,
    q_ref, kv_ref,
    tok, wq_wide, cos_tab, sin_tab, ssem, rsem,
):
    rows = hidden_ref.shape[0]
    half = rows // 2
    group = lax.axis_index("req")
    y, c, partner, up, down = head_neighbours()
    wait_all = greet([("head", partner), ("head", up), ("head", down)])
    tok[0] = rms(hidden_ref[...].astype(F32), gain_ref[...]).astype(BF16)
    wait_all()

    def copy(i, src, dst, to):
        return pltpu.make_async_remote_copy(
            src_ref=src, dst_ref=dst, send_sem=ssem.at[i], recv_sem=rsem.at[i],
            device_id={"head": to}, device_id_type=MESH,
        )

    low, high = pl.ds(0, half), pl.ds(half, half)
    copies = [
        copy(0, tok.at[0], tok.at[6], up),
        copy(1, tok.at[0], tok.at[2], down),
        copy(2, tok.at[0], tok.at[1], partner),
        copy(3, tok.at[6, low], tok.at[4, low], up),
        copy(4, tok.at[6], tok.at[7], partner),
        copy(5, tok.at[2, high], tok.at[4, high], down),
        copy(6, tok.at[2], tok.at[3], partner),
        copy(7, tok.at[4], tok.at[5], partner),
    ]
    for i in (0, 1, 2):
        copies[i].start()

    wq_wide[...] = jnp.zeros_like(wq_wide)
    for h in range(3):
        wq_wide[pl.ds(h * 128, 64), :] = wq_ref[pl.ds(h * 64, 64), :]

    lane = lax.broadcasted_iota(jnp.int32, (rows, 128), 1)

    @pl.loop(0, 8)
    def _(block):
        within = lax.broadcasted_iota(jnp.int32, (rows, 128), 0) + block * rows
        position = jnp.zeros((rows, 128), jnp.int32)
        begin = 0
        for j in range(4):
            shift = ctx_ref[group * 4 + j] - begin
            position = jnp.where(within >= begin, within + shift, position)
            begin = begin + span_ref[j, group]
        angles = position.astype(F32) * freq_ref[...]
        where_rows = pl.ds(pl.multiple_of(block * rows, rows), rows)
        cos_tab[where_rows, :] = jnp.where(lane < 64, jnp.cos(angles), 1.0)
        sine = jnp.sin(angles)
        sin_tab[where_rows, :] = jnp.where(lane < 32, -sine, jnp.where(lane < 64, sine, 0.0))

    def project(slot):
        block = ((y + slot // 2) % 4) * 2 + (c + slot % 2) % 2
        at = pl.ds(pl.multiple_of(block * rows, rows), rows)
        cosine, sine = cos_tab[at, :], sin_tab[at, :]

        def turn(values):
            other = jnp.where(lane < 32, pltpu.roll(values, 96, 1), pltpu.roll(values, 32, 1))
            return (values * cosine + other * sine).astype(BF16)

        own = tok[slot]
        wide = lax.dot_general(own, wq_wide[...], (((1,), (1,)), ((), ())), preferred_element_type=F32)
        for h in range(3):
            q_ref[at, h * 128 : (h + 1) * 128] = turn(wide[:, h * 128 : (h + 1) * 128])
        kv_ref[at, :] = turn(jnp.dot(own, wkv_ref[...], preferred_element_type=F32))

    project(0)
    copies[0].wait_recv()
    copies[3].start()
    copies[4].start()
    copies[1].wait_recv()
    copies[5].start()
    copies[6].start()
    copies[2].wait_recv()
    project(1)
    project(6)
    project(2)
    copies[3].wait_recv()
    copies[5].wait_recv()
    copies[7].start()
    copies[4].wait_recv()
    project(7)
    copies[6].wait_recv()
    project(3)
    project(4)
    copies[7].wait_recv()
    project(5)
    for one in copies:
        one.wait_send()


def project_tokens(hidden, gain, wq_t, wkv, freq, span_t, ctx):
    rows, width = hidden.shape
    tokens = rows * 8
    return pl.pallas_call(
        project_kernel,
        name="project_tokens",
        out_shape=(
            jax.ShapeDtypeStruct((tokens, 384), BF16),
            jax.ShapeDtypeStruct((tokens, 128), BF16),
        ),
        in_specs=[vmem()] * 5 + [smem()] * 2,
        out_specs=(vmem(), vmem()),
        scratch_shapes=[
            pltpu.VMEM((8, rows, width), BF16),
            pltpu.VMEM((384, width), BF16),
            pltpu.VMEM((tokens, 128), F32),
            pltpu.VMEM((tokens, 128), F32),
            pltpu.SemaphoreType.DMA((8,)),
            pltpu.SemaphoreType.DMA((8,)),
        ],
        compiler_params=pltpu.CompilerParams(
            collective_id=0, has_side_effects=True, vmem_limit_bytes=VMEM_BYTES
        ),
    )(hidden, gain, wq_t, wkv, freq, span_t, ctx)


KEYS = 512
NEW_KEYS = 256
TILE = 128


def attend_kernel(
    q_ref, kv_ref, cache_ref, routes_ref, gates_ref, span_ref, ctx_ref,
    attn_ref, kvx_ref,
    kv_wide, top, total, mixed,
):
    group = lax.axis_index("req")
    tokens = q_ref.shape[0]
    kv_wide[pl.ds(0, tokens), :] = kv_ref[...].astype(F32)
    scale = LOG2E / 8.0

    def fold(queries, keys, bias):
        scores = lax.dot_general(queries, keys, (((1,), (1,)), ((), ())), preferred_element_type=F32)
        scores = scores * scale + bias
        old = top[...]
        new = jnp.maximum(old, jnp.max(scores, axis=1, keepdims=True))
        probs = jnp.exp2(scores - new)
        fade = jnp.exp2(old - new)
        top[...] = new
        total[...] = total[...] * fade + jnp.sum(probs, axis=1, keepdims=True)
        mixed[...] = mixed[...] * fade + jnp.dot(probs.astype(BF16), keys, preferred_element_type=F32)

    def prompt(j, carry):
        begin, packed = carry
        length = span_ref[j, group]
        end = begin + length
        ctx = ctx_ref[group * 4 + j]

        def tile(t, _):
            first = pl.multiple_of(t * TILE, TILE)
            at = pl.ds(first, TILE)
            queries = jnp.concatenate([q_ref[at, h * 128 : (h + 1) * 128] for h in range(3)], axis=0)
            top[...] = jnp.full_like(top, -3e38)
            total[...] = jnp.zeros_like(total)
            mixed[...] = jnp.zeros_like(mixed)

            def old_keys(i, _):
                keys = cache_ref[j, pl.ds(pl.multiple_of(i * KEYS, KEYS), KEYS), :]
                col = lax.broadcasted_iota(jnp.int32, (1, KEYS), 1) + i * KEYS
                fold(queries, keys, jnp.where(col < ctx, 0.0, -1e30))
                return 0

            lax.fori_loop(0, (ctx + KEYS - 1) // KEYS, old_keys, 0)

            def new_keys(i, _):
                keys = kv_ref[pl.ds(pl.multiple_of(i * NEW_KEYS, NEW_KEYS), NEW_KEYS), :]
                col = lax.broadcasted_iota(jnp.int32, (3 * TILE, NEW_KEYS), 1) + i * NEW_KEYS
                row = lax.broadcasted_iota(jnp.int32, (3 * TILE, NEW_KEYS), 0) % TILE + first
                fold(queries, keys, jnp.where((col >= begin) & (col <= row), 0.0, -1e30))
                return 0

            lax.fori_loop(begin // NEW_KEYS, (first + TILE - 1) // NEW_KEYS + 1, new_keys, 0)
            out = mixed[...] / total[...]
            side = jnp.concatenate([out[h * TILE : (h + 1) * TILE, 64:] for h in range(3)], axis=1)
            row = lax.broadcasted_iota(jnp.int32, side.shape, 0) + first
            mine = (row >= begin) & (row < end)
            attn_ref[at, :] = jnp.where(mine, side, attn_ref[at, :].astype(F32)).astype(BF16)
            return 0

        lax.fori_loop(begin // TILE, (end + TILE - 1) // TILE, tile, 0)

        def pack(i, _):
            dst = pl.ds(pl.multiple_of(packed + i * 16, 16), 16)
            kvx_ref[dst, :] = kv_wide[pl.ds(begin + i * 16, 16), :].astype(BF16)
            return 0

        chunks = (length + 15) // 16
        lax.fori_loop(0, chunks, pack, 0)
        return end, packed + chunks * 16

    kv_wide[pl.ds(tokens, 16), :] = jnp.zeros((16, 128), F32)
    kvx_ref[...] = jnp.zeros_like(kvx_ref)
    attn_ref[...] = jnp.zeros_like(attn_ref)
    lax.fori_loop(0, 4, prompt, (0, 0))
    expert = lax.broadcasted_iota(jnp.int32, (32, 128), 0)
    gates = jnp.zeros((32, 128), F32)
    for k in range(8):
        hit = routes_ref[k : k + 1, :] == expert
        gates = gates + jnp.where(hit, gates_ref[k : k + 1, :].astype(F32), 0.0)
    kvx_ref[pl.ds(1088, 32), :] = gates.astype(BF16)


def attend(q, kv, cache, routes_t, gates_t, span_t, ctx):
    tokens = q.shape[0]
    return pl.pallas_call(
        attend_kernel,
        name="attend",
        out_shape=(
            jax.ShapeDtypeStruct((tokens, 192), BF16),
            jax.ShapeDtypeStruct((1152, 128), BF16),
        ),
        in_specs=[vmem()] * 5 + [smem()] * 2,
        out_specs=(vmem(), vmem()),
        scratch_shapes=[
            pltpu.VMEM((tokens + 16, 128), F32),
            pltpu.VMEM((3 * TILE, 1), F32),
            pltpu.VMEM((3 * TILE, 1), F32),
            pltpu.VMEM((3 * TILE, 128), F32),
        ],
        compiler_params=pltpu.CompilerParams(vmem_limit_bytes=VMEM_BYTES),
    )(q, kv, cache, routes_t, gates_t, span_t, ctx)


def body(
    hidden_in, attn_gain, w_query, keyvalue_weight, w_out, cache_kv, ctx_len, span_len,
    ffn_gain, routes, gate_weights, w_gate_up, w_down, req_prompt, cache_slot,
):
    rows_dev, width = hidden_in.shape
    prompts_dev = cache_kv.shape[0]
    span_t = span_len.T
    lane = jnp.arange(128)
    freq = (ROPE_BASE ** (-2.0 * (lane % 32).astype(F32) / 64.0))[None, :]
    q, kv = project_tokens(
        hidden_in, attn_gain[None, :], w_query.T, keyvalue_weight.reshape(width, 128), freq, span_t, ctx_len
    )
    attn, kvx = attend(
        q, kv, cache_kv.reshape(prompts_dev, -1, 128), routes.T, gate_weights.T, span_t, ctx_len
    )
    tok_dev = q.shape[0]
    span_most = tok_dev // 2
    projected = lax.psum_scatter(
        jnp.dot(attn, w_out, preferred_element_type=F32), "head", scatter_dimension=0, tiled=True
    )
    resid = hidden_in.astype(F32) + projected
    expert_in = rms(resid, ffn_gain).astype(BF16)
    n_owners = lax.axis_size("req")
    local_experts = w_gate_up.shape[0]
    experts_all = local_experts * n_owners
    slots_all = experts_all * CAP
    pair_expert = routes.reshape(-1)
    onehot = (pair_expert[:, None] == jnp.arange(experts_all)[None, :]).astype(jnp.int32)
    ranks = jnp.cumsum(onehot, axis=0) - onehot
    slot_pos = jnp.sum(ranks * onehot, axis=1)
    slot_ids = pair_expert * CAP + slot_pos
    table = jnp.arange(slots_all)[:, None] == slot_ids[None, :]
    topk = routes.shape[1]
    send_map = jnp.any(table.reshape(slots_all, rows_dev, topk), axis=-1).astype(BF16)
    gate_flat = gate_weights.reshape(-1).astype(F32)
    combine_map = jnp.sum(
        jnp.where(table, gate_flat[None, :], 0.0).reshape(slots_all, rows_dev, topk), axis=-1
    ).astype(BF16)
    buffer = jnp.dot(send_map, expert_in, preferred_element_type=F32).astype(BF16)
    ff_width = w_down.shape[1]
    received = lax.all_to_all(
        buffer.reshape(experts_all, CAP, width), "req", split_axis=0, concat_axis=0, tiled=True
    )
    slot_count = received.shape[1]
    blocks = received.reshape(n_owners, local_experts, slot_count, width)
    both = jnp.einsum("secd,edf->secf", blocks, w_gate_up, preferred_element_type=F32)
    act = (jax.nn.silu(both[..., :ff_width]) * both[..., ff_width:]).astype(BF16)
    outputs = jnp.einsum("secf,efd->secd", act, w_down, preferred_element_type=F32).astype(BF16)
    returned = lax.all_to_all(
        outputs.reshape(received.shape), "req", split_axis=0, concat_axis=0, tiled=True
    )
    moe_sum = jnp.einsum(
        "sr,sd->rd", combine_map, returned.reshape(slots_all, width), preferred_element_type=F32
    )
    layer_out = (resid + moe_sum).astype(BF16)
    all_kv = lax.all_gather(kvx[:1088], "req", axis=0, tiled=True)
    padded = (span_len + 15) // 16 * 16
    starts_table = jnp.cumsum(padded, axis=1) - padded
    starts_table = (starts_table + jnp.arange(16)[:, None] * 1088).reshape(-1)
    lengths_table = span_len.reshape(-1)
    slot_of = cache_slot[:, None] == jnp.arange(18)[None, :]
    prompt = jnp.sum(jnp.where(slot_of, req_prompt[:, None], 0), axis=0)
    pick = prompt[:, None] == jnp.arange(64)[None, :]
    req_start = jnp.sum(jnp.where(pick, starts_table[None, :], 0), axis=1)
    req_length = jnp.sum(jnp.where(pick, lengths_table[None, :], 0), axis=1)
    cache = slot_rows(all_kv, req_start, req_length)
    return (layer_out, cache.reshape(18, span_most, 1, 128))


def slot_kernel(start_ref, length_ref, all_ref, out_ref):
    s = pl.program_id(0)
    first = pl.multiple_of(start_ref[s], 16)

    @pl.loop(0, 32)
    def _(i):
        rows = all_ref[pl.ds(pl.multiple_of(jnp.minimum(first + i * 16, 17408 - 16), 16), 16), :]
        at = lax.broadcasted_iota(jnp.int32, rows.shape, 0) + i * 16
        kept = jnp.where(at < length_ref[s], rows.astype(F32), 0.0).astype(BF16)
        out_ref[0, pl.ds(pl.multiple_of(i * 16, 16), 16), :] = kept


def slot_rows(all_kv, start, length):
    return pl.pallas_call(
        slot_kernel,
        name="slot_rows",
        grid_spec=pltpu.PrefetchScalarGridSpec(
            num_scalar_prefetch=2,
            grid=(18,),
            in_specs=[pl.BlockSpec(all_kv.shape, lambda s, a, b: (0, 0), pipeline_mode=pl.Buffered(1))],
            out_specs=pl.BlockSpec((1, 512, 128), lambda s, a, b: (s, 0, 0)),
        ),
        out_shape=jax.ShapeDtypeStruct((18, 512, 128), BF16),
        compiler_params=pltpu.CompilerParams(vmem_limit_bytes=VMEM_BYTES),
    )(start, length, all_kv)


def solution(mesh):
    placed = (
        P(("req", "head"), None),
        P(),
        P(None, "head"),
        P(None, "head", None),
        P("head", None),
        P("req", None, "head", None),
        P(),
        P(),
        P(),
        P(("req", "head"), None),
        P(("req", "head"), None),
        P("req", None, None),
        P("req", None, None),
        P("req"),
        P("req"),
    )
    return jax.shard_map(
        body,
        mesh=mesh,
        in_specs=placed,
        out_specs=(P(("req", "head"), None), P("req", None, "head", None)),
        check_vma=False,
    )
```

```python
import functools

import jax
import jax.numpy as jnp
from jax import lax
from jax.experimental import pallas as pl
from jax.experimental.pallas import tpu as pltpu
from jax.sharding import PartitionSpec as P

CAP = 48
EPSILON = 1e-05
ROPE_BASE = 10000.0
LOG2E = 1.4426950408889634
MESH = pl.DeviceIdType.MESH
F32 = jnp.float32
BF16 = jnp.bfloat16
VMEM_BYTES = 60 * 1024 * 1024
KV_ROWS = 1152
GATE_ROW = 1088


def vmem():
    return pl.BlockSpec(memory_space=pltpu.VMEM)


def smem():
    return pl.BlockSpec(memory_space=pltpu.SMEM)


def anyspace():
    return pl.BlockSpec(memory_space=pl.ANY)


def rms(values, gain):
    mean_sq = jnp.mean(values * values, axis=-1, keepdims=True)
    return values * lax.rsqrt(mean_sq + EPSILON) * gain


def head_neighbours():
    hd = lax.axis_index("head")
    y, c = hd // 2, hd % 2
    partner = y * 2 + (1 - c)
    up = ((y + 1) % 4) * 2 + c
    down = ((y + 3) % 4) * 2 + c
    return y, c, partner, up, down


def greet(neighbours):
    barrier = pltpu.get_barrier_semaphore()
    for axis, where in neighbours:
        pl.semaphore_signal(barrier, inc=1, device_id={axis: where}, device_id_type=MESH)
    return lambda: pl.semaphore_wait(barrier, len(neighbours))


def project_kernel(
    hidden_ref, gain_ref, wq_ref, wkv_ref, freq_ref, span_ref, ctx_ref,
    q_ref, kv_ref,
    tok, wq_wide, cos_tab, sin_tab, ssem, rsem,
):
    rows = hidden_ref.shape[0]
    half = rows // 2
    group = lax.axis_index("req")
    y, c, partner, up, down = head_neighbours()
    wait_all = greet([("head", partner), ("head", up), ("head", down)])
    tok[0] = rms(hidden_ref[...].astype(F32), gain_ref[...]).astype(BF16)
    wait_all()

    def copy(i, src, dst, to):
        return pltpu.make_async_remote_copy(
            src_ref=src, dst_ref=dst, send_sem=ssem.at[i], recv_sem=rsem.at[i],
            device_id={"head": to}, device_id_type=MESH,
        )

    low, high = pl.ds(0, half), pl.ds(half, half)
    copies = [
        copy(0, tok.at[0], tok.at[6], up),
        copy(1, tok.at[0], tok.at[2], down),
        copy(2, tok.at[0], tok.at[1], partner),
        copy(3, tok.at[6, low], tok.at[4, low], up),
        copy(4, tok.at[6], tok.at[7], partner),
        copy(5, tok.at[2, high], tok.at[4, high], down),
        copy(6, tok.at[2], tok.at[3], partner),
        copy(7, tok.at[4], tok.at[5], partner),
    ]
    for i in (0, 1, 2):
        copies[i].start()

    wq_wide[...] = jnp.zeros_like(wq_wide)
    for h in range(3):
        wq_wide[pl.ds(h * 128, 64), :] = wq_ref[pl.ds(h * 64, 64), :]

    lane = lax.broadcasted_iota(jnp.int32, (rows, 128), 1)

    @pl.loop(0, 8)
    def _(block):
        within = lax.broadcasted_iota(jnp.int32, (rows, 128), 0) + block * rows
        position = jnp.zeros((rows, 128), jnp.int32)
        begin = 0
        for j in range(4):
            shift = ctx_ref[group * 4 + j] - begin
            position = jnp.where(within >= begin, within + shift, position)
            begin = begin + span_ref[j, group]
        angles = position.astype(F32) * freq_ref[...]
        where_rows = pl.ds(pl.multiple_of(block * rows, rows), rows)
        cos_tab[where_rows, :] = jnp.where(lane < 64, jnp.cos(angles), 1.0)
        sine = jnp.sin(angles)
        sin_tab[where_rows, :] = jnp.where(lane < 32, -sine, jnp.where(lane < 64, sine, 0.0))

    def project(slot):
        block = ((y + slot // 2) % 4) * 2 + (c + slot % 2) % 2
        at = pl.ds(pl.multiple_of(block * rows, rows), rows)
        cosine, sine = cos_tab[at, :], sin_tab[at, :]

        def turn(values):
            other = jnp.where(lane < 32, pltpu.roll(values, 96, 1), pltpu.roll(values, 32, 1))
            return (values * cosine + other * sine).astype(BF16)

        own = tok[slot]
        wide = lax.dot_general(own, wq_wide[...], (((1,), (1,)), ((), ())), preferred_element_type=F32)
        for h in range(3):
            q_ref[at, h * 128 : (h + 1) * 128] = turn(wide[:, h * 128 : (h + 1) * 128])
        kv_ref[at, :] = turn(jnp.dot(own, wkv_ref[...], preferred_element_type=F32))

    project(0)
    copies[0].wait_recv()
    copies[3].start()
    copies[4].start()
    copies[1].wait_recv()
    copies[5].start()
    copies[6].start()
    copies[2].wait_recv()
    project(1)
    project(6)
    project(2)
    copies[3].wait_recv()
    copies[5].wait_recv()
    copies[7].start()
    copies[4].wait_recv()
    project(7)
    copies[6].wait_recv()
    project(3)
    project(4)
    copies[7].wait_recv()
    project(5)
    for one in copies:
        one.wait_send()


def project_tokens(hidden, gain, wq_t, wkv, freq, span_t, ctx):
    rows, width = hidden.shape
    tokens = rows * 8
    return pl.pallas_call(
        project_kernel,
        name="project_tokens",
        out_shape=(
            jax.ShapeDtypeStruct((tokens, 384), BF16),
            jax.ShapeDtypeStruct((tokens, 128), BF16),
        ),
        in_specs=[vmem()] * 5 + [smem()] * 2,
        out_specs=(vmem(), vmem()),
        scratch_shapes=[
            pltpu.VMEM((8, rows, width), BF16),
            pltpu.VMEM((384, width), BF16),
            pltpu.VMEM((tokens, 128), F32),
            pltpu.VMEM((tokens, 128), F32),
            pltpu.SemaphoreType.DMA((8,)),
            pltpu.SemaphoreType.DMA((8,)),
        ],
        compiler_params=pltpu.CompilerParams(
            collective_id=0, has_side_effects=True, vmem_limit_bytes=VMEM_BYTES
        ),
    )(hidden, gain, wq_t, wkv, freq, span_t, ctx)


KEYS = 512
NEW_KEYS = 256
TILE = 128


def attend_kernel(
    q_ref, kv_ref, cache_ref, routes_ref, gates_ref, span_ref, ctx_ref, prompt_ref, place_ref,
    attn_ref, kvx_ref, place_rows_ref,
    kv_wide, top, total, mixed,
):
    group = lax.axis_index("req")
    tokens = q_ref.shape[0]
    kv_wide[pl.ds(0, tokens), :] = kv_ref[...].astype(F32)
    scale = LOG2E / 8.0

    def fold(queries, keys, bias):
        scores = lax.dot_general(queries, keys, (((1,), (1,)), ((), ())), preferred_element_type=F32)
        scores = scores * scale + bias
        old = top[...]
        new = jnp.maximum(old, jnp.max(scores, axis=1, keepdims=True))
        probs = jnp.exp2(scores - new)
        fade = jnp.exp2(old - new)
        top[...] = new
        total[...] = total[...] * fade + jnp.sum(probs, axis=1, keepdims=True)
        mixed[...] = mixed[...] * fade + jnp.dot(probs.astype(BF16), keys, preferred_element_type=F32)

    def prompt(j, carry):
        begin, packed = carry
        length = span_ref[j, group]
        end = begin + length
        ctx = ctx_ref[group * 4 + j]

        def tile(t, _):
            first = pl.multiple_of(t * TILE, TILE)
            at = pl.ds(first, TILE)
            queries = jnp.concatenate([q_ref[at, h * 128 : (h + 1) * 128] for h in range(3)], axis=0)
            top[...] = jnp.full_like(top, -3e38)
            total[...] = jnp.zeros_like(total)
            mixed[...] = jnp.zeros_like(mixed)

            def old_keys(i, _):
                keys = cache_ref[j, pl.ds(pl.multiple_of(i * KEYS, KEYS), KEYS), :]
                col = lax.broadcasted_iota(jnp.int32, (1, KEYS), 1) + i * KEYS
                fold(queries, keys, jnp.where(col < ctx, 0.0, -1e30))
                return 0

            lax.fori_loop(0, (ctx + KEYS - 1) // KEYS, old_keys, 0)

            def new_keys(i, _):
                keys = kv_ref[pl.ds(pl.multiple_of(i * NEW_KEYS, NEW_KEYS), NEW_KEYS), :]
                col = lax.broadcasted_iota(jnp.int32, (3 * TILE, NEW_KEYS), 1) + i * NEW_KEYS
                row = lax.broadcasted_iota(jnp.int32, (3 * TILE, NEW_KEYS), 0) % TILE + first
                fold(queries, keys, jnp.where((col >= begin) & (col <= row), 0.0, -1e30))
                return 0

            lax.fori_loop(begin // NEW_KEYS, (first + TILE - 1) // NEW_KEYS + 1, new_keys, 0)
            out = mixed[...] / total[...]
            side = jnp.concatenate([out[h * TILE : (h + 1) * TILE, 64:] for h in range(3)], axis=1)
            row = lax.broadcasted_iota(jnp.int32, side.shape, 0) + first
            mine = (row >= begin) & (row < end)
            attn_ref[at, :] = jnp.where(mine, side, attn_ref[at, :].astype(F32)).astype(BF16)
            return 0

        lax.fori_loop(begin // TILE, (end + TILE - 1) // TILE, tile, 0)

        def pack(i, _):
            dst = pl.ds(pl.multiple_of(packed + i * 16, 16), 16)
            kvx_ref[dst, :] = kv_wide[pl.ds(begin + i * 16, 16), :].astype(BF16)
            return 0

        chunks = (length + 15) // 16
        lax.fori_loop(0, chunks, pack, 0)
        return end, packed + chunks * 16

    kv_wide[pl.ds(tokens, 16), :] = jnp.zeros((16, 128), F32)
    kvx_ref[...] = jnp.zeros_like(kvx_ref)
    attn_ref[...] = jnp.zeros_like(attn_ref)
    lax.fori_loop(0, 4, prompt, (0, 0))
    expert = lax.broadcasted_iota(jnp.int32, (32, 128), 0)
    gates = jnp.zeros((32, 128), F32)
    for k in range(8):
        hit = routes_ref[k : k + 1, :] == expert
        gates = gates + jnp.where(hit, gates_ref[k : k + 1, :].astype(F32), 0.0)
    kvx_ref[pl.ds(GATE_ROW, 32), :] = gates.astype(BF16)

    x, z = group // 4, group % 4

    @pl.loop(0, 18)
    def _(i):
        asked, member = prompt_ref[i] // 4, prompt_ref[i] % 4
        first = ((asked // 4 - x + 4) % 4 * 4 + (asked % 4 - z + 4) % 4) * KV_ROWS
        for j in range(3):
            first = first + jnp.where(j < member, (span_ref[j, asked] + 15) // 16 * 16, 0)
        place_rows_ref[0, place_ref[i]] = first // 16
        place_rows_ref[1, place_ref[i]] = span_ref[member, asked]


def attend(q, kv, cache, routes_t, gates_t, span_t, ctx, req_prompt, cache_slot):
    tokens = q.shape[0]
    return pl.pallas_call(
        attend_kernel,
        name="attend",
        out_shape=(
            jax.ShapeDtypeStruct((tokens, 192), BF16),
            jax.ShapeDtypeStruct((KV_ROWS, 128), BF16),
            jax.ShapeDtypeStruct((2, 18), jnp.int32),
        ),
        in_specs=[vmem()] * 5 + [smem()] * 4,
        out_specs=(vmem(), vmem(), smem()),
        scratch_shapes=[
            pltpu.VMEM((tokens + 16, 128), F32),
            pltpu.VMEM((3 * TILE, 1), F32),
            pltpu.VMEM((3 * TILE, 1), F32),
            pltpu.VMEM((3 * TILE, 128), F32),
        ],
        compiler_params=pltpu.CompilerParams(vmem_limit_bytes=VMEM_BYTES),
    )(q, kv, cache, routes_t, gates_t, span_t, ctx, req_prompt, cache_slot)


GROUPS = (
    ((0, 0), (0, 1), (0, 3), (1, 0), (3, 0)),
    ((0, 2), (2, 0), (1, 1), (1, 3), (3, 1), (3, 3)),
    ((2, 2), (2, 1), (2, 3), (1, 2), (3, 2)),
)


def slot_of(which, first, second):
    return first * 4 + second if which == 0 else second * 4 + first


class Line:
    def __init__(self, make, ssem, rsem, base, outs, passes):
        self.copies = [
            make(src, dst, ssem.at[base + i], rsem.at[base + i], to)
            for i, (src, dst, to) in enumerate(outs + passes)
        ]

    def out(self):
        self.copies[0].start()
        self.copies[1].start()

    def forward(self):
        self.copies[0].wait_recv()
        self.copies[2].start()
        self.copies[1].wait_recv()
        self.copies[3].start()

    def finish(self):
        self.copies[2].wait_recv()
        self.copies[3].wait_recv()

    def drain(self):
        for one in self.copies:
            one.wait_send()


def remote(axis):
    def make(src, dst, send, recv, to):
        return pltpu.make_async_remote_copy(
            src_ref=src, dst_ref=dst, send_sem=send, recv_sem=recv, device_id={axis: to}, device_id_type=MESH
        )

    return make


def gather_lines(buf, rows, ssem, rsem, ring):
    half, quarter = rows // 2, rows // 4
    lines = []
    for which in (0, 1):
        plus, minus = ring[which]
        plus2, minus2 = ring[1 - which]
        low = which * half

        def part(first, second, piece, which=which, low=low):
            row, count = {"all": (low, half), "a": (low, quarter), "b": (low + quarter, quarter)}[piece]
            return buf(slot_of(which, first, second), row, count)

        def along(base, at, p, m, part=part):
            return Line(
                remote("req"), ssem, rsem, base,
                [(part(*at(0), "all"), part(*at(3), "all"), p), (part(*at(0), "all"), part(*at(1), "all"), m)],
                [(part(*at(3), "a"), part(*at(2), "a"), p), (part(*at(1), "b"), part(*at(2), "b"), m)],
            )

        these = [along(which * 20, lambda k: (k, 0), plus, minus)]
        for i in range(4):
            these.append(along(which * 20 + 4 + 4 * i, lambda k, i=i: (i, k), plus2, minus2))
        lines.append(these)
    return lines


def gather_steps(lines):
    def both(*steps):
        for one in lines:
            for index, name in steps:
                getattr(one[index], name)()

    return [
        lambda: both((0, "out"), (1, "out")),
        lambda: both((0, "forward"), (4, "out"), (2, "out")),
        lambda: both((1, "forward")),
        lambda: both((0, "finish"), (3, "out")),
        lambda: both((4, "forward"), (2, "forward")),
        lambda: both((1, "finish")),
        lambda: both((3, "forward")),
        lambda: both((4, "finish"), (2, "finish")),
        lambda: both((3, "finish")),
        lambda: [line.drain() for one in lines for line in one],
    ]


def finish_kernel(
    attn_ref, wout_ref, hidden_ref, gain_ref, kvx_ref, place_ref, wgu_hbm, wd_hbm,
    out_ref, cache_hbm,
    wgu, wd, part, pin, head_half, head_full, resid, kvall, rows_in, sums, red_half, red_full,
    gates, ranks, picked, acts, outs, staged,
    wsem, csem, hssem, hrsem, kssem, krsem, assem, arsem, rssem, rrsem,
):
    width = hidden_ref.shape[1]
    r = lax.axis_index("req")
    x, z = r // 4, r % 4
    xp, xm = ((x + 1) % 4) * 4 + z, ((x + 3) % 4) * 4 + z
    zp, zm = x * 4 + (z + 1) % 4, x * 4 + (z + 3) % 4
    ring = ((xp, xm), (zp, zm))
    y, c, partner, up, down = head_neighbours()
    wait_all = greet(
        [("head", partner), ("head", up), ("head", down), ("req", xp), ("req", xm), ("req", zp), ("req", zm)]
    )
    loads = [
        pltpu.make_async_copy(wgu_hbm, wgu, wsem.at[0]),
        pltpu.make_async_copy(wd_hbm, wd, wsem.at[1]),
        pltpu.make_async_copy(kvx_ref, kvall.at[pl.ds(0, KV_ROWS), :], wsem.at[2]),
    ]
    loads[2].start()
    for one in loads[:2]:
        one.start()
    kvall[pl.ds(16 * KV_ROWS, 512), :] = jnp.zeros((512, 128), BF16)
    loads[2].wait()
    wait_all()

    kv_lines = gather_lines(
        lambda slot, row, count: kvall.at[pl.ds(slot * KV_ROWS + row, count), :], KV_ROWS, kssem, krsem, ring
    )
    kv_steps = gather_steps(kv_lines)
    row_lines = gather_lines(
        lambda slot, row, count: rows_in.at[slot, pl.ds(row, count), :], 128, assem, arsem, ring
    )
    row_steps = gather_steps(row_lines)
    kv_steps[0]()

    def project(dy, dc, store, extra=()):
        target = ((y + dy) % 4) * 2 + (c + dc) % 2
        own = attn_ref[pl.ds(pl.multiple_of(target * 128, 128), 128), :]

        @pl.loop(0, width // 256)
        def _(n):
            cols = pl.ds(pl.multiple_of(n * 256, 256), 256)
            total = jnp.dot(own, wout_ref[:, cols], preferred_element_type=F32)
            store(cols, total)

    def into(index):
        def store(cols, total):
            part[index, :, cols] = total.astype(BF16)

        return store

    make = remote("head")
    low, high = pl.ds(0, 64), pl.ds(64, 64)
    to_partner = {
        dy: make(part.at[2 * dy + 1], pin.at[dy], hssem.at[dy], hrsem.at[dy], partner) for dy in range(4)
    }
    halves = [
        make(part.at[4, low], head_half.at[0], hssem.at[4], hrsem.at[4], up),
        make(part.at[4, high], head_half.at[1], hssem.at[5], hrsem.at[5], down),
    ]
    fulls = [
        make(part.at[2], head_full.at[0], hssem.at[6], hrsem.at[6], up),
        make(part.at[6], head_full.at[1], hssem.at[7], hrsem.at[7], down),
    ]
    for dy in (2, 1, 3, 0):
        project(dy, 1, into(2 * dy + 1))
        to_partner[dy].start()

    to_partner[2].wait_recv()

    def store_two(cols, total):
        part[4, :, cols] = (total + pin[2, :, cols].astype(F32)).astype(BF16)

    project(2, 0, store_two)
    for one in halves:
        one.start()
    kv_steps[1]()
    to_partner[1].wait_recv()
    halves[0].wait_recv()

    def store_one(cols, total):
        total = total + pin[1, :, cols].astype(F32)
        part[2, low, cols] = (total[:64] + head_half[0, :, cols].astype(F32)).astype(BF16)
        part[2, high, cols] = total[64:].astype(BF16)

    project(1, 0, store_one)
    fulls[0].start()
    to_partner[3].wait_recv()
    halves[1].wait_recv()

    def store_three(cols, total):
        total = total + pin[3, :, cols].astype(F32)
        part[6, low, cols] = total[:64].astype(BF16)
        part[6, high, cols] = (total[64:] + head_half[1, :, cols].astype(F32)).astype(BF16)

    project(3, 0, store_three)
    fulls[1].start()
    kv_steps[2]()
    kv_steps[3]()
    kv_steps[4]()
    to_partner[0].wait_recv()
    fulls[0].wait_recv()
    fulls[1].wait_recv()

    def store_own(cols, total):
        total = total + pin[0, :, cols].astype(F32) + hidden_ref[:, cols].astype(F32)
        total = total + head_full[0, :, cols].astype(F32) + head_full[1, :, cols].astype(F32)
        resid[:, cols] = total

    project(0, 0, store_own)

    @pl.loop(0, 8)
    def _(i):
        at = pl.ds(pl.multiple_of(i * 16, 16), 16)
        rows_in[0, at, :] = rms(resid[at, :], gain_ref[...]).astype(BF16)

    row_steps[0]()
    kv_steps[5]()
    kv_steps[6]()
    kv_steps[7]()
    kv_steps[8]()
    expert = lax.broadcasted_iota(jnp.int32, (32, 128), 0)

    @pl.loop(0, 16)
    def _(slot):
        table = kvall[pl.ds(pl.multiple_of(slot * KV_ROWS + GATE_ROW, 16), 32), :].astype(F32)
        for j in range(2):
            mine = jnp.sum(jnp.where(expert == r * 2 + j, table, 0.0), axis=0, keepdims=True)
            gates[pl.ds(slot * 2 + j, 1), :] = mine

    before = lax.broadcasted_iota(jnp.int32, (128, 128), 0) < lax.broadcasted_iota(jnp.int32, (128, 128), 1)
    hits = jnp.where(gates[...] > 0.0, 1.0, 0.0).astype(BF16)
    ranks[...] = jnp.dot(hits, jnp.where(before, 1.0, 0.0).astype(BF16), preferred_element_type=F32)

    def chosen(slot, weighted):
        place = lax.broadcasted_iota(jnp.int32, (CAP, 128), 0).astype(F32)
        maps = []
        for j in range(2):
            gate = gates[slot * 2 + j : slot * 2 + j + 1, :]
            value = gate if weighted else 1.0
            hit = (ranks[slot * 2 + j : slot * 2 + j + 1, :] == place) & (gate > 0.0)
            maps.append(jnp.where(hit, value, 0.0))
        return jnp.concatenate(maps, axis=0).astype(BF16)

    def experts(group):
        count = len(group) * CAP
        for k, (a, b) in enumerate(group):
            slot = a * 4 + b
            select = chosen(slot, False)

            @pl.loop(0, width // 512)
            def _(n, k=k, slot=slot, select=select):
                cols = pl.ds(pl.multiple_of(n * 512, 512), 512)
                got = jnp.dot(select, rows_in[slot, :, cols], preferred_element_type=F32).astype(BF16)
                picked[0, pl.ds(k * CAP, CAP), cols] = got[:CAP]
                picked[1, pl.ds(k * CAP, CAP), cols] = got[CAP:]

        @pl.loop(0, 2)
        def _(e):
            @pl.loop(0, 2)
            def _(n):
                cols = pl.ds(pl.multiple_of(n * 256, 256), 256)
                later = pl.ds(pl.multiple_of(n * 256 + 512, 256), 256)
                own = picked[e, pl.ds(0, count), :]
                gate = jnp.dot(own, wgu[e, :, cols], preferred_element_type=F32)
                lift = jnp.dot(own, wgu[e, :, later], preferred_element_type=F32)
                acts[pl.ds(0, count), cols] = (gate / (1.0 + jnp.exp(-gate)) * lift).astype(BF16)

            @pl.loop(0, width // 256)
            def _(n):
                cols = pl.ds(pl.multiple_of(n * 256, 256), 256)
                outs[e, pl.ds(0, count), cols] = jnp.dot(
                    acts[pl.ds(0, count), :], wd[e, :, cols], preferred_element_type=F32
                ).astype(BF16)

        for k, (a, b) in enumerate(group):
            slot = a * 4 + b
            spread = chosen(slot, True)

            @pl.loop(0, width // 512)
            def _(n, k=k, slot=slot, spread=spread):
                cols = pl.ds(pl.multiple_of(n * 512, 512), 512)
                given = jnp.concatenate(
                    [outs[0, pl.ds(k * CAP, CAP), cols], outs[1, pl.ds(k * CAP, CAP), cols]], axis=0
                )
                sums[slot, :, cols] = lax.dot_general(
                    spread, given, (((0,), (0,)), ((), ())), preferred_element_type=F32
                ).astype(BF16)

    def add(dst, row, src, count):
        @pl.loop(0, count // 16)
        def _(i):
            to = pl.ds(pl.multiple_of(row + i * 16, 16), 16)
            at = pl.ds(pl.multiple_of(i * 16, 16), 16)
            total = sums[dst, to, :].astype(F32)
            for one in src:
                total = total + one[at, :].astype(F32)
            sums[dst, to, :] = total.astype(BF16)

    def reduce_line(n, which, at, plus, minus):
        base = which * 64
        send = remote("req")

        def piece(k, row, count):
            return sums.at[at(k), pl.ds(base + row, count), :]

        s = [rssem.at[4 * n + i] for i in range(4)]
        g = [rrsem.at[4 * n + i] for i in range(4)]
        copies = [
            send(piece(2, 0, 32), red_half.at[n, 0], s[0], g[0], plus),
            send(piece(2, 32, 32), red_half.at[n, 1], s[1], g[1], minus),
            send(piece(1, 0, 64), red_full.at[n, 0], s[2], g[2], plus),
            send(piece(3, 0, 64), red_full.at[n, 1], s[3], g[3], minus),
        ]

        def out():
            copies[0].start()
            copies[1].start()

        def middle():
            copies[0].wait_recv()
            add(at(1), base, [red_half.at[n, 0]], 32)
            copies[2].start()
            copies[1].wait_recv()
            add(at(3), base + 32, [red_half.at[n, 1]], 32)
            copies[3].start()

        def last():
            copies[2].wait_recv()
            copies[3].wait_recv()

        def fold():
            last()
            add(at(0), base, [red_full.at[n, 0], red_full.at[n, 1]], 64)

        def drain():
            for one in copies:
                one.wait_send()

        return out, middle, fold, last, drain

    back = []
    for which in (0, 1):
        plus, minus = ring[which]
        plus2, minus2 = ring[1 - which]
        these = [
            reduce_line(which * 5 + i, which, lambda k, i=i, w=which: slot_of(w, i, k), plus2, minus2)
            for i in range(4)
        ]
        these.append(reduce_line(which * 5 + 4, which, lambda k, w=which: slot_of(w, k, 0), plus, minus))
        back.append(these)

    def go(line, step):
        for these in back:
            these[line][step]()

    row_steps[1]()
    row_steps[2]()
    for one in loads[:2]:
        one.wait()
    experts(GROUPS[0])
    row_steps[3]()
    row_steps[4]()

    @pl.loop(0, 18)
    def _(s):
        start, length = place_ref[0, s], place_ref[1, s]
        for i in range(4):
            rows = kvall[pl.ds(start * 16 + i * 128, 128), :].astype(F32)
            at = lax.broadcasted_iota(jnp.int32, (128, 128), 0) + i * 128
            staged[s, pl.ds(i * 128, 128), :] = jnp.where(at < length, rows, 0.0).astype(BF16)

    store = pltpu.make_async_copy(staged, cache_hbm, csem.at[0])
    store.start()
    row_steps[5]()
    experts(GROUPS[1])
    go(0, 0)
    row_steps[6]()
    row_steps[7]()
    go(0, 1)
    row_steps[8]()
    experts(GROUPS[2])
    go(2, 0)
    go(1, 0)
    go(3, 0)
    go(0, 2)
    go(2, 1)
    go(1, 1)
    go(3, 1)
    go(2, 2)
    go(4, 0)
    go(1, 2)
    go(3, 2)
    go(4, 1)
    go(4, 3)
    for which, n in ((0, 4), (1, 9)):
        @pl.loop(0, 4)
        def _(i, which=which, n=n):
            to = pl.ds(pl.multiple_of(which * 64 + i * 16, 16), 16)
            at = pl.ds(pl.multiple_of(i * 16, 16), 16)
            total = resid[to, :] + sums[0, to, :].astype(F32)
            total = total + red_full[n, 0, at, :].astype(F32) + red_full[n, 1, at, :].astype(F32)
            out_ref[to, :] = total.astype(BF16)

    for dy in range(4):
        to_partner[dy].wait_send()
    for one in halves + fulls:
        one.wait_send()
    kv_steps[9]()
    row_steps[9]()
    for line in range(5):
        go(line, 4)
    store.wait()


def finish(attn, w_out, hidden, gain, kvx, place_rows, w_gate_up, w_down):
    rows, width = hidden.shape
    most = max(len(group) for group in GROUPS) * CAP
    return pl.pallas_call(
        finish_kernel,
        name="finish",
        out_shape=(
            jax.ShapeDtypeStruct((rows, width), BF16),
            jax.ShapeDtypeStruct((18, 512, 128), BF16),
        ),
        in_specs=[vmem()] * 5 + [smem()] + [anyspace()] * 2,
        out_specs=(vmem(), anyspace()),
        scratch_shapes=[
            pltpu.VMEM(w_gate_up.shape, BF16),
            pltpu.VMEM(w_down.shape, BF16),
            pltpu.VMEM((8, rows, width), BF16),
            pltpu.VMEM((4, rows, width), BF16),
            pltpu.VMEM((2, rows // 2, width), BF16),
            pltpu.VMEM((2, rows, width), BF16),
            pltpu.VMEM((rows, width), F32),
            pltpu.VMEM((16 * KV_ROWS + 512, 128), BF16),
            pltpu.VMEM((16, rows, width), BF16),
            pltpu.VMEM((16, rows, width), BF16),
            pltpu.VMEM((10, 2, rows // 4, width), BF16),
            pltpu.VMEM((10, 2, rows // 2, width), BF16),
            pltpu.VMEM((32, 128), F32),
            pltpu.VMEM((32, 128), F32),
            pltpu.VMEM((2, most, width), BF16),
            pltpu.VMEM((most, w_down.shape[1]), BF16),
            pltpu.VMEM((2, most, width), BF16),
            pltpu.VMEM((18, 512, 128), BF16),
            pltpu.SemaphoreType.DMA((3,)),
            pltpu.SemaphoreType.DMA((1,)),
            pltpu.SemaphoreType.DMA((8,)),
            pltpu.SemaphoreType.DMA((8,)),
            pltpu.SemaphoreType.DMA((40,)),
            pltpu.SemaphoreType.DMA((40,)),
            pltpu.SemaphoreType.DMA((40,)),
            pltpu.SemaphoreType.DMA((40,)),
            pltpu.SemaphoreType.DMA((40,)),
            pltpu.SemaphoreType.DMA((40,)),
        ],
        compiler_params=pltpu.CompilerParams(
            collective_id=1, has_side_effects=True, vmem_limit_bytes=VMEM_BYTES
        ),
    )(attn, w_out, hidden, gain, kvx, place_rows, w_gate_up, w_down)


def body(
    hidden_in, attn_gain, w_query, keyvalue_weight, w_out, cache_kv, ctx_len, span_len,
    ffn_gain, routes, gate_weights, w_gate_up, w_down, req_prompt, cache_slot,
):
    width = hidden_in.shape[1]
    prompts_dev = cache_kv.shape[0]
    span_t = span_len.T
    lane = jnp.arange(128)
    freq = (ROPE_BASE ** (-2.0 * (lane % 32).astype(F32) / 64.0))[None, :]
    q, kv = project_tokens(
        hidden_in, attn_gain[None, :], w_query.T, keyvalue_weight.reshape(width, 128), freq, span_t, ctx_len
    )
    attn, kvx, place_rows = attend(
        q, kv, cache_kv.reshape(prompts_dev, -1, 128), routes.T, gate_weights.T, span_t, ctx_len,
        req_prompt, cache_slot,
    )
    layer_out, cache = finish(
        attn, w_out, hidden_in, ffn_gain[None, :], kvx, place_rows, w_gate_up, w_down
    )
    return (layer_out, cache.reshape(18, 512, 1, 128))


def solution(mesh):
    placed = (
        P(("req", "head"), None),
        P(),
        P(None, "head"),
        P(None, "head", None),
        P("head", None),
        P("req", None, "head", None),
        P(),
        P(),
        P(),
        P(("req", "head"), None),
        P(("req", "head"), None),
        P("req", None, None),
        P("req", None, None),
        P("req"),
        P("req"),
    )
    return jax.shard_map(
        body,
        mesh=mesh,
        in_specs=placed,
        out_specs=(P(("req", "head"), None), P("req", None, "head", None)),
        check_vma=False,
    )
```

```python
import functools

import jax
import jax.numpy as jnp
from jax import lax
from jax.experimental import pallas as pl
from jax.experimental.pallas import tpu as pltpu
from jax.sharding import PartitionSpec as P

CAP = 48
EPSILON = 1e-05
ROPE_BASE = 10000.0
LOG2E = 1.4426950408889634
MESH = pl.DeviceIdType.MESH
F32 = jnp.float32
BF16 = jnp.bfloat16
VMEM_BYTES = 60 * 1024 * 1024
KV_ROWS = 1152
GATE_ROW = 1088


def vmem():
    return pl.BlockSpec(memory_space=pltpu.VMEM)


def smem():
    return pl.BlockSpec(memory_space=pltpu.SMEM)


def anyspace():
    return pl.BlockSpec(memory_space=pl.ANY)


def rms(values, gain):
    mean_sq = jnp.mean(values * values, axis=-1, keepdims=True)
    return values * lax.rsqrt(mean_sq + EPSILON) * gain


def head_neighbours():
    hd = lax.axis_index("head")
    y, c = hd // 2, hd % 2
    partner = y * 2 + (1 - c)
    up = ((y + 1) % 4) * 2 + c
    down = ((y + 3) % 4) * 2 + c
    return y, c, partner, up, down


def greet(neighbours):
    barrier = pltpu.get_barrier_semaphore()
    for axis, where in neighbours:
        pl.semaphore_signal(barrier, inc=1, device_id={axis: where}, device_id_type=MESH)
    return lambda: pl.semaphore_wait(barrier, len(neighbours))


def project_kernel(
    hidden_ref, gain_ref, wq_ref, wkv_ref, freq_ref, span_ref, ctx_ref,
    q_ref, kv_ref,
    tok, wq_wide, cos_tab, sin_tab, ssem, rsem,
):
    rows = hidden_ref.shape[0]
    half = rows // 2
    group = lax.axis_index("req")
    y, c, partner, up, down = head_neighbours()
    wait_all = greet([("head", partner), ("head", up), ("head", down)])
    tok[0] = rms(hidden_ref[...].astype(F32), gain_ref[...]).astype(BF16)
    wait_all()

    def copy(i, src, dst, to):
        return pltpu.make_async_remote_copy(
            src_ref=src, dst_ref=dst, send_sem=ssem.at[i], recv_sem=rsem.at[i],
            device_id={"head": to}, device_id_type=MESH,
        )

    low, high = pl.ds(0, half), pl.ds(half, half)
    copies = [
        copy(0, tok.at[0], tok.at[6], up),
        copy(1, tok.at[0], tok.at[2], down),
        copy(2, tok.at[0], tok.at[1], partner),
        copy(3, tok.at[6, low], tok.at[4, low], up),
        copy(4, tok.at[6], tok.at[7], partner),
        copy(5, tok.at[2, high], tok.at[4, high], down),
        copy(6, tok.at[2], tok.at[3], partner),
        copy(7, tok.at[4], tok.at[5], partner),
    ]
    for i in (0, 1, 2):
        copies[i].start()

    wq_wide[...] = jnp.zeros_like(wq_wide)
    for h in range(3):
        wq_wide[pl.ds(h * 128, 64), :] = wq_ref[pl.ds(h * 64, 64), :]

    lane = lax.broadcasted_iota(jnp.int32, (rows, 128), 1)

    @pl.loop(0, 8)
    def _(block):
        within = lax.broadcasted_iota(jnp.int32, (rows, 128), 0) + block * rows
        position = jnp.zeros((rows, 128), jnp.int32)
        begin = 0
        for j in range(4):
            shift = ctx_ref[group * 4 + j] - begin
            position = jnp.where(within >= begin, within + shift, position)
            begin = begin + span_ref[j, group]
        angles = position.astype(F32) * freq_ref[...]
        where_rows = pl.ds(pl.multiple_of(block * rows, rows), rows)
        cos_tab[where_rows, :] = jnp.where(lane < 64, jnp.cos(angles), 1.0)
        sine = jnp.sin(angles)
        sin_tab[where_rows, :] = jnp.where(lane < 32, -sine, jnp.where(lane < 64, sine, 0.0))

    def project(slot):
        block = ((y + slot // 2) % 4) * 2 + (c + slot % 2) % 2
        at = pl.ds(pl.multiple_of(block * rows, rows), rows)
        cosine, sine = cos_tab[at, :], sin_tab[at, :]

        def turn(values):
            other = jnp.where(lane < 32, pltpu.roll(values, 96, 1), pltpu.roll(values, 32, 1))
            return (values * cosine + other * sine).astype(BF16)

        own = tok[slot]
        wide = lax.dot_general(own, wq_wide[...], (((1,), (1,)), ((), ())), preferred_element_type=F32)
        for h in range(3):
            q_ref[at, h * 128 : (h + 1) * 128] = turn(wide[:, h * 128 : (h + 1) * 128])
        kv_ref[at, :] = turn(jnp.dot(own, wkv_ref[...], preferred_element_type=F32))

    project(0)
    copies[0].wait_recv()
    copies[3].start()
    copies[4].start()
    copies[1].wait_recv()
    copies[5].start()
    copies[6].start()
    copies[2].wait_recv()
    project(1)
    project(6)
    project(2)
    copies[3].wait_recv()
    copies[5].wait_recv()
    copies[7].start()
    copies[4].wait_recv()
    project(7)
    copies[6].wait_recv()
    project(3)
    project(4)
    copies[7].wait_recv()
    project(5)
    for one in copies:
        one.wait_send()


def project_tokens(hidden, gain, wq_t, wkv, freq, span_t, ctx):
    rows, width = hidden.shape
    tokens = rows * 8
    return pl.pallas_call(
        project_kernel,
        name="project_tokens",
        out_shape=(
            jax.ShapeDtypeStruct((tokens, 384), BF16),
            jax.ShapeDtypeStruct((tokens, 128), BF16),
        ),
        in_specs=[vmem()] * 5 + [smem()] * 2,
        out_specs=(vmem(), vmem()),
        scratch_shapes=[
            pltpu.VMEM((8, rows, width), BF16),
            pltpu.VMEM((384, width), BF16),
            pltpu.VMEM((tokens, 128), F32),
            pltpu.VMEM((tokens, 128), F32),
            pltpu.SemaphoreType.DMA((8,)),
            pltpu.SemaphoreType.DMA((8,)),
        ],
        compiler_params=pltpu.CompilerParams(
            collective_id=0, has_side_effects=True, vmem_limit_bytes=VMEM_BYTES
        ),
    )(hidden, gain, wq_t, wkv, freq, span_t, ctx)


KEYS = 256
LONG = 4
TILE = 128


def attend_kernel(
    q_ref, kv_ref, cache_ref, routes_ref, gates_ref, span_ref, ctx_ref, prompt_ref, place_ref,
    attn_ref, kvx_ref, place_rows_ref,
    kv_wide, old_turned, new_turned, attn_turned, near, top, total, mixed,
):
    group = lax.axis_index("req")
    tokens = q_ref.shape[0]
    kv_wide[pl.ds(0, tokens), :] = kv_ref[...].astype(F32)
    scale = LOG2E / 8.0

    def score(queries, keys):
        return lax.dot_general(keys, queries, (((1,), (1,)), ((), ())), preferred_element_type=F32)

    def mix(scores, values):
        probs = jnp.exp2(scores * scale - top[...])
        total[...] += jnp.sum(probs.reshape(-1, 8, probs.shape[1]), axis=0)
        mixed[...] += jnp.dot(values, probs.astype(BF16), preferred_element_type=F32)

    def new_rows(i):
        return kv_ref[pl.ds(pl.multiple_of(i * KEYS, KEYS), KEYS), :]

    @pl.loop(0, tokens // KEYS)
    def _(i):
        new_turned[i] = new_rows(i).T[64:, :]

    def prompt(j, carry):
        begin, packed = carry
        length = span_ref[j, group]
        end = begin + length
        ctx = ctx_ref[group * 4 + j]
        long = ctx // (LONG * KEYS)
        whole = ctx // KEYS
        new_first = begin // KEYS
        most_chunks = cache_ref.shape[1] // KEYS

        def old_rows(i, count):
            return cache_ref[j, pl.ds(pl.multiple_of(i * KEYS, KEYS), count * KEYS), :]

        @pl.loop(0, (ctx + KEYS - 1) // KEYS)
        def _(i):
            old_turned[i] = old_rows(i, 1).T[64:, :]

        def tile(t, _):
            first = pl.multiple_of(t * TILE, TILE)
            at = pl.ds(first, TILE)
            queries = jnp.concatenate([q_ref[at, h * 128 : (h + 1) * 128] for h in range(3)], axis=0)
            total[...] = jnp.zeros_like(total)
            mixed[...] = jnp.zeros_like(mixed)
            lane_row = lax.broadcasted_iota(jnp.int32, (1, 3 * TILE), 1) % TILE + first
            own_lane = (lane_row >= begin) & (lane_row < end)
            new_last = (first + TILE - 1) // KEYS

            def new_scores(i):
                scores = score(queries, new_rows(i))
                key = lax.broadcasted_iota(jnp.int32, (KEYS, TILE), 0) + i * KEYS
                row = lax.broadcasted_iota(jnp.int32, (KEYS, TILE), 1) + first
                bias = jnp.where((key >= begin) & (key <= row), 0.0, -1e30)
                return scores + jnp.concatenate([bias] * 3, axis=1)

            def last_old():
                scores = score(queries, old_rows(jnp.minimum(whole, most_chunks - 1), 1))
                key = lax.broadcasted_iota(jnp.int32, scores.shape, 0)
                return jnp.where(key < ctx - whole * KEYS, scores, -1e30)

            near[...] = new_scores(new_last)
            top[...] = jnp.where(own_lane, jnp.max(near[...], axis=0, keepdims=True) * scale, 1e30)
            mix(near[...], new_turned[new_last])

            @pl.loop(new_first, new_last)
            def _(i):
                mix(new_scores(i), new_turned[i])

            @pl.loop(0, long)
            def _(i):
                values = jnp.concatenate([old_turned[i * LONG + k] for k in range(LONG)], axis=1)
                mix(score(queries, old_rows(i * LONG, LONG)), values)

            @pl.loop(long * LONG, whole)
            def _(i):
                mix(score(queries, old_rows(i, 1)), old_turned[i])

            @pl.when(ctx > whole * KEYS)
            def _():
                mix(last_old(), old_turned[whole])

            @pl.when(jnp.max(jnp.where(own_lane, jnp.max(total[...], axis=0, keepdims=True), 0.0)) > 2.0**64)
            def _():
                def higher(scores):
                    return jnp.max(scores, axis=0, keepdims=True)

                most = higher(near[...])
                most = lax.fori_loop(new_first, new_last, lambda i, m: jnp.maximum(m, higher(new_scores(i))), most)
                most = lax.fori_loop(
                    0, whole, lambda i, m: jnp.maximum(m, higher(score(queries, old_rows(i, 1)))), most
                )
                last = jnp.where(ctx > whole * KEYS, 0.0, -1e30)
                most = jnp.maximum(most, higher(last_old()) + last)
                top[...] = jnp.where(own_lane, most * scale, 1e30)
                total[...] = jnp.zeros_like(total)
                mixed[...] = jnp.zeros_like(mixed)

                @pl.loop(new_first, new_last + 1)
                def _(i):
                    mix(new_scores(i), new_turned[i])

                @pl.loop(0, whole)
                def _(i):
                    mix(score(queries, old_rows(i, 1)), old_turned[i])

                @pl.when(ctx > whole * KEYS)
                def _():
                    mix(last_old(), old_turned[whole])

            out = mixed[...] / jnp.sum(total[...], axis=0, keepdims=True)
            side = jnp.concatenate([out[:, h * TILE : (h + 1) * TILE] for h in range(3)], axis=0)
            row = lax.broadcasted_iota(jnp.int32, side.shape, 1) + first
            mine = (row >= begin) & (row < end)
            attn_turned[t] = jnp.where(mine, side, attn_turned[t])
            return 0

        lax.fori_loop(begin // TILE, (end + TILE - 1) // TILE, tile, 0)

        def pack(i, _):
            dst = pl.ds(pl.multiple_of(packed + i * 16, 16), 16)
            kvx_ref[dst, :] = kv_wide[pl.ds(begin + i * 16, 16), :].astype(BF16)
            return 0

        chunks = (length + 15) // 16
        lax.fori_loop(0, chunks, pack, 0)
        return end, packed + chunks * 16

    kv_wide[pl.ds(tokens, 16), :] = jnp.zeros((16, 128), F32)
    kvx_ref[...] = jnp.zeros_like(kvx_ref)
    attn_turned[...] = jnp.zeros_like(attn_turned)
    lax.fori_loop(0, 4, prompt, (0, 0))

    @pl.loop(0, tokens // TILE)
    def _(t):
        attn_ref[pl.ds(pl.multiple_of(t * TILE, TILE), TILE), :] = attn_turned[t].T.astype(BF16)

    expert = lax.broadcasted_iota(jnp.int32, (32, 128), 0)
    gates = jnp.zeros((32, 128), F32)
    for k in range(8):
        hit = routes_ref[k : k + 1, :] == expert
        gates = gates + jnp.where(hit, gates_ref[k : k + 1, :].astype(F32), 0.0)
    kvx_ref[pl.ds(GATE_ROW, 32), :] = gates.astype(BF16)

    x, z = group // 4, group % 4

    for i in range(18):
        asked, member = prompt_ref[i] // 4, prompt_ref[i] % 4
        first = ((asked // 4 - x + 4) % 4 * 4 + (asked % 4 - z + 4) % 4) * KV_ROWS
        for j in range(3):
            first = first + jnp.where(j < member, (span_ref[j, asked] + 15) // 16 * 16, 0)
        place_rows_ref[0, place_ref[i]] = first // 16
        place_rows_ref[1, place_ref[i]] = span_ref[member, asked]


def attend(q, kv, cache, routes_t, gates_t, span_t, ctx, req_prompt, cache_slot):
    tokens = q.shape[0]
    return pl.pallas_call(
        attend_kernel,
        name="attend",
        out_shape=(
            jax.ShapeDtypeStruct((tokens, 192), BF16),
            jax.ShapeDtypeStruct((KV_ROWS, 128), BF16),
            jax.ShapeDtypeStruct((2, 18), jnp.int32),
        ),
        in_specs=[vmem()] * 5 + [smem()] * 4,
        out_specs=(vmem(), vmem(), smem()),
        scratch_shapes=[
            pltpu.VMEM((tokens + 16, 128), F32),
            pltpu.VMEM((cache.shape[1] // KEYS + 1, 64, KEYS), BF16),
            pltpu.VMEM((tokens // KEYS, 64, KEYS), BF16),
            pltpu.VMEM((tokens // TILE, 192, TILE), F32),
            pltpu.VMEM((KEYS, 3 * TILE), F32),
            pltpu.VMEM((1, 3 * TILE), F32),
            pltpu.VMEM((8, 3 * TILE), F32),
            pltpu.VMEM((64, 3 * TILE), F32),
        ],
        compiler_params=pltpu.CompilerParams(vmem_limit_bytes=VMEM_BYTES),
    )(q, kv, cache, routes_t, gates_t, span_t, ctx, req_prompt, cache_slot)


GROUPS = (
    ((0, 0), (0, 1), (0, 3), (1, 0), (3, 0)),
    ((0, 2), (2, 0), (1, 1), (1, 3), (3, 1), (3, 3)),
    ((2, 2), (2, 1), (2, 3), (1, 2), (3, 2)),
)


def slot_of(which, first, second):
    return first * 4 + second if which == 0 else second * 4 + first


class Line:
    def __init__(self, make, ssem, rsem, base, outs, passes):
        self.copies = [
            make(src, dst, ssem.at[base + i], rsem.at[base + i], to)
            for i, (src, dst, to) in enumerate(outs + passes)
        ]

    def out(self):
        self.copies[0].start()
        self.copies[1].start()

    def forward(self):
        self.copies[0].wait_recv()
        self.copies[2].start()
        self.copies[1].wait_recv()
        self.copies[3].start()

    def finish(self):
        self.copies[2].wait_recv()
        self.copies[3].wait_recv()

    def drain(self):
        for one in self.copies:
            one.wait_send()


def remote(axis):
    def make(src, dst, send, recv, to):
        return pltpu.make_async_remote_copy(
            src_ref=src, dst_ref=dst, send_sem=send, recv_sem=recv, device_id={axis: to}, device_id_type=MESH
        )

    return make


def gather_lines(buf, rows, ssem, rsem, ring):
    half, quarter = rows // 2, rows // 4
    lines = []
    for which in (0, 1):
        plus, minus = ring[which]
        plus2, minus2 = ring[1 - which]
        low = which * half

        def part(first, second, piece, which=which, low=low):
            row, count = {"all": (low, half), "a": (low, quarter), "b": (low + quarter, quarter)}[piece]
            return buf(slot_of(which, first, second), row, count)

        def along(base, at, p, m, part=part):
            return Line(
                remote("req"), ssem, rsem, base,
                [(part(*at(0), "all"), part(*at(3), "all"), p), (part(*at(0), "all"), part(*at(1), "all"), m)],
                [(part(*at(3), "a"), part(*at(2), "a"), p), (part(*at(1), "b"), part(*at(2), "b"), m)],
            )

        these = [along(which * 20, lambda k: (k, 0), plus, minus)]
        for i in range(4):
            these.append(along(which * 20 + 4 + 4 * i, lambda k, i=i: (i, k), plus2, minus2))
        lines.append(these)
    return lines


def gather_steps(lines):
    def both(*steps):
        for one in lines:
            for index, name in steps:
                getattr(one[index], name)()

    return [
        lambda: both((0, "out"), (1, "out")),
        lambda: both((0, "forward"), (4, "out"), (2, "out")),
        lambda: both((1, "forward")),
        lambda: both((0, "finish"), (3, "out")),
        lambda: both((4, "forward"), (2, "forward")),
        lambda: both((1, "finish")),
        lambda: both((3, "forward")),
        lambda: both((4, "finish"), (2, "finish")),
        lambda: both((3, "finish")),
        lambda: [line.drain() for one in lines for line in one],
    ]


def finish_kernel(
    attn_ref, wout_ref, hidden_ref, gain_ref, kvx_ref, place_ref, wgu_hbm, wd_hbm,
    out_ref, cache_hbm,
    wgu, wd, part, pin, head_half, head_full, resid, kvall, rows_in, sums, red_half, red_full,
    gates, ranks, picked, acts, outs, staged,
    wsem, csem, hssem, hrsem, kssem, krsem, assem, arsem, rssem, rrsem,
):
    width = hidden_ref.shape[1]
    r = lax.axis_index("req")
    x, z = r // 4, r % 4
    xp, xm = ((x + 1) % 4) * 4 + z, ((x + 3) % 4) * 4 + z
    zp, zm = x * 4 + (z + 1) % 4, x * 4 + (z + 3) % 4
    ring = ((xp, xm), (zp, zm))
    y, c, partner, up, down = head_neighbours()
    wait_all = greet(
        [("head", partner), ("head", up), ("head", down), ("req", xp), ("req", xm), ("req", zp), ("req", zm)]
    )
    loads = [
        pltpu.make_async_copy(wgu_hbm, wgu, wsem.at[0]),
        pltpu.make_async_copy(wd_hbm, wd, wsem.at[1]),
        pltpu.make_async_copy(kvx_ref, kvall.at[pl.ds(0, KV_ROWS), :], wsem.at[2]),
    ]
    loads[2].start()
    for one in loads[:2]:
        one.start()
    kvall[pl.ds(16 * KV_ROWS, 512), :] = jnp.zeros((512, 128), BF16)
    loads[2].wait()
    wait_all()

    kv_lines = gather_lines(
        lambda slot, row, count: kvall.at[pl.ds(slot * KV_ROWS + row, count), :], KV_ROWS, kssem, krsem, ring
    )
    kv_steps = gather_steps(kv_lines)
    row_lines = gather_lines(
        lambda slot, row, count: rows_in.at[slot, pl.ds(row, count), :], 128, assem, arsem, ring
    )
    row_steps = gather_steps(row_lines)
    kv_steps[0]()

    def project(dy, dc, store, extra=()):
        target = ((y + dy) % 4) * 2 + (c + dc) % 2
        own = attn_ref[pl.ds(pl.multiple_of(target * 128, 128), 128), :]

        @pl.loop(0, width // 256)
        def _(n):
            cols = pl.ds(pl.multiple_of(n * 256, 256), 256)
            total = jnp.dot(own, wout_ref[:, cols], preferred_element_type=F32)
            store(cols, total)

    def into(index):
        def store(cols, total):
            part[index, :, cols] = total.astype(BF16)

        return store

    make = remote("head")
    low, high = pl.ds(0, 64), pl.ds(64, 64)
    to_partner = {
        dy: make(part.at[2 * dy + 1], pin.at[dy], hssem.at[dy], hrsem.at[dy], partner) for dy in range(4)
    }
    halves = [
        make(part.at[4, low], head_half.at[0], hssem.at[4], hrsem.at[4], up),
        make(part.at[4, high], head_half.at[1], hssem.at[5], hrsem.at[5], down),
    ]
    fulls = [
        make(part.at[2], head_full.at[0], hssem.at[6], hrsem.at[6], up),
        make(part.at[6], head_full.at[1], hssem.at[7], hrsem.at[7], down),
    ]
    for dy in (2, 1, 3, 0):
        project(dy, 1, into(2 * dy + 1))
        to_partner[dy].start()

    to_partner[2].wait_recv()

    def store_two(cols, total):
        part[4, :, cols] = (total + pin[2, :, cols].astype(F32)).astype(BF16)

    project(2, 0, store_two)
    for one in halves:
        one.start()
    kv_steps[1]()
    to_partner[1].wait_recv()
    halves[0].wait_recv()

    def store_one(cols, total):
        total = total + pin[1, :, cols].astype(F32)
        part[2, low, cols] = (total[:64] + head_half[0, :, cols].astype(F32)).astype(BF16)
        part[2, high, cols] = total[64:].astype(BF16)

    project(1, 0, store_one)
    fulls[0].start()
    to_partner[3].wait_recv()
    halves[1].wait_recv()

    def store_three(cols, total):
        total = total + pin[3, :, cols].astype(F32)
        part[6, low, cols] = total[:64].astype(BF16)
        part[6, high, cols] = (total[64:] + head_half[1, :, cols].astype(F32)).astype(BF16)

    project(3, 0, store_three)
    fulls[1].start()
    kv_steps[2]()
    kv_steps[3]()
    kv_steps[4]()
    to_partner[0].wait_recv()
    fulls[0].wait_recv()
    fulls[1].wait_recv()

    def store_own(cols, total):
        total = total + pin[0, :, cols].astype(F32) + hidden_ref[:, cols].astype(F32)
        total = total + head_full[0, :, cols].astype(F32) + head_full[1, :, cols].astype(F32)
        resid[:, cols] = total

    project(0, 0, store_own)

    @pl.loop(0, 8)
    def _(i):
        at = pl.ds(pl.multiple_of(i * 16, 16), 16)
        rows_in[0, at, :] = rms(resid[at, :], gain_ref[...]).astype(BF16)

    row_steps[0]()
    kv_steps[5]()
    kv_steps[6]()
    kv_steps[7]()
    kv_steps[8]()
    expert = lax.broadcasted_iota(jnp.int32, (32, 128), 0)

    @pl.loop(0, 16)
    def _(slot):
        table = kvall[pl.ds(pl.multiple_of(slot * KV_ROWS + GATE_ROW, 16), 32), :].astype(F32)
        for j in range(2):
            mine = jnp.sum(jnp.where(expert == r * 2 + j, table, 0.0), axis=0, keepdims=True)
            gates[pl.ds(slot * 2 + j, 1), :] = mine

    before = lax.broadcasted_iota(jnp.int32, (128, 128), 0) < lax.broadcasted_iota(jnp.int32, (128, 128), 1)
    hits = jnp.where(gates[...] > 0.0, 1.0, 0.0).astype(BF16)
    ranks[...] = jnp.dot(hits, jnp.where(before, 1.0, 0.0).astype(BF16), preferred_element_type=F32)

    def chosen(slot, weighted):
        place = lax.broadcasted_iota(jnp.int32, (CAP, 128), 0).astype(F32)
        maps = []
        for j in range(2):
            gate = gates[slot * 2 + j : slot * 2 + j + 1, :]
            value = gate if weighted else 1.0
            hit = (ranks[slot * 2 + j : slot * 2 + j + 1, :] == place) & (gate > 0.0)
            maps.append(jnp.where(hit, value, 0.0))
        return jnp.concatenate(maps, axis=0).astype(BF16)

    def experts(group):
        count = len(group) * CAP
        for k, (a, b) in enumerate(group):
            slot = a * 4 + b
            select = chosen(slot, False)

            @pl.loop(0, width // 512)
            def _(n, k=k, slot=slot, select=select):
                cols = pl.ds(pl.multiple_of(n * 512, 512), 512)
                got = jnp.dot(select, rows_in[slot, :, cols], preferred_element_type=F32).astype(BF16)
                picked[0, pl.ds(k * CAP, CAP), cols] = got[:CAP]
                picked[1, pl.ds(k * CAP, CAP), cols] = got[CAP:]

        @pl.loop(0, 2)
        def _(e):
            @pl.loop(0, 2)
            def _(n):
                cols = pl.ds(pl.multiple_of(n * 256, 256), 256)
                later = pl.ds(pl.multiple_of(n * 256 + 512, 256), 256)
                own = picked[e, pl.ds(0, count), :]
                gate = jnp.dot(own, wgu[e, :, cols], preferred_element_type=F32)
                lift = jnp.dot(own, wgu[e, :, later], preferred_element_type=F32)
                acts[pl.ds(0, count), cols] = (gate / (1.0 + jnp.exp(-gate)) * lift).astype(BF16)

            @pl.loop(0, width // 256)
            def _(n):
                cols = pl.ds(pl.multiple_of(n * 256, 256), 256)
                outs[e, pl.ds(0, count), cols] = jnp.dot(
                    acts[pl.ds(0, count), :], wd[e, :, cols], preferred_element_type=F32
                ).astype(BF16)

        for k, (a, b) in enumerate(group):
            slot = a * 4 + b
            spread = chosen(slot, True)

            @pl.loop(0, width // 512)
            def _(n, k=k, slot=slot, spread=spread):
                cols = pl.ds(pl.multiple_of(n * 512, 512), 512)
                given = jnp.concatenate(
                    [outs[0, pl.ds(k * CAP, CAP), cols], outs[1, pl.ds(k * CAP, CAP), cols]], axis=0
                )
                sums[slot, :, cols] = lax.dot_general(
                    spread, given, (((0,), (0,)), ((), ())), preferred_element_type=F32
                ).astype(BF16)

    def add(dst, row, src, count):
        @pl.loop(0, count // 16)
        def _(i):
            to = pl.ds(pl.multiple_of(row + i * 16, 16), 16)
            at = pl.ds(pl.multiple_of(i * 16, 16), 16)
            total = sums[dst, to, :].astype(F32)
            for one in src:
                total = total + one[at, :].astype(F32)
            sums[dst, to, :] = total.astype(BF16)

    def reduce_line(n, which, at, plus, minus):
        base = which * 64
        send = remote("req")

        def piece(k, row, count):
            return sums.at[at(k), pl.ds(base + row, count), :]

        s = [rssem.at[4 * n + i] for i in range(4)]
        g = [rrsem.at[4 * n + i] for i in range(4)]
        copies = [
            send(piece(2, 0, 32), red_half.at[n, 0], s[0], g[0], plus),
            send(piece(2, 32, 32), red_half.at[n, 1], s[1], g[1], minus),
            send(piece(1, 0, 64), red_full.at[n, 0], s[2], g[2], plus),
            send(piece(3, 0, 64), red_full.at[n, 1], s[3], g[3], minus),
        ]

        def out():
            copies[0].start()
            copies[1].start()

        def middle():
            copies[0].wait_recv()
            add(at(1), base, [red_half.at[n, 0]], 32)
            copies[2].start()
            copies[1].wait_recv()
            add(at(3), base + 32, [red_half.at[n, 1]], 32)
            copies[3].start()

        def last():
            copies[2].wait_recv()
            copies[3].wait_recv()

        def fold():
            last()
            add(at(0), base, [red_full.at[n, 0], red_full.at[n, 1]], 64)

        def drain():
            for one in copies:
                one.wait_send()

        return out, middle, fold, last, drain

    back = []
    for which in (0, 1):
        plus, minus = ring[which]
        plus2, minus2 = ring[1 - which]
        these = [
            reduce_line(which * 5 + i, which, lambda k, i=i, w=which: slot_of(w, i, k), plus2, minus2)
            for i in range(4)
        ]
        these.append(reduce_line(which * 5 + 4, which, lambda k, w=which: slot_of(w, k, 0), plus, minus))
        back.append(these)

    def go(line, step):
        for these in back:
            these[line][step]()

    row_steps[1]()
    row_steps[2]()
    for one in loads[:2]:
        one.wait()
    experts(GROUPS[0])
    row_steps[3]()
    row_steps[4]()

    @pl.loop(0, 18)
    def _(s):
        start, length = place_ref[0, s], place_ref[1, s]
        for i in range(4):
            rows = kvall[pl.ds(start * 16 + i * 128, 128), :].astype(F32)
            at = lax.broadcasted_iota(jnp.int32, (128, 128), 0) + i * 128
            staged[s, pl.ds(i * 128, 128), :] = jnp.where(at < length, rows, 0.0).astype(BF16)

    store = pltpu.make_async_copy(staged, cache_hbm, csem.at[0])
    store.start()
    row_steps[5]()
    experts(GROUPS[1])
    go(0, 0)
    row_steps[6]()
    row_steps[7]()
    go(0, 1)
    row_steps[8]()
    experts(GROUPS[2])
    go(2, 0)
    go(1, 0)
    go(3, 0)
    go(0, 2)
    go(2, 1)
    go(1, 1)
    go(3, 1)
    go(2, 2)
    go(4, 0)
    go(1, 2)
    go(3, 2)
    go(4, 1)
    go(4, 3)
    for which, n in ((0, 4), (1, 9)):
        @pl.loop(0, 4)
        def _(i, which=which, n=n):
            to = pl.ds(pl.multiple_of(which * 64 + i * 16, 16), 16)
            at = pl.ds(pl.multiple_of(i * 16, 16), 16)
            total = resid[to, :] + sums[0, to, :].astype(F32)
            total = total + red_full[n, 0, at, :].astype(F32) + red_full[n, 1, at, :].astype(F32)
            out_ref[to, :] = total.astype(BF16)

    for dy in range(4):
        to_partner[dy].wait_send()
    for one in halves + fulls:
        one.wait_send()
    kv_steps[9]()
    row_steps[9]()
    for line in range(5):
        go(line, 4)
    store.wait()


def finish(attn, w_out, hidden, gain, kvx, place_rows, w_gate_up, w_down):
    rows, width = hidden.shape
    most = max(len(group) for group in GROUPS) * CAP
    return pl.pallas_call(
        finish_kernel,
        name="finish",
        out_shape=(
            jax.ShapeDtypeStruct((rows, width), BF16),
            jax.ShapeDtypeStruct((18, 512, 128), BF16),
        ),
        in_specs=[vmem()] * 5 + [smem()] + [anyspace()] * 2,
        out_specs=(vmem(), anyspace()),
        scratch_shapes=[
            pltpu.VMEM(w_gate_up.shape, BF16),
            pltpu.VMEM(w_down.shape, BF16),
            pltpu.VMEM((8, rows, width), BF16),
            pltpu.VMEM((4, rows, width), BF16),
            pltpu.VMEM((2, rows // 2, width), BF16),
            pltpu.VMEM((2, rows, width), BF16),
            pltpu.VMEM((rows, width), F32),
            pltpu.VMEM((16 * KV_ROWS + 512, 128), BF16),
            pltpu.VMEM((16, rows, width), BF16),
            pltpu.VMEM((16, rows, width), BF16),
            pltpu.VMEM((10, 2, rows // 4, width), BF16),
            pltpu.VMEM((10, 2, rows // 2, width), BF16),
            pltpu.VMEM((32, 128), F32),
            pltpu.VMEM((32, 128), F32),
            pltpu.VMEM((2, most, width), BF16),
            pltpu.VMEM((most, w_down.shape[1]), BF16),
            pltpu.VMEM((2, most, width), BF16),
            pltpu.VMEM((18, 512, 128), BF16),
            pltpu.SemaphoreType.DMA((3,)),
            pltpu.SemaphoreType.DMA((1,)),
            pltpu.SemaphoreType.DMA((8,)),
            pltpu.SemaphoreType.DMA((8,)),
            pltpu.SemaphoreType.DMA((40,)),
            pltpu.SemaphoreType.DMA((40,)),
            pltpu.SemaphoreType.DMA((40,)),
            pltpu.SemaphoreType.DMA((40,)),
            pltpu.SemaphoreType.DMA((40,)),
            pltpu.SemaphoreType.DMA((40,)),
        ],
        compiler_params=pltpu.CompilerParams(
            collective_id=1, has_side_effects=True, vmem_limit_bytes=VMEM_BYTES
        ),
    )(attn, w_out, hidden, gain, kvx, place_rows, w_gate_up, w_down)


def body(
    hidden_in, attn_gain, w_query, keyvalue_weight, w_out, cache_kv, ctx_len, span_len,
    ffn_gain, routes, gate_weights, w_gate_up, w_down, req_prompt, cache_slot,
):
    width = hidden_in.shape[1]
    prompts_dev = cache_kv.shape[0]
    span_t = span_len.T
    lane = jnp.arange(128)
    freq = (ROPE_BASE ** (-2.0 * (lane % 32).astype(F32) / 64.0))[None, :]
    q, kv = project_tokens(
        hidden_in, attn_gain[None, :], w_query.T, keyvalue_weight.reshape(width, 128), freq, span_t, ctx_len
    )
    attn, kvx, place_rows = attend(
        q, kv, cache_kv.reshape(prompts_dev, -1, 128), routes.T, gate_weights.T, span_t, ctx_len,
        req_prompt, cache_slot,
    )
    layer_out, cache = finish(
        attn, w_out, hidden_in, ffn_gain[None, :], kvx, place_rows, w_gate_up, w_down
    )
    return (layer_out, cache.reshape(18, 512, 1, 128))


def solution(mesh):
    placed = (
        P(("req", "head"), None),
        P(),
        P(None, "head"),
        P(None, "head", None),
        P("head", None),
        P("req", None, "head", None),
        P(),
        P(),
        P(),
        P(("req", "head"), None),
        P(("req", "head"), None),
        P("req", None, None),
        P("req", None, None),
        P("req"),
        P("req"),
    )
    return jax.shard_map(
        body,
        mesh=mesh,
        in_specs=placed,
        out_specs=(P(("req", "head"), None), P("req", None, "head", None)),
        check_vma=False,
    )
```

```python
import functools

import jax
import jax.numpy as jnp
import numpy as np
from jax import lax
from jax.experimental import pallas as pl
from jax.experimental.pallas import tpu as pltpu
from jax.sharding import PartitionSpec as P

CAP = 48
EPSILON = 1e-05
ROPE_BASE = 10000.0
LOG2E = 1.4426950408889634
MESH = pl.DeviceIdType.MESH
F32 = jnp.float32
BF16 = jnp.bfloat16
VMEM_BYTES = 60 * 1024 * 1024
KV_ROWS = 1152
GATE_ROW = 1088


def vmem():
    return pl.BlockSpec(memory_space=pltpu.VMEM)


def smem():
    return pl.BlockSpec(memory_space=pltpu.SMEM)


def anyspace():
    return pl.BlockSpec(memory_space=pl.ANY)


def rms(values, gain):
    mean_sq = jnp.mean(values * values, axis=-1, keepdims=True)
    return values * lax.rsqrt(mean_sq + EPSILON) * gain


def head_neighbours():
    hd = lax.axis_index("head")
    y, c = hd // 2, hd % 2
    partner = y * 2 + (1 - c)
    up = ((y + 1) % 4) * 2 + c
    down = ((y + 3) % 4) * 2 + c
    return y, c, partner, up, down


def greet(neighbours):
    barrier = pltpu.get_barrier_semaphore()
    for axis, where in neighbours:
        pl.semaphore_signal(barrier, inc=1, device_id={axis: where}, device_id_type=MESH)
    return lambda: pl.semaphore_wait(barrier, len(neighbours))


def project_kernel(
    hidden_ref, gain_ref, wq_ref, wkv_ref, freq_ref, span_ref, ctx_ref,
    q_ref, kv_ref,
    tok, wq_wide, cos_tab, sin_tab, ssem, rsem,
):
    rows = hidden_ref.shape[0]
    half = rows // 2
    group = lax.axis_index("req")
    y, c, partner, up, down = head_neighbours()
    wait_all = greet([("head", partner), ("head", up), ("head", down)])
    tok[0] = rms(hidden_ref[...].astype(F32), gain_ref[...].reshape(1, -1)).astype(BF16)
    wait_all()

    def copy(i, src, dst, to):
        return pltpu.make_async_remote_copy(
            src_ref=src, dst_ref=dst, send_sem=ssem.at[i], recv_sem=rsem.at[i],
            device_id={"head": to}, device_id_type=MESH,
        )

    low, high = pl.ds(0, half), pl.ds(half, half)
    copies = [
        copy(0, tok.at[0, low], tok.at[6, low], up),
        copy(1, tok.at[0, high], tok.at[2, high], down),
        copy(2, tok.at[0], tok.at[1], partner),
        copy(3, tok.at[6, low], tok.at[4, low], up),
        copy(4, tok.at[6], tok.at[7], partner),
        copy(5, tok.at[2, high], tok.at[4, high], down),
        copy(6, tok.at[2], tok.at[3], partner),
        copy(7, tok.at[4, low], tok.at[5, low], partner),
        copy(8, tok.at[0, high], tok.at[6, high], up),
        copy(9, tok.at[0, low], tok.at[2, low], down),
        copy(10, tok.at[4, high], tok.at[5, high], partner),
    ]
    for i in (0, 1, 8, 9, 2):
        copies[i].start()

    wq_wide[...] = jnp.zeros_like(wq_wide)
    for h in range(3):
        wq_wide[pl.ds(h * 128, 64), :] = wq_ref[pl.ds(h * 64, 64), :]

    lane = lax.broadcasted_iota(jnp.int32, (rows, 128), 1)

    @pl.loop(0, 8)
    def _(block):
        within = lax.broadcasted_iota(jnp.int32, (rows, 128), 0) + block * rows
        position = jnp.zeros((rows, 128), jnp.int32)
        begin = 0
        for j in range(4):
            shift = ctx_ref[group * 4 + j] - begin
            position = jnp.where(within >= begin, within + shift, position)
            begin = begin + span_ref[j, group]
        angles = position.astype(F32) * freq_ref[...]
        where_rows = pl.ds(pl.multiple_of(block * rows, rows), rows)
        cos_tab[where_rows, :] = jnp.where(lane < 64, jnp.cos(angles), 1.0)
        sine = jnp.sin(angles)
        sin_tab[where_rows, :] = jnp.where(lane < 32, -sine, jnp.where(lane < 64, sine, 0.0))

    def project(slot):
        block = ((y + slot // 2) % 4) * 2 + (c + slot % 2) % 2
        at = pl.ds(pl.multiple_of(block * rows, rows), rows)
        cosine, sine = cos_tab[at, :], sin_tab[at, :]

        def turn(values):
            other = jnp.where(lane < 32, pltpu.roll(values, 96, 1), pltpu.roll(values, 32, 1))
            return (values * cosine + other * sine).astype(BF16)

        own = tok[slot]
        wide = lax.dot_general(own, wq_wide[...], (((1,), (1,)), ((), ())), preferred_element_type=F32)
        for h in range(3):
            q_ref[at, h * 128 : (h + 1) * 128] = turn(wide[:, h * 128 : (h + 1) * 128])
        kv_ref[at, :] = turn(jnp.dot(own, wkv_ref[...], preferred_element_type=F32))

    copies[0].wait_recv()
    copies[3].start()
    copies[1].wait_recv()
    copies[5].start()
    project(0)
    copies[2].wait_recv()
    project(1)
    copies[8].wait_recv()
    copies[4].start()
    copies[9].wait_recv()
    copies[6].start()
    project(6)
    project(2)
    copies[3].wait_recv()
    copies[7].start()
    copies[5].wait_recv()
    copies[10].start()
    copies[4].wait_recv()
    project(7)
    copies[6].wait_recv()
    project(3)
    project(4)
    copies[7].wait_recv()
    copies[10].wait_recv()
    project(5)
    for one in copies:
        one.wait_send()


def project_tokens(hidden, gain, wq_t, wkv, freq, span_t, ctx):
    rows, width = hidden.shape
    tokens = rows * 8
    return pl.pallas_call(
        project_kernel,
        name="project_tokens",
        out_shape=(
            jax.ShapeDtypeStruct((tokens, 384), BF16),
            jax.ShapeDtypeStruct((tokens, 128), BF16),
        ),
        in_specs=[vmem()] * 5 + [smem()] * 2,
        out_specs=(vmem(), vmem()),
        scratch_shapes=[
            pltpu.VMEM((8, rows, width), BF16),
            pltpu.VMEM((384, width), BF16),
            pltpu.VMEM((tokens, 128), F32),
            pltpu.VMEM((tokens, 128), F32),
            pltpu.SemaphoreType.DMA((11,)),
            pltpu.SemaphoreType.DMA((11,)),
        ],
        compiler_params=pltpu.CompilerParams(
            collective_id=0, has_side_effects=True, vmem_limit_bytes=VMEM_BYTES
        ),
    )(hidden, gain, wq_t, wkv, freq, span_t, ctx)


KEYS = 256
LONG = 4
TILE = 128


def attend_kernel(
    q_ref, kv_ref, cache_ref, routes_ref, gates_ref, span_ref, ctx_ref, prompt_ref, place_ref,
    attn_ref, kvx_ref, place_rows_ref,
    kv_wide, old_turned, new_turned, attn_turned, near, top, total, mixed,
):
    group = lax.axis_index("req")
    tokens = q_ref.shape[0]
    kv_wide[pl.ds(0, tokens), :] = kv_ref[...].astype(F32)
    scale = LOG2E / 8.0

    def score(queries, keys):
        return lax.dot_general(keys, queries, (((1,), (1,)), ((), ())), preferred_element_type=F32)

    def mix(scores, values):
        probs = jnp.exp2(scores * scale - top[...])
        total[...] += jnp.sum(probs.reshape(-1, 8, probs.shape[1]), axis=0)
        mixed[...] += jnp.dot(values, probs.astype(BF16), preferred_element_type=F32)

    def new_rows(i):
        return kv_ref[pl.ds(pl.multiple_of(i * KEYS, KEYS), KEYS), :]

    @pl.loop(0, tokens // KEYS)
    def _(i):
        new_turned[i] = new_rows(i).T[64:, :]

    def prompt(j, carry):
        begin, packed = carry
        length = span_ref[j, group]
        end = begin + length
        ctx = ctx_ref[group * 4 + j]
        long = ctx // (LONG * KEYS)
        whole = ctx // KEYS
        new_first = begin // KEYS
        most_chunks = cache_ref.shape[1] // KEYS

        def old_rows(i, count):
            return cache_ref[j, pl.ds(pl.multiple_of(i * KEYS, KEYS), count * KEYS), :]

        @pl.loop(0, (ctx + KEYS - 1) // KEYS)
        def _(i):
            old_turned[i] = old_rows(i, 1).T[64:, :]

        def tile(t, _):
            first = pl.multiple_of(t * TILE, TILE)
            at = pl.ds(first, TILE)
            queries = jnp.concatenate([q_ref[at, h * 128 : (h + 1) * 128] for h in range(3)], axis=0)
            total[...] = jnp.zeros_like(total)
            mixed[...] = jnp.zeros_like(mixed)
            lane_row = lax.broadcasted_iota(jnp.int32, (1, 3 * TILE), 1) % TILE + first
            own_lane = (lane_row >= begin) & (lane_row < end)
            new_last = (first + TILE - 1) // KEYS

            def new_scores(i):
                scores = score(queries, new_rows(i))
                key = lax.broadcasted_iota(jnp.int32, (KEYS, TILE), 0) + i * KEYS
                row = lax.broadcasted_iota(jnp.int32, (KEYS, TILE), 1) + first
                bias = jnp.where((key >= begin) & (key <= row), 0.0, -1e30)
                return scores + jnp.concatenate([bias] * 3, axis=1)

            def last_old():
                scores = score(queries, old_rows(jnp.minimum(whole, most_chunks - 1), 1))
                key = lax.broadcasted_iota(jnp.int32, scores.shape, 0)
                return jnp.where(key < ctx - whole * KEYS, scores, -1e30)

            near[...] = new_scores(new_last)
            top[...] = jnp.where(own_lane, jnp.max(near[...], axis=0, keepdims=True) * scale, 1e30)
            mix(near[...], new_turned[new_last])

            @pl.loop(new_first, new_last)
            def _(i):
                mix(new_scores(i), new_turned[i])

            @pl.loop(0, long)
            def _(i):
                values = jnp.concatenate([old_turned[i * LONG + k] for k in range(LONG)], axis=1)
                mix(score(queries, old_rows(i * LONG, LONG)), values)

            @pl.loop(long * LONG, whole)
            def _(i):
                mix(score(queries, old_rows(i, 1)), old_turned[i])

            @pl.when(ctx > whole * KEYS)
            def _():
                mix(last_old(), old_turned[whole])

            @pl.when(jnp.max(jnp.where(own_lane, jnp.max(total[...], axis=0, keepdims=True), 0.0)) > 2.0**64)
            def _():
                def higher(scores):
                    return jnp.max(scores, axis=0, keepdims=True)

                most = higher(near[...])
                most = lax.fori_loop(new_first, new_last, lambda i, m: jnp.maximum(m, higher(new_scores(i))), most)
                most = lax.fori_loop(
                    0, whole, lambda i, m: jnp.maximum(m, higher(score(queries, old_rows(i, 1)))), most
                )
                last = jnp.where(ctx > whole * KEYS, 0.0, -1e30)
                most = jnp.maximum(most, higher(last_old()) + last)
                top[...] = jnp.where(own_lane, most * scale, 1e30)
                total[...] = jnp.zeros_like(total)
                mixed[...] = jnp.zeros_like(mixed)

                @pl.loop(new_first, new_last + 1)
                def _(i):
                    mix(new_scores(i), new_turned[i])

                @pl.loop(0, whole)
                def _(i):
                    mix(score(queries, old_rows(i, 1)), old_turned[i])

                @pl.when(ctx > whole * KEYS)
                def _():
                    mix(last_old(), old_turned[whole])

            out = mixed[...] / jnp.sum(total[...], axis=0, keepdims=True)
            side = jnp.concatenate([out[:, h * TILE : (h + 1) * TILE] for h in range(3)], axis=0)
            row = lax.broadcasted_iota(jnp.int32, side.shape, 1) + first
            mine = (row >= begin) & (row < end)
            attn_turned[t] = jnp.where(mine, side, attn_turned[t])
            return 0

        lax.fori_loop(begin // TILE, (end + TILE - 1) // TILE, tile, 0)

        def pack(i, _):
            dst = pl.ds(pl.multiple_of(packed + i * 16, 16), 16)
            kvx_ref[dst, :] = kv_wide[pl.ds(begin + i * 16, 16), :].astype(BF16)
            return 0

        chunks = (length + 15) // 16
        lax.fori_loop(0, chunks, pack, 0)
        return end, packed + chunks * 16

    kv_wide[pl.ds(tokens, 16), :] = jnp.zeros((16, 128), F32)
    kvx_ref[...] = jnp.zeros_like(kvx_ref)
    attn_turned[...] = jnp.zeros_like(attn_turned)
    lax.fori_loop(0, 4, prompt, (0, 0))

    @pl.loop(0, tokens // TILE)
    def _(t):
        attn_ref[pl.ds(pl.multiple_of(t * TILE, TILE), TILE), :] = attn_turned[t].T.astype(BF16)

    expert = lax.broadcasted_iota(jnp.int32, (32, 128), 0)
    gates = jnp.zeros((32, 128), F32)
    for k in range(8):
        hit = routes_ref[k : k + 1, :] == expert
        gates = gates + jnp.where(hit, gates_ref[k : k + 1, :].astype(F32), 0.0)
    kvx_ref[pl.ds(GATE_ROW, 32), :] = gates.astype(BF16)

    x, z = group // 4, group % 4

    for i in range(18):
        asked, member = prompt_ref[i] // 4, prompt_ref[i] % 4
        first = ((asked // 4 - x + 4) % 4 * 4 + (asked % 4 - z + 4) % 4) * KV_ROWS
        for j in range(3):
            first = first + jnp.where(j < member, (span_ref[j, asked] + 15) // 16 * 16, 0)
        place_rows_ref[0, place_ref[i]] = first // 16
        place_rows_ref[1, place_ref[i]] = span_ref[member, asked]


def attend(q, kv, cache, routes_t, gates_t, span_t, ctx, req_prompt, cache_slot):
    tokens = q.shape[0]
    return pl.pallas_call(
        attend_kernel,
        name="attend",
        out_shape=(
            jax.ShapeDtypeStruct((tokens, 192), BF16),
            jax.ShapeDtypeStruct((KV_ROWS, 128), BF16),
            jax.ShapeDtypeStruct((2, 18), jnp.int32),
        ),
        in_specs=[vmem()] * 5 + [smem()] * 4,
        out_specs=(vmem(), vmem(), smem()),
        scratch_shapes=[
            pltpu.VMEM((tokens + 16, 128), F32),
            pltpu.VMEM((cache.shape[1] // KEYS + 1, 64, KEYS), BF16),
            pltpu.VMEM((tokens // KEYS, 64, KEYS), BF16),
            pltpu.VMEM((tokens // TILE, 192, TILE), F32),
            pltpu.VMEM((KEYS, 3 * TILE), F32),
            pltpu.VMEM((1, 3 * TILE), F32),
            pltpu.VMEM((8, 3 * TILE), F32),
            pltpu.VMEM((64, 3 * TILE), F32),
        ],
        compiler_params=pltpu.CompilerParams(vmem_limit_bytes=VMEM_BYTES),
    )(q, kv, cache, routes_t, gates_t, span_t, ctx, req_prompt, cache_slot)


GROUPS = (
    ((0, 0), (0, 1), (0, 3), (1, 0), (3, 0)),
    ((0, 2), (2, 0), (1, 1), (1, 3), (3, 1), (3, 3)),
    ((2, 2), (2, 1), (2, 3), (1, 2), (3, 2)),
)


def slot_of(which, first, second):
    return first * 4 + second if which == 0 else second * 4 + first


class Line:
    def __init__(self, make, ssem, rsem, base, outs, passes):
        self.copies = [
            make(src, dst, ssem.at[base + i], rsem.at[base + i], to)
            for i, (src, dst, to) in enumerate(outs + passes)
        ]

    def out(self):
        self.copies[0].start()
        self.copies[1].start()

    def forward(self):
        self.copies[0].wait_recv()
        self.copies[2].start()
        self.copies[1].wait_recv()
        self.copies[3].start()

    def finish(self):
        self.copies[2].wait_recv()
        self.copies[3].wait_recv()

    def drain(self):
        for one in self.copies:
            one.wait_send()


def remote(axis):
    def make(src, dst, send, recv, to):
        return pltpu.make_async_remote_copy(
            src_ref=src, dst_ref=dst, send_sem=send, recv_sem=recv, device_id={axis: to}, device_id_type=MESH
        )

    return make


def gather_lines(buf, rows, ssem, rsem, ring):
    half, quarter = rows // 2, rows // 4
    lines = []
    for which in (0, 1):
        plus, minus = ring[which]
        plus2, minus2 = ring[1 - which]
        low = which * half

        def part(first, second, piece, which=which, low=low):
            row, count = {"all": (low, half), "a": (low, quarter), "b": (low + quarter, quarter)}[piece]
            return buf(slot_of(which, first, second), row, count)

        def along(base, at, p, m, part=part):
            return Line(
                remote("req"), ssem, rsem, base,
                [(part(*at(0), "all"), part(*at(3), "all"), p), (part(*at(0), "all"), part(*at(1), "all"), m)],
                [(part(*at(3), "a"), part(*at(2), "a"), p), (part(*at(1), "b"), part(*at(2), "b"), m)],
            )

        these = [along(which * 20, lambda k: (k, 0), plus, minus)]
        for i in range(4):
            these.append(along(which * 20 + 4 + 4 * i, lambda k, i=i: (i, k), plus2, minus2))
        lines.append(these)
    return lines


def gather_steps(lines):
    def both(*steps):
        for one in lines:
            for index, name in steps:
                getattr(one[index], name)()

    return [
        lambda: both((0, "out"), (1, "out")),
        lambda: both((0, "forward"), (4, "out"), (2, "out")),
        lambda: both((1, "forward")),
        lambda: both((0, "finish"), (3, "out")),
        lambda: both((4, "forward"), (2, "forward")),
        lambda: both((1, "finish")),
        lambda: both((3, "forward")),
        lambda: both((4, "finish"), (2, "finish")),
        lambda: both((3, "finish")),
        lambda: [line.drain() for one in lines for line in one],
    ]


def finish_kernel(
    attn_ref, wout_ref, hidden_ref, gain_ref, kvx_ref, place_ref, wgu_hbm, wd_hbm,
    out_ref, cache_hbm,
    wgu, wd, part, pin, head_half, head_full, kept, resid, kvall, rows_in, sums, red_half, red_full,
    gates, ranks, picked, acts, outs, staged,
    wsem, csem, hssem, hrsem, kssem, krsem, assem, arsem, rssem, rrsem,
):
    width = hidden_ref.shape[1]
    r = lax.axis_index("req")
    x, z = r // 4, r % 4
    xp, xm = ((x + 1) % 4) * 4 + z, ((x + 3) % 4) * 4 + z
    zp, zm = x * 4 + (z + 1) % 4, x * 4 + (z + 3) % 4
    ring = ((xp, xm), (zp, zm))
    y, c, partner, up, down = head_neighbours()
    wait_all = greet(
        [("head", partner), ("head", up), ("head", down), ("req", xp), ("req", xm), ("req", zp), ("req", zm)]
    )
    loads = [
        pltpu.make_async_copy(wgu_hbm, wgu, wsem.at[0]),
        pltpu.make_async_copy(wd_hbm, wd, wsem.at[1]),
        pltpu.make_async_copy(kvx_ref, kvall.at[pl.ds(0, KV_ROWS), :], wsem.at[2]),
    ]
    loads[2].start()
    for one in loads[:2]:
        one.start()
    kvall[pl.ds(16 * KV_ROWS, 512), :] = jnp.zeros((512, 128), BF16)
    loads[2].wait()
    wait_all()

    kv_lines = gather_lines(
        lambda slot, row, count: kvall.at[pl.ds(slot * KV_ROWS + row, count), :], KV_ROWS, kssem, krsem, ring
    )
    kv_steps = gather_steps(kv_lines)
    row_lines = gather_lines(
        lambda slot, row, count: rows_in.at[slot, pl.ds(row, count), :], 128, assem, arsem, ring
    )
    row_steps = gather_steps(row_lines)
    kv_steps[0]()

    wide = width // 2

    def project(dy, dc, piece, store):
        target = ((y + dy) % 4) * 2 + (c + dc) % 2
        own = attn_ref[pl.ds(pl.multiple_of(target * 128, 128), 128), :]

        @pl.loop(0, wide // 256)
        def _(n):
            cols = pl.ds(pl.multiple_of(piece * wide + n * 256, 256), 256)
            store(cols, jnp.dot(own, wout_ref[:, cols], preferred_element_type=F32))

    make = remote("head")
    low, high = pl.ds(0, 64), pl.ds(64, 64)
    pieces = [pl.ds(i * wide, wide) for i in range(2)]
    to_partner = [
        [
            make(part.at[2 * dy + 1, :, p], pin.at[dy, :, p], hssem.at[8 * i + dy], hrsem.at[8 * i + dy], partner)
            for i, p in enumerate(pieces)
        ]
        for dy in range(4)
    ]
    halves, fulls = [], []
    for i, p in enumerate(pieces):
        at = 8 * i + 4
        halves.append(
            [
                make(part.at[4, low, p], head_half.at[0, :, p], hssem.at[at], hrsem.at[at], up),
                make(part.at[4, high, p], head_half.at[1, :, p], hssem.at[at + 1], hrsem.at[at + 1], down),
            ]
        )
        fulls.append(
            [
                make(part.at[2, :, p], head_full.at[0, :, p], hssem.at[at + 2], hrsem.at[at + 2], up),
                make(part.at[6, :, p], head_full.at[1, :, p], hssem.at[at + 3], hrsem.at[at + 3], down),
            ]
        )

    def give(dy, piece):
        def store(cols, total):
            part[2 * dy + 1, :, cols] = total.astype(BF16)

        project(dy, 1, piece, store)
        to_partner[dy][piece].start()

    for i in range(2):
        give(2, i)
    for i in range(2):
        to_partner[2][i].wait_recv()

        def store_far(cols, total):
            part[4, :, cols] = (total + pin[2, :, cols].astype(F32)).astype(BF16)

        project(2, 0, i, store_far)
        halves[i][0].start()
        halves[i][1].start()
    for dy in (1, 3, 0):
        for i in range(2):
            give(dy, i)
    for k, dy in enumerate((1, 3, 0)):
        for i in range(2):

            def store_own(cols, total, k=k, dy=dy):
                kept[k, :, cols] = total + hidden_ref[:, cols].astype(F32) if dy == 0 else total

            project(dy, 0, i, store_own)
    kv_steps[1]()

    def pass_on(k, dy, index, side, piece):
        to_partner[dy][piece].wait_recv()
        halves[piece][side].wait_recv()
        reached = (0, 4) if side == 0 else (4, 8)
        for lo, hi, with_half in ((*reached, True), ((4, 8) if side == 0 else (0, 4)) + (False,)):

            @pl.loop(0, 4)
            def _(n, lo=lo, with_half=with_half):
                at = pl.ds(pl.multiple_of(lo * 16 + n * 16, 16), 16)
                cols = pieces[piece]
                total = kept[k, at, cols] + pin[dy, at, cols].astype(F32)
                if with_half:
                    total = total + head_half[side, pl.ds(pl.multiple_of(n * 16, 16), 16), cols].astype(F32)
                part[index, at, cols] = total.astype(BF16)

        fulls[piece][side].start()

    for i in range(2):
        pass_on(0, 1, 2, 0, i)
        pass_on(1, 3, 6, 1, i)
    kv_steps[2]()
    kv_steps[3]()
    kv_steps[4]()
    for i in range(2):
        to_partner[0][i].wait_recv()
        fulls[i][0].wait_recv()
        fulls[i][1].wait_recv()

        @pl.loop(0, 8)
        def _(n, i=i):
            at = pl.ds(pl.multiple_of(n * 16, 16), 16)
            cols = pieces[i]
            total = kept[2, at, cols] + pin[0, at, cols].astype(F32)
            resid[at, cols] = total + head_full[0, at, cols].astype(F32) + head_full[1, at, cols].astype(F32)

    @pl.loop(0, 8, unroll=4)
    def _(i):
        at = pl.ds(pl.multiple_of(i * 16, 16), 16)
        rows_in[0, at, :] = rms(resid[at, :], gain_ref[...].reshape(1, -1)).astype(BF16)

    row_steps[0]()
    kv_steps[5]()
    kv_steps[6]()
    kv_steps[7]()
    kv_steps[8]()
    expert = lax.broadcasted_iota(jnp.int32, (32, 128), 0)

    @pl.loop(0, 16)
    def _(slot):
        table = kvall[pl.ds(pl.multiple_of(slot * KV_ROWS + GATE_ROW, 16), 32), :].astype(F32)
        for j in range(2):
            mine = jnp.sum(jnp.where(expert == r * 2 + j, table, 0.0), axis=0, keepdims=True)
            gates[pl.ds(slot * 2 + j, 1), :] = mine

    before = lax.broadcasted_iota(jnp.int32, (128, 128), 0) < lax.broadcasted_iota(jnp.int32, (128, 128), 1)
    hits = jnp.where(gates[...] > 0.0, 1.0, 0.0).astype(BF16)
    ranks[...] = jnp.dot(hits, jnp.where(before, 1.0, 0.0).astype(BF16), preferred_element_type=F32)

    def chosen(slot, weighted):
        place = lax.broadcasted_iota(jnp.int32, (CAP, 128), 0).astype(F32)
        maps = []
        for j in range(2):
            gate = gates[slot * 2 + j : slot * 2 + j + 1, :]
            value = gate if weighted else 1.0
            hit = (ranks[slot * 2 + j : slot * 2 + j + 1, :] == place) & (gate > 0.0)
            maps.append(jnp.where(hit, value, 0.0))
        return jnp.concatenate(maps, axis=0).astype(BF16)

    def experts(group):
        count = len(group) * CAP
        for k, (a, b) in enumerate(group):
            slot = a * 4 + b
            select = chosen(slot, False)

            @pl.loop(0, width // 512)
            def _(n, k=k, slot=slot, select=select):
                cols = pl.ds(pl.multiple_of(n * 512, 512), 512)
                got = jnp.dot(select, rows_in[slot, :, cols], preferred_element_type=F32).astype(BF16)
                picked[0, pl.ds(k * CAP, CAP), cols] = got[:CAP]
                picked[1, pl.ds(k * CAP, CAP), cols] = got[CAP:]

        @pl.loop(0, 2)
        def _(e):
            @pl.loop(0, 2)
            def _(n):
                cols = pl.ds(pl.multiple_of(n * 256, 256), 256)
                later = pl.ds(pl.multiple_of(n * 256 + 512, 256), 256)
                own = picked[e, pl.ds(0, count), :]
                gate = jnp.dot(own, wgu[e, :, cols], preferred_element_type=F32)
                lift = jnp.dot(own, wgu[e, :, later], preferred_element_type=F32)
                acts[pl.ds(0, count), cols] = (gate / (1.0 + jnp.exp(-gate)) * lift).astype(BF16)

            @pl.loop(0, width // 256)
            def _(n):
                cols = pl.ds(pl.multiple_of(n * 256, 256), 256)
                outs[e, pl.ds(0, count), cols] = jnp.dot(
                    acts[pl.ds(0, count), :], wd[e, :, cols], preferred_element_type=F32
                ).astype(BF16)

        for k, (a, b) in enumerate(group):
            slot = a * 4 + b
            spread = chosen(slot, True)

            @pl.loop(0, width // 512)
            def _(n, k=k, slot=slot, spread=spread):
                cols = pl.ds(pl.multiple_of(n * 512, 512), 512)
                given = jnp.concatenate(
                    [outs[0, pl.ds(k * CAP, CAP), cols], outs[1, pl.ds(k * CAP, CAP), cols]], axis=0
                )
                sums[slot, :, cols] = lax.dot_general(
                    spread, given, (((0,), (0,)), ((), ())), preferred_element_type=F32
                ).astype(BF16)

    def add(dst, row, src, count):
        @pl.loop(0, count // 16)
        def _(i):
            to = pl.ds(pl.multiple_of(row + i * 16, 16), 16)
            at = pl.ds(pl.multiple_of(i * 16, 16), 16)
            total = sums[dst, to, :].astype(F32)
            for one in src:
                total = total + one[at, :].astype(F32)
            sums[dst, to, :] = total.astype(BF16)

    def reduce_line(n, which, at, plus, minus):
        base = which * 64
        send = remote("req")

        def piece(k, row, count):
            return sums.at[at(k), pl.ds(base + row, count), :]

        s = [rssem.at[4 * n + i] for i in range(4)]
        g = [rrsem.at[4 * n + i] for i in range(4)]
        copies = [
            send(piece(2, 0, 32), red_half.at[n, 0], s[0], g[0], plus),
            send(piece(2, 32, 32), red_half.at[n, 1], s[1], g[1], minus),
            send(piece(1, 0, 64), red_full.at[n, 0], s[2], g[2], plus),
            send(piece(3, 0, 64), red_full.at[n, 1], s[3], g[3], minus),
        ]

        def out():
            copies[0].start()
            copies[1].start()

        def middle():
            copies[0].wait_recv()
            add(at(1), base, [red_half.at[n, 0]], 32)
            copies[2].start()
            copies[1].wait_recv()
            add(at(3), base + 32, [red_half.at[n, 1]], 32)
            copies[3].start()

        def last():
            copies[2].wait_recv()
            copies[3].wait_recv()

        def fold():
            last()
            add(at(0), base, [red_full.at[n, 0], red_full.at[n, 1]], 64)

        def drain():
            for one in copies:
                one.wait_send()

        return out, middle, fold, last, drain

    back = []
    for which in (0, 1):
        plus, minus = ring[which]
        plus2, minus2 = ring[1 - which]
        these = [
            reduce_line(which * 5 + i, which, lambda k, i=i, w=which: slot_of(w, i, k), plus2, minus2)
            for i in range(4)
        ]
        these.append(reduce_line(which * 5 + 4, which, lambda k, w=which: slot_of(w, k, 0), plus, minus))
        back.append(these)

    def go(line, step):
        for these in back:
            these[line][step]()

    row_steps[1]()
    row_steps[2]()
    for one in loads[:2]:
        one.wait()
    experts(GROUPS[0])
    row_steps[3]()
    row_steps[4]()

    @pl.loop(0, 18)
    def _(s):
        start, length = place_ref[0, s], place_ref[1, s]
        for i in range(4):
            rows = kvall[pl.ds(start * 16 + i * 128, 128), :].astype(F32)
            at = lax.broadcasted_iota(jnp.int32, (128, 128), 0) + i * 128
            staged[s, pl.ds(i * 128, 128), :] = jnp.where(at < length, rows, 0.0).astype(BF16)

    store = pltpu.make_async_copy(staged, cache_hbm, csem.at[0])
    store.start()
    row_steps[5]()
    experts(GROUPS[1])
    go(0, 0)
    row_steps[6]()
    row_steps[7]()
    go(0, 1)
    row_steps[8]()
    experts(GROUPS[2])
    go(2, 0)
    go(1, 0)
    go(3, 0)
    go(0, 2)
    go(2, 1)
    go(1, 1)
    go(3, 1)
    go(2, 2)
    go(4, 0)
    go(1, 2)
    go(3, 2)
    go(4, 1)
    go(4, 3)
    for which, n in ((0, 4), (1, 9)):
        @pl.loop(0, 4)
        def _(i, which=which, n=n):
            to = pl.ds(pl.multiple_of(which * 64 + i * 16, 16), 16)
            at = pl.ds(pl.multiple_of(i * 16, 16), 16)
            total = resid[to, :] + sums[0, to, :].astype(F32)
            total = total + red_full[n, 0, at, :].astype(F32) + red_full[n, 1, at, :].astype(F32)
            out_ref[to, :] = total.astype(BF16)

    for some in to_partner + halves + fulls:
        for one in some:
            one.wait_send()
    kv_steps[9]()
    row_steps[9]()
    for line in range(5):
        go(line, 4)
    store.wait()


def finish(attn, w_out, hidden, gain, kvx, place_rows, w_gate_up, w_down):
    rows, width = hidden.shape
    most = max(len(group) for group in GROUPS) * CAP
    return pl.pallas_call(
        finish_kernel,
        name="finish",
        out_shape=(
            jax.ShapeDtypeStruct((rows, width), BF16),
            jax.ShapeDtypeStruct((18, 512, 128), BF16),
        ),
        in_specs=[vmem()] * 5 + [smem()] + [anyspace()] * 2,
        out_specs=(vmem(), anyspace()),
        scratch_shapes=[
            pltpu.VMEM(w_gate_up.shape, BF16),
            pltpu.VMEM(w_down.shape, BF16),
            pltpu.VMEM((8, rows, width), BF16),
            pltpu.VMEM((4, rows, width), BF16),
            pltpu.VMEM((2, rows // 2, width), BF16),
            pltpu.VMEM((2, rows, width), BF16),
            pltpu.VMEM((3, rows, width), F32),
            pltpu.VMEM((rows, width), F32),
            pltpu.VMEM((16 * KV_ROWS + 512, 128), BF16),
            pltpu.VMEM((16, rows, width), BF16),
            pltpu.VMEM((16, rows, width), BF16),
            pltpu.VMEM((10, 2, rows // 4, width), BF16),
            pltpu.VMEM((10, 2, rows // 2, width), BF16),
            pltpu.VMEM((32, 128), F32),
            pltpu.VMEM((32, 128), F32),
            pltpu.VMEM((2, most, width), BF16),
            pltpu.VMEM((most, w_down.shape[1]), BF16),
            pltpu.VMEM((2, most, width), BF16),
            pltpu.VMEM((18, 512, 128), BF16),
            pltpu.SemaphoreType.DMA((3,)),
            pltpu.SemaphoreType.DMA((1,)),
            pltpu.SemaphoreType.DMA((16,)),
            pltpu.SemaphoreType.DMA((16,)),
            pltpu.SemaphoreType.DMA((40,)),
            pltpu.SemaphoreType.DMA((40,)),
            pltpu.SemaphoreType.DMA((40,)),
            pltpu.SemaphoreType.DMA((40,)),
            pltpu.SemaphoreType.DMA((40,)),
            pltpu.SemaphoreType.DMA((40,)),
        ],
        compiler_params=pltpu.CompilerParams(
            collective_id=1, has_side_effects=True, vmem_limit_bytes=VMEM_BYTES
        ),
    )(attn, w_out, hidden, gain, kvx, place_rows, w_gate_up, w_down)


def body(
    hidden_in, attn_gain, w_query, keyvalue_weight, w_out, cache_kv, ctx_len, span_len,
    ffn_gain, routes, gate_weights, w_gate_up, w_down, req_prompt, cache_slot,
):
    width = hidden_in.shape[1]
    prompts_dev = cache_kv.shape[0]
    span_t = span_len.T
    freq = (ROPE_BASE ** (-2.0 * (np.arange(128) % 32) / 64.0)).astype(np.float32)[None, :]
    q, kv = project_tokens(
        hidden_in, attn_gain, w_query.T, keyvalue_weight.reshape(width, 128), freq, span_t, ctx_len
    )
    attn, kvx, place_rows = attend(
        q, kv, cache_kv.reshape(prompts_dev, -1, 128), routes.T, gate_weights.T, span_t, ctx_len,
        req_prompt, cache_slot,
    )
    layer_out, cache = finish(
        attn, w_out, hidden_in, ffn_gain, kvx, place_rows, w_gate_up, w_down
    )
    return (layer_out, cache.reshape(18, 512, 1, 128))


def solution(mesh):
    placed = (
        P(("req", "head"), None),
        P(),
        P(None, "head"),
        P(None, "head", None),
        P("head", None),
        P("req", None, "head", None),
        P(),
        P(),
        P(),
        P(("req", "head"), None),
        P(("req", "head"), None),
        P("req", None, None),
        P("req", None, None),
        P("req"),
        P("req"),
    )
    return jax.shard_map(
        body,
        mesh=mesh,
        in_specs=placed,
        out_specs=(P(("req", "head"), None), P("req", None, "head", None)),
        check_vma=False,
    )
```

```python
import functools

import jax
import jax.numpy as jnp
import numpy as np
from jax import lax
from jax.experimental import pallas as pl
from jax.experimental.pallas import tpu as pltpu
from jax.sharding import PartitionSpec as P

CAP = 48
EPSILON = 1e-05
ROPE_BASE = 10000.0
LOG2E = 1.4426950408889634
MESH = pl.DeviceIdType.MESH
F32 = jnp.float32
BF16 = jnp.bfloat16
VMEM_BYTES = 60 * 1024 * 1024
KV_ROWS = 1152
GATE_ROW = 1088


def vmem():
    return pl.BlockSpec(memory_space=pltpu.VMEM)


def smem():
    return pl.BlockSpec(memory_space=pltpu.SMEM)


def anyspace():
    return pl.BlockSpec(memory_space=pl.ANY)


def rms(values, gain):
    mean_sq = jnp.mean(values * values, axis=-1, keepdims=True)
    return values * lax.rsqrt(mean_sq + EPSILON) * gain


def head_neighbours():
    hd = lax.axis_index("head")
    y, c = hd // 2, hd % 2
    partner = y * 2 + (1 - c)
    up = ((y + 1) % 4) * 2 + c
    down = ((y + 3) % 4) * 2 + c
    return y, c, partner, up, down


def greet(neighbours):
    barrier = pltpu.get_barrier_semaphore()
    for axis, where in neighbours:
        pl.semaphore_signal(barrier, inc=1, device_id={axis: where}, device_id_type=MESH)
    return lambda: pl.semaphore_wait(barrier, len(neighbours))


def project_kernel(
    hidden_ref, gain_ref, wq_ref, wkv_ref, freq_ref, span_ref, ctx_ref,
    q_ref, kv_ref,
    tok, wq_wide, cos_tab, sin_tab, ssem, rsem,
):
    rows = hidden_ref.shape[0]
    half = rows // 2
    group = lax.axis_index("req")
    y, c, partner, up, down = head_neighbours()
    wait_all = greet([("head", partner), ("head", up), ("head", down)])
    tok[0] = rms(hidden_ref[...].astype(F32), gain_ref[...].reshape(1, -1)).astype(BF16)
    wait_all()

    def copy(i, src, dst, to):
        return pltpu.make_async_remote_copy(
            src_ref=src, dst_ref=dst, send_sem=ssem.at[i], recv_sem=rsem.at[i],
            device_id={"head": to}, device_id_type=MESH,
        )

    low, high = pl.ds(0, half), pl.ds(half, half)
    copies = [
        copy(0, tok.at[0, low], tok.at[6, low], up),
        copy(1, tok.at[0, high], tok.at[2, high], down),
        copy(2, tok.at[0], tok.at[1], partner),
        copy(3, tok.at[6, low], tok.at[4, low], up),
        copy(4, tok.at[6], tok.at[7], partner),
        copy(5, tok.at[2, high], tok.at[4, high], down),
        copy(6, tok.at[2], tok.at[3], partner),
        copy(7, tok.at[4, low], tok.at[5, low], partner),
        copy(8, tok.at[0, high], tok.at[6, high], up),
        copy(9, tok.at[0, low], tok.at[2, low], down),
        copy(10, tok.at[4, high], tok.at[5, high], partner),
    ]
    for i in (0, 1, 8, 9, 2):
        copies[i].start()

    wq_wide[...] = jnp.zeros_like(wq_wide)
    for h in range(3):
        wq_wide[pl.ds(h * 128, 64), :] = wq_ref[pl.ds(h * 64, 64), :]

    lane = lax.broadcasted_iota(jnp.int32, (rows, 128), 1)

    @pl.loop(0, 8)
    def _(block):
        within = lax.broadcasted_iota(jnp.int32, (rows, 128), 0) + block * rows
        position = jnp.zeros((rows, 128), jnp.int32)
        begin = 0
        for j in range(4):
            shift = ctx_ref[group * 4 + j] - begin
            position = jnp.where(within >= begin, within + shift, position)
            begin = begin + span_ref[j, group]
        angles = position.astype(F32) * freq_ref[...]
        where_rows = pl.ds(pl.multiple_of(block * rows, rows), rows)
        cos_tab[where_rows, :] = jnp.where(lane < 64, jnp.cos(angles), 1.0)
        sine = jnp.sin(angles)
        sin_tab[where_rows, :] = jnp.where(lane < 32, -sine, jnp.where(lane < 64, sine, 0.0))

    def project(slot):
        block = ((y + slot // 2) % 4) * 2 + (c + slot % 2) % 2
        at = pl.ds(pl.multiple_of(block * rows, rows), rows)
        cosine, sine = cos_tab[at, :], sin_tab[at, :]

        def turn(values):
            other = jnp.where(lane < 32, pltpu.roll(values, 96, 1), pltpu.roll(values, 32, 1))
            return (values * cosine + other * sine).astype(BF16)

        own = tok[slot]
        wide = lax.dot_general(own, wq_wide[...], (((1,), (1,)), ((), ())), preferred_element_type=F32)
        for h in range(3):
            q_ref[at, h * 128 : (h + 1) * 128] = turn(wide[:, h * 128 : (h + 1) * 128])
        kv_ref[at, :] = turn(jnp.dot(own, wkv_ref[...], preferred_element_type=F32))

    copies[0].wait_recv()
    copies[3].start()
    copies[1].wait_recv()
    copies[5].start()
    project(0)
    copies[2].wait_recv()
    project(1)
    copies[8].wait_recv()
    copies[4].start()
    copies[9].wait_recv()
    copies[6].start()
    project(6)
    project(2)
    copies[3].wait_recv()
    copies[7].start()
    copies[5].wait_recv()
    copies[10].start()
    copies[4].wait_recv()
    project(7)
    copies[6].wait_recv()
    project(3)
    project(4)
    copies[7].wait_recv()
    copies[10].wait_recv()
    project(5)
    for one in copies:
        one.wait_send()


def project_tokens(hidden, gain, wq_t, wkv, freq, span_t, ctx):
    rows, width = hidden.shape
    tokens = rows * 8
    return pl.pallas_call(
        project_kernel,
        name="project_tokens",
        out_shape=(
            jax.ShapeDtypeStruct((tokens, 384), BF16),
            jax.ShapeDtypeStruct((tokens, 128), BF16),
        ),
        in_specs=[vmem()] * 5 + [smem()] * 2,
        out_specs=(vmem(), vmem()),
        scratch_shapes=[
            pltpu.VMEM((8, rows, width), BF16),
            pltpu.VMEM((384, width), BF16),
            pltpu.VMEM((tokens, 128), F32),
            pltpu.VMEM((tokens, 128), F32),
            pltpu.SemaphoreType.DMA((11,)),
            pltpu.SemaphoreType.DMA((11,)),
        ],
        compiler_params=pltpu.CompilerParams(
            collective_id=0, has_side_effects=True, vmem_limit_bytes=VMEM_BYTES
        ),
    )(hidden, gain, wq_t, wkv, freq, span_t, ctx)


KEYS = 256
LONG = 4
TILE = 128


def attend_kernel(
    q_ref, kv_ref, cache_ref, routes_ref, gates_ref, span_ref, ctx_ref, prompt_ref, place_ref,
    attn_ref, kvx_ref, place_rows_ref,
    kv_wide, old_turned, new_turned, attn_turned, near, top, total, mixed,
):
    group = lax.axis_index("req")
    tokens = q_ref.shape[0]
    kv_wide[pl.ds(0, tokens), :] = kv_ref[...].astype(F32)
    scale = LOG2E / 8.0

    def score(queries, keys):
        return lax.dot_general(keys, queries, (((1,), (1,)), ((), ())), preferred_element_type=F32)

    def mix(scores, values):
        probs = jnp.exp2(scores * scale - top[...])
        total[...] += jnp.sum(probs.reshape(-1, 8, probs.shape[1]), axis=0)
        mixed[...] += jnp.dot(values, probs.astype(BF16), preferred_element_type=F32)

    def new_rows(i):
        return kv_ref[pl.ds(pl.multiple_of(i * KEYS, KEYS), KEYS), :]

    @pl.loop(0, tokens // KEYS)
    def _(i):
        new_turned[i] = new_rows(i).T[64:, :]

    def prompt(j, carry):
        begin, packed = carry
        length = span_ref[j, group]
        end = begin + length
        ctx = ctx_ref[group * 4 + j]
        long = ctx // (LONG * KEYS)
        whole = ctx // KEYS
        new_first = begin // KEYS
        most_chunks = cache_ref.shape[1] // KEYS

        def old_rows(i, count):
            return cache_ref[j, pl.ds(pl.multiple_of(i * KEYS, KEYS), count * KEYS), :]

        @pl.loop(0, (ctx + KEYS - 1) // KEYS)
        def _(i):
            old_turned[i] = old_rows(i, 1).T[64:, :]

        def tile(t, _):
            first = pl.multiple_of(t * TILE, TILE)
            at = pl.ds(first, TILE)
            queries = jnp.concatenate([q_ref[at, h * 128 : (h + 1) * 128] for h in range(3)], axis=0)
            total[...] = jnp.zeros_like(total)
            mixed[...] = jnp.zeros_like(mixed)
            lane_row = lax.broadcasted_iota(jnp.int32, (1, 3 * TILE), 1) % TILE + first
            own_lane = (lane_row >= begin) & (lane_row < end)
            new_last = (first + TILE - 1) // KEYS

            def new_scores(i):
                scores = score(queries, new_rows(i))
                key = lax.broadcasted_iota(jnp.int32, (KEYS, TILE), 0) + i * KEYS
                row = lax.broadcasted_iota(jnp.int32, (KEYS, TILE), 1) + first
                bias = jnp.where((key >= begin) & (key <= row), 0.0, -1e30)
                return scores + jnp.concatenate([bias] * 3, axis=1)

            def last_old():
                scores = score(queries, old_rows(jnp.minimum(whole, most_chunks - 1), 1))
                key = lax.broadcasted_iota(jnp.int32, scores.shape, 0)
                return jnp.where(key < ctx - whole * KEYS, scores, -1e30)

            near[...] = new_scores(new_last)
            top[...] = jnp.where(own_lane, jnp.max(near[...], axis=0, keepdims=True) * scale, 1e30)
            mix(near[...], new_turned[new_last])

            @pl.loop(new_first, new_last)
            def _(i):
                mix(new_scores(i), new_turned[i])

            @pl.loop(0, long)
            def _(i):
                values = jnp.concatenate([old_turned[i * LONG + k] for k in range(LONG)], axis=1)
                mix(score(queries, old_rows(i * LONG, LONG)), values)

            @pl.loop(long * LONG, whole)
            def _(i):
                mix(score(queries, old_rows(i, 1)), old_turned[i])

            @pl.when(ctx > whole * KEYS)
            def _():
                mix(last_old(), old_turned[whole])

            @pl.when(jnp.max(jnp.where(own_lane, jnp.max(total[...], axis=0, keepdims=True), 0.0)) > 2.0**64)
            def _():
                def higher(scores):
                    return jnp.max(scores, axis=0, keepdims=True)

                most = higher(near[...])
                most = lax.fori_loop(new_first, new_last, lambda i, m: jnp.maximum(m, higher(new_scores(i))), most)
                most = lax.fori_loop(
                    0, whole, lambda i, m: jnp.maximum(m, higher(score(queries, old_rows(i, 1)))), most
                )
                last = jnp.where(ctx > whole * KEYS, 0.0, -1e30)
                most = jnp.maximum(most, higher(last_old()) + last)
                top[...] = jnp.where(own_lane, most * scale, 1e30)
                total[...] = jnp.zeros_like(total)
                mixed[...] = jnp.zeros_like(mixed)

                @pl.loop(new_first, new_last + 1)
                def _(i):
                    mix(new_scores(i), new_turned[i])

                @pl.loop(0, whole)
                def _(i):
                    mix(score(queries, old_rows(i, 1)), old_turned[i])

                @pl.when(ctx > whole * KEYS)
                def _():
                    mix(last_old(), old_turned[whole])

            out = mixed[...] / jnp.sum(total[...], axis=0, keepdims=True)
            side = jnp.concatenate([out[:, h * TILE : (h + 1) * TILE] for h in range(3)], axis=0)
            row = lax.broadcasted_iota(jnp.int32, side.shape, 1) + first
            mine = (row >= begin) & (row < end)
            attn_turned[t] = jnp.where(mine, side, attn_turned[t])
            return 0

        lax.fori_loop(begin // TILE, (end + TILE - 1) // TILE, tile, 0)

        def pack(i, _):
            dst = pl.ds(pl.multiple_of(packed + i * 16, 16), 16)
            kvx_ref[dst, :] = kv_wide[pl.ds(begin + i * 16, 16), :].astype(BF16)
            return 0

        chunks = (length + 15) // 16
        lax.fori_loop(0, chunks, pack, 0)
        return end, packed + chunks * 16

    kv_wide[pl.ds(tokens, 16), :] = jnp.zeros((16, 128), F32)
    kvx_ref[...] = jnp.zeros_like(kvx_ref)
    attn_turned[...] = jnp.zeros_like(attn_turned)
    lax.fori_loop(0, 4, prompt, (0, 0))

    @pl.loop(0, tokens // TILE)
    def _(t):
        attn_ref[pl.ds(pl.multiple_of(t * TILE, TILE), TILE), :] = attn_turned[t].T.astype(BF16)

    expert = lax.broadcasted_iota(jnp.int32, (32, 128), 0)
    gates = jnp.zeros((32, 128), F32)
    for k in range(8):
        hit = routes_ref[k : k + 1, :] == expert
        gates = gates + jnp.where(hit, gates_ref[k : k + 1, :].astype(F32), 0.0)
    kvx_ref[pl.ds(GATE_ROW, 32), :] = gates.astype(BF16)

    x, z = group // 4, group % 4

    for i in range(18):
        asked, member = prompt_ref[i] // 4, prompt_ref[i] % 4
        first = ((asked // 4 - x + 4) % 4 * 4 + (asked % 4 - z + 4) % 4) * KV_ROWS
        for j in range(3):
            first = first + jnp.where(j < member, (span_ref[j, asked] + 15) // 16 * 16, 0)
        place_rows_ref[0, place_ref[i]] = first // 16
        place_rows_ref[1, place_ref[i]] = span_ref[member, asked]


def attend(q, kv, cache, routes_t, gates_t, span_t, ctx, req_prompt, cache_slot):
    tokens = q.shape[0]
    return pl.pallas_call(
        attend_kernel,
        name="attend",
        out_shape=(
            jax.ShapeDtypeStruct((tokens, 192), BF16),
            jax.ShapeDtypeStruct((KV_ROWS, 128), BF16),
            jax.ShapeDtypeStruct((2, 18), jnp.int32),
        ),
        in_specs=[vmem()] * 5 + [smem()] * 4,
        out_specs=(vmem(), vmem(), smem()),
        scratch_shapes=[
            pltpu.VMEM((tokens + 16, 128), F32),
            pltpu.VMEM((cache.shape[1] // KEYS + 1, 64, KEYS), BF16),
            pltpu.VMEM((tokens // KEYS, 64, KEYS), BF16),
            pltpu.VMEM((tokens // TILE, 192, TILE), F32),
            pltpu.VMEM((KEYS, 3 * TILE), F32),
            pltpu.VMEM((1, 3 * TILE), F32),
            pltpu.VMEM((8, 3 * TILE), F32),
            pltpu.VMEM((64, 3 * TILE), F32),
        ],
        compiler_params=pltpu.CompilerParams(vmem_limit_bytes=VMEM_BYTES),
    )(q, kv, cache, routes_t, gates_t, span_t, ctx, req_prompt, cache_slot)


GROUPS = (
    ((0, 0), (0, 1), (0, 3), (1, 0), (3, 0)),
    ((1, 1), (1, 3), (3, 1), (3, 3)),
    ((0, 2), (2, 0)),
    ((2, 2), (2, 1), (2, 3), (1, 2), (3, 2)),
)


def slot_of(which, first, second):
    return first * 4 + second if which == 0 else second * 4 + first


class Line:
    def __init__(self, make, ssem, rsem, base, outs, passes):
        self.copies = [
            make(src, dst, ssem.at[base + i], rsem.at[base + i], to)
            for i, (src, dst, to) in enumerate(outs + passes)
        ]

    def out(self):
        self.copies[0].start()
        self.copies[1].start()

    def forward(self):
        self.copies[0].wait_recv()
        self.copies[2].start()
        self.copies[1].wait_recv()
        self.copies[3].start()

    def finish(self):
        self.copies[2].wait_recv()
        self.copies[3].wait_recv()

    def drain(self):
        for one in self.copies:
            one.wait_send()


def remote(axis):
    def make(src, dst, send, recv, to):
        return pltpu.make_async_remote_copy(
            src_ref=src, dst_ref=dst, send_sem=send, recv_sem=recv, device_id={axis: to}, device_id_type=MESH
        )

    return make


def gather_lines(buf, rows, ssem, rsem, ring):
    half, quarter = rows // 2, rows // 4
    lines = []
    for which in (0, 1):
        plus, minus = ring[which]
        plus2, minus2 = ring[1 - which]
        low = which * half

        def part(first, second, piece, which=which, low=low):
            row, count = {"all": (low, half), "a": (low, quarter), "b": (low + quarter, quarter)}[piece]
            return buf(slot_of(which, first, second), row, count)

        def along(base, at, p, m, part=part):
            return Line(
                remote("req"), ssem, rsem, base,
                [(part(*at(0), "all"), part(*at(3), "all"), p), (part(*at(0), "all"), part(*at(1), "all"), m)],
                [(part(*at(3), "a"), part(*at(2), "a"), p), (part(*at(1), "b"), part(*at(2), "b"), m)],
            )

        these = [along(which * 20, lambda k: (k, 0), plus, minus)]
        for i in range(4):
            these.append(along(which * 20 + 4 + 4 * i, lambda k, i=i: (i, k), plus2, minus2))
        lines.append(these)
    return lines


def gather_steps(lines):
    def both(*steps):
        for one in lines:
            for index, name in steps:
                getattr(one[index], name)()

    return [
        lambda: both((0, "out"), (1, "out")),
        lambda: both((0, "forward"), (4, "out"), (2, "out")),
        lambda: both((1, "forward")),
        lambda: both((0, "finish"), (3, "out")),
        lambda: both((4, "forward"), (2, "forward")),
        lambda: both((1, "finish")),
        lambda: both((3, "forward")),
        lambda: both((4, "finish"), (2, "finish")),
        lambda: both((3, "finish")),
        lambda: [line.drain() for one in lines for line in one],
    ]


def finish_kernel(
    attn_ref, wout_ref, hidden_ref, gain_ref, kvx_ref, place_ref, wgu_hbm, wd_hbm,
    out_ref, cache_hbm,
    wgu, wd, part, pin, head_half, head_full, kept, resid, kvall, rows_in, sums, red_half, red_full,
    gates, ranks, picked, acts, outs, staged,
    wsem, csem, hssem, hrsem, kssem, krsem, assem, arsem, rssem, rrsem,
):
    width = hidden_ref.shape[1]
    r = lax.axis_index("req")
    x, z = r // 4, r % 4
    xp, xm = ((x + 1) % 4) * 4 + z, ((x + 3) % 4) * 4 + z
    zp, zm = x * 4 + (z + 1) % 4, x * 4 + (z + 3) % 4
    ring = ((xp, xm), (zp, zm))
    y, c, partner, up, down = head_neighbours()
    wait_all = greet(
        [("head", partner), ("head", up), ("head", down), ("req", xp), ("req", xm), ("req", zp), ("req", zm)]
    )
    loads = [
        pltpu.make_async_copy(wgu_hbm, wgu, wsem.at[0]),
        pltpu.make_async_copy(wd_hbm, wd, wsem.at[1]),
        pltpu.make_async_copy(kvx_ref, kvall.at[pl.ds(0, KV_ROWS), :], wsem.at[2]),
    ]
    loads[2].start()
    for one in loads[:2]:
        one.start()
    kvall[pl.ds(16 * KV_ROWS, 512), :] = jnp.zeros((512, 128), BF16)
    loads[2].wait()
    wait_all()

    kv_lines = gather_lines(
        lambda slot, row, count: kvall.at[pl.ds(slot * KV_ROWS + row, count), :], KV_ROWS, kssem, krsem, ring
    )
    kv_steps = gather_steps(kv_lines)
    row_lines = gather_lines(
        lambda slot, row, count: rows_in.at[slot, pl.ds(row, count), :], 128, assem, arsem, ring
    )
    row_steps = gather_steps(row_lines)
    kv_steps[0]()

    def project(dy, dc, store):
        target = ((y + dy) % 4) * 2 + (c + dc) % 2
        own = attn_ref[pl.ds(pl.multiple_of(target * 128, 128), 128), :]

        @pl.loop(0, width // 256)
        def _(n):
            cols = pl.ds(pl.multiple_of(n * 256, 256), 256)
            store(cols, jnp.dot(own, wout_ref[:, cols], preferred_element_type=F32))

    make = remote("head")
    low, high = pl.ds(0, 64), pl.ds(64, 64)
    to_partner = [
        make(part.at[2 * dy + 1], pin.at[dy], hssem.at[dy], hrsem.at[dy], partner) for dy in range(4)
    ]

    def ring_copy(i, src, dst, to):
        return make(src, dst, hssem.at[4 + i], hrsem.at[4 + i], to)

    far = (
        ring_copy(0, part.at[4, low], head_half.at[0], up),
        ring_copy(1, part.at[4, high], head_half.at[1], down),
    )
    free = (
        ring_copy(2, part.at[2, high], head_full.at[0, high], up),
        ring_copy(3, part.at[6, low], head_full.at[1, low], down),
    )
    bound = (
        ring_copy(4, part.at[2, low], head_full.at[0, low], up),
        ring_copy(5, part.at[6, high], head_full.at[1, high], down),
    )

    def give(dy):
        def store(cols, total):
            part[2 * dy + 1, :, cols] = total.astype(BF16)

        project(dy, 1, store)
        to_partner[dy].start()

    def keep(k, dy):
        def store(cols, total):
            kept[k, :, cols] = total + hidden_ref[:, cols].astype(F32) if dy == 0 else total

        project(dy, 0, store)

    def sum_rows(k, dy, index, first, half=None):
        @pl.loop(0, 4)
        def _(n):
            at = pl.ds(pl.multiple_of(first + n * 16, 16), 16)
            total = kept[k, at, :] + pin[dy, at, :].astype(F32)
            if half is not None:
                total = total + head_half[half, pl.ds(pl.multiple_of(n * 16, 16), 16), :].astype(F32)
            part[index, at, :] = total.astype(BF16)

    give(2)
    give(1)
    give(3)
    to_partner[2].wait_recv()

    def store_far(cols, total):
        part[4, :, cols] = (total + pin[2, :, cols].astype(F32)).astype(BF16)

    project(2, 0, store_far)
    far[0].start()
    far[1].start()
    keep(0, 1)
    to_partner[1].wait_recv()
    sum_rows(0, 1, 2, 64)
    free[0].start()
    keep(1, 3)
    to_partner[3].wait_recv()
    sum_rows(1, 3, 6, 0)
    free[1].start()
    give(0)
    keep(2, 0)
    kv_steps[1]()
    far[0].wait_recv()
    sum_rows(0, 1, 2, 0, 0)
    bound[0].start()
    far[1].wait_recv()
    sum_rows(1, 3, 6, 64, 1)
    bound[1].start()
    kv_steps[2]()
    kv_steps[3]()
    kv_steps[4]()
    to_partner[0].wait_recv()
    for one in free + bound:
        one.wait_recv()

    @pl.loop(0, 8, unroll=2)
    def _(n):
        at = pl.ds(pl.multiple_of(n * 16, 16), 16)
        total = kept[2, at, :] + pin[0, at, :].astype(F32)
        total = total + head_full[0, at, :].astype(F32) + head_full[1, at, :].astype(F32)
        resid[at, :] = total
        rows_in[0, at, :] = rms(total, gain_ref[...].reshape(1, -1)).astype(BF16)

    row_steps[0]()
    kv_steps[5]()
    kv_steps[6]()
    expert = lax.broadcasted_iota(jnp.int32, (32, 128), 0)
    before = lax.broadcasted_iota(jnp.int32, (128, 128), 0) < lax.broadcasted_iota(jnp.int32, (128, 128), 1)
    order = jnp.where(before, 1.0, 0.0).astype(BF16)

    def read_gates(slots):
        for slot in slots:
            table = kvall[slot * KV_ROWS + GATE_ROW : slot * KV_ROWS + GATE_ROW + 32, :].astype(F32)
            for j in range(2):
                mine = jnp.sum(jnp.where(expert == r * 2 + j, table, 0.0), axis=0, keepdims=True)
                gates[slot * 2 + j : slot * 2 + j + 1, :] = mine
        hits = jnp.where(gates[...] > 0.0, 1.0, 0.0).astype(BF16)
        ranks[...] = jnp.dot(hits, order, preferred_element_type=F32)

    def chosen(slot, weighted):
        place = lax.broadcasted_iota(jnp.int32, (CAP, 128), 0).astype(F32)
        maps = []
        for j in range(2):
            gate = gates[slot * 2 + j : slot * 2 + j + 1, :]
            value = gate if weighted else 1.0
            hit = (ranks[slot * 2 + j : slot * 2 + j + 1, :] == place) & (gate > 0.0)
            maps.append(jnp.where(hit, value, 0.0))
        return jnp.concatenate(maps, axis=0).astype(BF16)

    def experts(group):
        count = len(group) * CAP
        for k, (a, b) in enumerate(group):
            slot = a * 4 + b
            select = chosen(slot, False)

            @pl.loop(0, width // 512, unroll=width // 512)
            def _(n, k=k, slot=slot, select=select):
                cols = pl.ds(pl.multiple_of(n * 512, 512), 512)
                got = jnp.dot(select, rows_in[slot, :, cols], preferred_element_type=F32).astype(BF16)
                picked[0, pl.ds(k * CAP, CAP), cols] = got[:CAP]
                picked[1, pl.ds(k * CAP, CAP), cols] = got[CAP:]

        @pl.loop(0, 2)
        def _(e):
            @pl.loop(0, 2)
            def _(n):
                cols = pl.ds(pl.multiple_of(n * 256, 256), 256)
                later = pl.ds(pl.multiple_of(n * 256 + 512, 256), 256)
                own = picked[e, pl.ds(0, count), :]
                gate = jnp.dot(own, wgu[e, :, cols], preferred_element_type=F32)
                lift = jnp.dot(own, wgu[e, :, later], preferred_element_type=F32)
                acts[pl.ds(0, count), cols] = (gate / (1.0 + jnp.exp(-gate)) * lift).astype(BF16)

            @pl.loop(0, width // 256, unroll=2)
            def _(n):
                cols = pl.ds(pl.multiple_of(n * 256, 256), 256)
                outs[e, pl.ds(0, count), cols] = jnp.dot(
                    acts[pl.ds(0, count), :], wd[e, :, cols], preferred_element_type=F32
                ).astype(BF16)

        for k, (a, b) in enumerate(group):
            slot = a * 4 + b
            spread = chosen(slot, True)

            @pl.loop(0, width // 512, unroll=width // 512)
            def _(n, k=k, slot=slot, spread=spread):
                cols = pl.ds(pl.multiple_of(n * 512, 512), 512)
                given = jnp.concatenate(
                    [outs[0, pl.ds(k * CAP, CAP), cols], outs[1, pl.ds(k * CAP, CAP), cols]], axis=0
                )
                sums[slot, :, cols] = lax.dot_general(
                    spread, given, (((0,), (0,)), ((), ())), preferred_element_type=F32
                ).astype(BF16)

    store = pltpu.make_async_copy(staged, cache_hbm, csem.at[0])

    def fill_cache():
        @pl.loop(0, 18)
        def _(s):
            start, length = place_ref[0, s], place_ref[1, s]
            for i in range(4):
                rows = kvall[pl.ds(start * 16 + i * 128, 128), :].astype(F32)
                at = lax.broadcasted_iota(jnp.int32, (128, 128), 0) + i * 128
                staged[s, pl.ds(i * 128, 128), :] = jnp.where(at < length, rows, 0.0).astype(BF16)

        store.start()

    def add(dst, row, src, count):
        @pl.loop(0, count // 16)
        def _(i):
            to = pl.ds(pl.multiple_of(row + i * 16, 16), 16)
            at = pl.ds(pl.multiple_of(i * 16, 16), 16)
            total = sums[dst, to, :].astype(F32)
            for one in src:
                total = total + one[at, :].astype(F32)
            sums[dst, to, :] = total.astype(BF16)

    def reduce_line(n, which, at, plus, minus):
        base = which * 64
        send = remote("req")

        def piece(k, row, count):
            return sums.at[at(k), pl.ds(base + row, count), :]

        def copy(i, src, dst, to):
            return send(src, dst, rssem.at[6 * n + i], rrsem.at[6 * n + i], to)

        first, second = pl.ds(0, 32), pl.ds(32, 32)
        copies = [
            copy(0, piece(2, 0, 32), red_half.at[n, 0], plus),
            copy(1, piece(2, 32, 32), red_half.at[n, 1], minus),
            copy(2, piece(1, 32, 32), red_full.at[n, 0, second], plus),
            copy(3, piece(3, 0, 32), red_full.at[n, 1, first], minus),
            copy(4, piece(1, 0, 32), red_full.at[n, 0, first], plus),
            copy(5, piece(3, 32, 32), red_full.at[n, 1, second], minus),
        ]

        def far():
            copies[0].start()
            copies[1].start()

        def near():
            copies[2].start()
            copies[3].start()

        def middle():
            copies[0].wait_recv()
            add(at(1), base, [red_half.at[n, 0]], 32)
            copies[4].start()
            copies[1].wait_recv()
            add(at(3), base + 32, [red_half.at[n, 1]], 32)
            copies[5].start()

        def last():
            for one in copies[2:]:
                one.wait_recv()

        def fold():
            last()
            add(at(0), base, [red_full.at[n, 0], red_full.at[n, 1]], 64)

        def drain():
            for one in copies:
                one.wait_send()

        return {"far": far, "near": near, "middle": middle, "fold": fold, "last": last, "drain": drain}

    back = []
    for which in (0, 1):
        plus, minus = ring[which]
        plus2, minus2 = ring[1 - which]
        these = [
            reduce_line(which * 5 + i, which, lambda k, i=i, w=which: slot_of(w, i, k), plus2, minus2)
            for i in range(4)
        ]
        these.append(reduce_line(which * 5 + 4, which, lambda k, w=which: slot_of(w, k, 0), plus, minus))
        back.append(these)

    def go(line, step):
        for these in back:
            these[line][step]()

    near = [a * 4 + b for a, b in GROUPS[0]]
    gates[...] = jnp.zeros_like(gates)
    read_gates(near)
    for one in loads[:2]:
        one.wait()
    row_steps[1]()
    row_steps[2]()
    experts(GROUPS[0])
    kv_steps[7]()
    kv_steps[8]()
    row_steps[3]()
    row_steps[4]()
    read_gates([slot for slot in range(16) if slot not in near])

    experts(GROUPS[1])
    row_steps[5]()
    row_steps[6]()
    experts(GROUPS[2])
    row_steps[7]()
    go(0, "far")
    go(0, "near")
    row_steps[8]()
    experts(GROUPS[3])
    go(0, "middle")
    for line, step in (
        (2, "far"), (2, "near"), (1, "far"), (1, "near"), (3, "far"), (3, "near"), (0, "fold"), (2, "middle"),
        (1, "middle"), (3, "middle"),
    ):
        go(line, step)
    fill_cache()
    for line, step in (
        (2, "fold"), (4, "far"), (1, "fold"), (3, "fold"), (4, "near"), (4, "middle"), (4, "last"),
    ):
        go(line, step)
    for which, n in ((0, 4), (1, 9)):
        @pl.loop(0, 4)
        def _(i, which=which, n=n):
            to = pl.ds(pl.multiple_of(which * 64 + i * 16, 16), 16)
            at = pl.ds(pl.multiple_of(i * 16, 16), 16)
            total = resid[to, :] + sums[0, to, :].astype(F32)
            total = total + red_full[n, 0, at, :].astype(F32) + red_full[n, 1, at, :].astype(F32)
            out_ref[to, :] = total.astype(BF16)

    for one in (*to_partner, *far, *free, *bound):
        one.wait_send()
    kv_steps[9]()
    row_steps[9]()
    for line in range(5):
        go(line, "drain")
    store.wait()


def finish(attn, w_out, hidden, gain, kvx, place_rows, w_gate_up, w_down):
    rows, width = hidden.shape
    most = max(len(group) for group in GROUPS) * CAP
    return pl.pallas_call(
        finish_kernel,
        name="finish",
        out_shape=(
            jax.ShapeDtypeStruct((rows, width), BF16),
            jax.ShapeDtypeStruct((18, 512, 128), BF16),
        ),
        in_specs=[vmem()] * 5 + [smem()] + [anyspace()] * 2,
        out_specs=(vmem(), anyspace()),
        scratch_shapes=[
            pltpu.VMEM(w_gate_up.shape, BF16),
            pltpu.VMEM(w_down.shape, BF16),
            pltpu.VMEM((8, rows, width), BF16),
            pltpu.VMEM((4, rows, width), BF16),
            pltpu.VMEM((2, rows // 2, width), BF16),
            pltpu.VMEM((2, rows, width), BF16),
            pltpu.VMEM((3, rows, width), F32),
            pltpu.VMEM((rows, width), F32),
            pltpu.VMEM((16 * KV_ROWS + 512, 128), BF16),
            pltpu.VMEM((16, rows, width), BF16),
            pltpu.VMEM((16, rows, width), BF16),
            pltpu.VMEM((10, 2, rows // 4, width), BF16),
            pltpu.VMEM((10, 2, rows // 2, width), BF16),
            pltpu.VMEM((32, 128), F32),
            pltpu.VMEM((32, 128), F32),
            pltpu.VMEM((2, most, width), BF16),
            pltpu.VMEM((most, w_down.shape[1]), BF16),
            pltpu.VMEM((2, most, width), BF16),
            pltpu.VMEM((18, 512, 128), BF16),
            pltpu.SemaphoreType.DMA((3,)),
            pltpu.SemaphoreType.DMA((1,)),
            pltpu.SemaphoreType.DMA((10,)),
            pltpu.SemaphoreType.DMA((10,)),
            pltpu.SemaphoreType.DMA((40,)),
            pltpu.SemaphoreType.DMA((40,)),
            pltpu.SemaphoreType.DMA((40,)),
            pltpu.SemaphoreType.DMA((40,)),
            pltpu.SemaphoreType.DMA((60,)),
            pltpu.SemaphoreType.DMA((60,)),
        ],
        compiler_params=pltpu.CompilerParams(
            collective_id=1, has_side_effects=True, vmem_limit_bytes=VMEM_BYTES
        ),
    )(attn, w_out, hidden, gain, kvx, place_rows, w_gate_up, w_down)


def body(
    hidden_in, attn_gain, w_query, keyvalue_weight, w_out, cache_kv, ctx_len, span_len,
    ffn_gain, routes, gate_weights, w_gate_up, w_down, req_prompt, cache_slot,
):
    width = hidden_in.shape[1]
    prompts_dev = cache_kv.shape[0]
    span_t = span_len.T
    freq = (ROPE_BASE ** (-2.0 * (np.arange(128) % 32) / 64.0)).astype(np.float32)[None, :]
    q, kv = project_tokens(
        hidden_in, attn_gain, w_query.T, keyvalue_weight.reshape(width, 128), freq, span_t, ctx_len
    )
    attn, kvx, place_rows = attend(
        q, kv, cache_kv.reshape(prompts_dev, -1, 128), routes.T, gate_weights.T, span_t, ctx_len,
        req_prompt, cache_slot,
    )
    layer_out, cache = finish(
        attn, w_out, hidden_in, ffn_gain, kvx, place_rows, w_gate_up, w_down
    )
    return (layer_out, cache.reshape(18, 512, 1, 128))


def solution(mesh):
    placed = (
        P(("req", "head"), None),
        P(),
        P(None, "head"),
        P(None, "head", None),
        P("head", None),
        P("req", None, "head", None),
        P(),
        P(),
        P(),
        P(("req", "head"), None),
        P(("req", "head"), None),
        P("req", None, None),
        P("req", None, None),
        P("req"),
        P("req"),
    )
    return jax.shard_map(
        body,
        mesh=mesh,
        in_specs=placed,
        out_specs=(P(("req", "head"), None), P("req", None, "head", None)),
        check_vma=False,
    )
```

```python
import functools

import jax
import jax.numpy as jnp
import numpy as np
from jax import lax
from jax.experimental import pallas as pl
from jax.experimental.pallas import tpu as pltpu
from jax.sharding import PartitionSpec as P

CAP = 48
EPSILON = 1e-05
ROPE_BASE = 10000.0
LOG2E = 1.4426950408889634
MESH = pl.DeviceIdType.MESH
F32 = jnp.float32
BF16 = jnp.bfloat16
VMEM_BYTES = 60 * 1024 * 1024
KV_ROWS = 1152
GATE_ROW = 1088


def vmem():
    return pl.BlockSpec(memory_space=pltpu.VMEM)


def smem():
    return pl.BlockSpec(memory_space=pltpu.SMEM)


def anyspace():
    return pl.BlockSpec(memory_space=pl.ANY)


def rms(values, gain):
    mean_sq = jnp.mean(values * values, axis=-1, keepdims=True)
    return values * lax.rsqrt(mean_sq + EPSILON) * gain


def head_neighbours():
    hd = lax.axis_index("head")
    y, c = hd // 2, hd % 2
    partner = y * 2 + (1 - c)
    up = ((y + 1) % 4) * 2 + c
    down = ((y + 3) % 4) * 2 + c
    return y, c, partner, up, down


def greet(neighbours):
    barrier = pltpu.get_barrier_semaphore()
    for axis, where in neighbours:
        pl.semaphore_signal(barrier, inc=1, device_id={axis: where}, device_id_type=MESH)
    return lambda: pl.semaphore_wait(barrier, len(neighbours))


def project_kernel(
    hidden_ref, gain_ref, wq_ref, wkv_ref, freq_ref, span_ref, ctx_ref,
    q_ref, kv_ref,
    tok, wq_wide, cos_tab, sin_tab, ssem, rsem,
):
    rows = hidden_ref.shape[0]
    half = rows // 2
    group = lax.axis_index("req")
    y, c, partner, up, down = head_neighbours()
    wait_all = greet([("head", partner), ("head", up), ("head", down)])
    tok[0] = rms(hidden_ref[...].astype(F32), gain_ref[...].reshape(1, -1)).astype(BF16)
    wait_all()

    def copy(i, src, dst, to):
        return pltpu.make_async_remote_copy(
            src_ref=src, dst_ref=dst, send_sem=ssem.at[i], recv_sem=rsem.at[i],
            device_id={"head": to}, device_id_type=MESH,
        )

    low, high = pl.ds(0, half), pl.ds(half, half)
    copies = [
        copy(0, tok.at[0, low], tok.at[6, low], up),
        copy(1, tok.at[0, high], tok.at[2, high], down),
        copy(2, tok.at[0], tok.at[1], partner),
        copy(3, tok.at[6, low], tok.at[4, low], up),
        copy(4, tok.at[6], tok.at[7], partner),
        copy(5, tok.at[2, high], tok.at[4, high], down),
        copy(6, tok.at[2], tok.at[3], partner),
        copy(7, tok.at[4, low], tok.at[5, low], partner),
        copy(8, tok.at[0, high], tok.at[6, high], up),
        copy(9, tok.at[0, low], tok.at[2, low], down),
        copy(10, tok.at[4, high], tok.at[5, high], partner),
    ]
    for i in (0, 1, 8, 9, 2):
        copies[i].start()

    wq_wide[...] = jnp.zeros_like(wq_wide)
    for h in range(3):
        wq_wide[pl.ds(h * 128, 64), :] = wq_ref[pl.ds(h * 64, 64), :]

    lane = lax.broadcasted_iota(jnp.int32, (rows, 128), 1)

    @pl.loop(0, 8)
    def _(block):
        within = lax.broadcasted_iota(jnp.int32, (rows, 128), 0) + block * rows
        position = jnp.zeros((rows, 128), jnp.int32)
        begin = 0
        for j in range(4):
            shift = ctx_ref[group * 4 + j] - begin
            position = jnp.where(within >= begin, within + shift, position)
            begin = begin + span_ref[j, group]
        angles = position.astype(F32) * freq_ref[...]
        where_rows = pl.ds(pl.multiple_of(block * rows, rows), rows)
        cos_tab[where_rows, :] = jnp.where(lane < 64, jnp.cos(angles), 1.0)
        sine = jnp.sin(angles)
        sin_tab[where_rows, :] = jnp.where(lane < 32, -sine, jnp.where(lane < 64, sine, 0.0))

    def project(slot):
        block = ((y + slot // 2) % 4) * 2 + (c + slot % 2) % 2
        at = pl.ds(pl.multiple_of(block * rows, rows), rows)
        cosine, sine = cos_tab[at, :], sin_tab[at, :]

        def turn(values):
            other = jnp.where(lane < 32, pltpu.roll(values, 96, 1), pltpu.roll(values, 32, 1))
            return (values * cosine + other * sine).astype(BF16)

        own = tok[slot]
        wide = lax.dot_general(own, wq_wide[...], (((1,), (1,)), ((), ())), preferred_element_type=F32)
        for h in range(3):
            q_ref[at, h * 128 : (h + 1) * 128] = turn(wide[:, h * 128 : (h + 1) * 128])
        kv_ref[at, :] = turn(jnp.dot(own, wkv_ref[...], preferred_element_type=F32))

    copies[0].wait_recv()
    copies[3].start()
    copies[1].wait_recv()
    copies[5].start()
    project(0)
    copies[2].wait_recv()
    project(1)
    copies[8].wait_recv()
    copies[4].start()
    copies[9].wait_recv()
    copies[6].start()
    project(6)
    project(2)
    copies[3].wait_recv()
    copies[7].start()
    copies[5].wait_recv()
    copies[10].start()
    copies[4].wait_recv()
    project(7)
    copies[6].wait_recv()
    project(3)
    project(4)
    copies[7].wait_recv()
    copies[10].wait_recv()
    project(5)
    for one in copies:
        one.wait_send()


def project_tokens(hidden, gain, wq_t, wkv, freq, span_t, ctx):
    rows, width = hidden.shape
    tokens = rows * 8
    return pl.pallas_call(
        project_kernel,
        name="project_tokens",
        out_shape=(
            jax.ShapeDtypeStruct((tokens, 384), BF16),
            jax.ShapeDtypeStruct((tokens, 128), BF16),
        ),
        in_specs=[vmem()] * 5 + [smem()] * 2,
        out_specs=(vmem(), vmem()),
        scratch_shapes=[
            pltpu.VMEM((8, rows, width), BF16),
            pltpu.VMEM((384, width), BF16),
            pltpu.VMEM((tokens, 128), F32),
            pltpu.VMEM((tokens, 128), F32),
            pltpu.SemaphoreType.DMA((11,)),
            pltpu.SemaphoreType.DMA((11,)),
        ],
        compiler_params=pltpu.CompilerParams(
            collective_id=0, has_side_effects=True, vmem_limit_bytes=VMEM_BYTES
        ),
    )(hidden, gain, wq_t, wkv, freq, span_t, ctx)


KEYS = 256
LONG = 4
TILE = 128


def attend_kernel(
    q_ref, kv_ref, cache_ref, routes_ref, gates_ref, span_ref, ctx_ref, prompt_ref, place_ref,
    attn_ref, kvx_ref, place_rows_ref,
    kv_wide, old_turned, new_turned, attn_turned, near, top, total, mixed, largest,
):
    group = lax.axis_index("req")
    tokens = q_ref.shape[0]
    kv_wide[pl.ds(0, tokens), :] = kv_ref[...].astype(F32)
    scale = LOG2E / 8.0

    def score(queries, keys):
        return lax.dot_general(keys, queries, (((1,), (1,)), ((), ())), preferred_element_type=F32)

    def mix(scores, values):
        probs = jnp.exp2(scores * scale - top[...])
        total[...] += jnp.sum(probs.reshape(-1, 8, probs.shape[1]), axis=0)
        mixed[...] += jnp.dot(values, probs.astype(BF16), preferred_element_type=F32)

    def new_rows(i):
        return kv_ref[pl.ds(pl.multiple_of(i * KEYS, KEYS), KEYS), :]

    @pl.loop(0, tokens // KEYS)
    def _(i):
        new_turned[i] = new_rows(i).T[64:, :]

    def prompt(j, carry, exact):
        begin, packed = carry
        length = span_ref[j, group]
        end = begin + length
        ctx = ctx_ref[group * 4 + j]
        last = (ctx - 1) // KEYS
        long = last // LONG
        new_first = begin // KEYS

        def old_rows(i, count):
            return cache_ref[j, pl.ds(pl.multiple_of(i * KEYS, KEYS), count * KEYS), :]

        @pl.loop(0, last + 1)
        def _(i):
            old_turned[i] = old_rows(i, 1).T[64:, :]

        def tile(t, _):
            first = pl.multiple_of(t * TILE, TILE)
            at = pl.ds(first, TILE)
            queries = jnp.concatenate([q_ref[at, h * 128 : (h + 1) * 128] for h in range(3)], axis=0)
            lane_row = lax.broadcasted_iota(jnp.int32, (1, 3 * TILE), 1) % TILE + first
            own_lane = (lane_row >= begin) & (lane_row < end)
            new_last = (first + TILE - 1) // KEYS

            def new_scores(i):
                scores = score(queries, new_rows(i))
                key = lax.broadcasted_iota(jnp.int32, (KEYS, TILE), 0) + i * KEYS
                row = lax.broadcasted_iota(jnp.int32, (KEYS, TILE), 1) + first
                bias = jnp.where((key >= begin) & (key <= row), 0.0, -1e30)
                return scores + jnp.concatenate([bias] * 3, axis=1)

            def higher(scores):
                return jnp.max(scores, axis=0, keepdims=True)

            scores = score(queries, old_rows(last, 1))
            key = lax.broadcasted_iota(jnp.int32, scores.shape, 0)
            near[pl.ds(KEYS, KEYS), :] = jnp.where(key < ctx - last * KEYS, scores, -1e30)
            near[pl.ds(0, KEYS), :] = new_scores(new_last)
            most = higher(near[...])
            if exact:
                most = lax.fori_loop(new_first, new_last, lambda i, m: jnp.maximum(m, higher(new_scores(i))), most)
                most = lax.fori_loop(
                    0, last, lambda i, m: jnp.maximum(m, higher(score(queries, old_rows(i, 1)))), most
                )
            top[...] = jnp.where(own_lane, most * scale, 1e30)
            total[...] = jnp.zeros_like(total)
            mixed[...] = jnp.zeros_like(mixed)
            mix(near[...], jnp.concatenate([new_turned[new_last], old_turned[last]], axis=1))

            @pl.loop(new_first, new_last)
            def _(i):
                mix(new_scores(i), new_turned[i])

            def mix_old(i, count):
                values = jnp.concatenate([old_turned[i + k] for k in range(count)], axis=1)
                mix(score(queries, old_rows(i, count)), values)

            @pl.loop(0, long)
            def _(i):
                mix_old(i * LONG, LONG)

            @pl.when(last % LONG == 3)
            def _():
                mix_old(long * LONG, 3)

            @pl.when(last % LONG == 2)
            def _():
                mix_old(long * LONG, 2)

            @pl.when(last % LONG == 1)
            def _():
                mix_old(long * LONG, 1)

            weight = jnp.sum(total[...], axis=0, keepdims=True)
            largest[...] = jnp.maximum(largest[...], jnp.where(own_lane, weight, 0.0))
            out = mixed[...] / weight
            side = jnp.concatenate([out[:, h * TILE : (h + 1) * TILE] for h in range(3)], axis=0)
            row = lax.broadcasted_iota(jnp.int32, side.shape, 1) + first
            mine = (row >= begin) & (row < end)
            attn_turned[t] = jnp.where(mine, side, attn_turned[t])
            return 0

        lax.fori_loop(begin // TILE, (end + TILE - 1) // TILE, tile, 0)
        if exact:
            return end, packed

        def pack(i, _):
            dst = pl.ds(pl.multiple_of(packed + i * 16, 16), 16)
            kvx_ref[dst, :] = kv_wide[pl.ds(begin + i * 16, 16), :].astype(BF16)
            return 0

        chunks = (length + 15) // 16
        lax.fori_loop(0, chunks, pack, 0)
        return end, packed + chunks * 16

    kv_wide[pl.ds(tokens, 16), :] = jnp.zeros((16, 128), F32)
    kvx_ref[...] = jnp.zeros_like(kvx_ref)
    attn_turned[...] = jnp.zeros_like(attn_turned)
    largest[...] = jnp.zeros_like(largest)
    lax.fori_loop(0, 4, functools.partial(prompt, exact=False), (0, 0))

    @pl.when(jnp.logical_not(jnp.max(largest[...]) < 2.0**64))
    def _():
        lax.fori_loop(0, 4, functools.partial(prompt, exact=True), (0, 0))

    @pl.loop(0, tokens // TILE)
    def _(t):
        attn_ref[pl.ds(pl.multiple_of(t * TILE, TILE), TILE), :] = attn_turned[t].T.astype(BF16)

    expert = lax.broadcasted_iota(jnp.int32, (32, 128), 0)
    gates = jnp.zeros((32, 128), F32)
    for k in range(8):
        hit = routes_ref[k : k + 1, :] == expert
        gates = gates + jnp.where(hit, gates_ref[k : k + 1, :].astype(F32), 0.0)
    kvx_ref[pl.ds(GATE_ROW, 32), :] = gates.astype(BF16)

    x, z = group // 4, group % 4

    for i in range(18):
        asked, member = prompt_ref[i] // 4, prompt_ref[i] % 4
        first = ((asked // 4 - x + 4) % 4 * 4 + (asked % 4 - z + 4) % 4) * KV_ROWS
        for j in range(3):
            first = first + jnp.where(j < member, (span_ref[j, asked] + 15) // 16 * 16, 0)
        place_rows_ref[0, place_ref[i]] = first // 16
        place_rows_ref[1, place_ref[i]] = span_ref[member, asked]


def attend(q, kv, cache, routes_t, gates_t, span_t, ctx, req_prompt, cache_slot):
    tokens = q.shape[0]
    return pl.pallas_call(
        attend_kernel,
        name="attend",
        out_shape=(
            jax.ShapeDtypeStruct((tokens, 192), BF16),
            jax.ShapeDtypeStruct((KV_ROWS, 128), BF16),
            jax.ShapeDtypeStruct((2, 18), jnp.int32),
        ),
        in_specs=[vmem()] * 5 + [smem()] * 4,
        out_specs=(vmem(), vmem(), smem()),
        scratch_shapes=[
            pltpu.VMEM((tokens + 16, 128), F32),
            pltpu.VMEM((cache.shape[1] // KEYS, 64, KEYS), BF16),
            pltpu.VMEM((tokens // KEYS, 64, KEYS), BF16),
            pltpu.VMEM((tokens // TILE, 192, TILE), F32),
            pltpu.VMEM((2 * KEYS, 3 * TILE), F32),
            pltpu.VMEM((1, 3 * TILE), F32),
            pltpu.VMEM((8, 3 * TILE), F32),
            pltpu.VMEM((64, 3 * TILE), F32),
            pltpu.VMEM((1, 3 * TILE), F32),
        ],
        compiler_params=pltpu.CompilerParams(vmem_limit_bytes=VMEM_BYTES),
    )(q, kv, cache, routes_t, gates_t, span_t, ctx, req_prompt, cache_slot)


GROUPS = (
    ((0, 0), (0, 1), (0, 3), (1, 0), (3, 0)),
    ((1, 1), (1, 3), (3, 1), (3, 3)),
    ((0, 2), (2, 0)),
    ((2, 2), (2, 1), (2, 3), (1, 2), (3, 2)),
)


def slot_of(which, first, second):
    return first * 4 + second if which == 0 else second * 4 + first


class Line:
    def __init__(self, make, ssem, rsem, base, outs, passes):
        self.copies = [
            make(src, dst, ssem.at[base + i], rsem.at[base + i], to)
            for i, (src, dst, to) in enumerate(outs + passes)
        ]

    def out(self):
        self.copies[0].start()
        self.copies[1].start()

    def forward(self):
        self.copies[0].wait_recv()
        self.copies[2].start()
        self.copies[1].wait_recv()
        self.copies[3].start()

    def finish(self):
        self.copies[2].wait_recv()
        self.copies[3].wait_recv()

    def drain(self):
        for one in self.copies:
            one.wait_send()


def remote(axis):
    def make(src, dst, send, recv, to):
        return pltpu.make_async_remote_copy(
            src_ref=src, dst_ref=dst, send_sem=send, recv_sem=recv, device_id={axis: to}, device_id_type=MESH
        )

    return make


def gather_lines(buf, rows, ssem, rsem, ring):
    half, quarter = rows // 2, rows // 4
    lines = []
    for which in (0, 1):
        plus, minus = ring[which]
        plus2, minus2 = ring[1 - which]
        low = which * half

        def part(first, second, piece, which=which, low=low):
            row, count = {"all": (low, half), "a": (low, quarter), "b": (low + quarter, quarter)}[piece]
            return buf(slot_of(which, first, second), row, count)

        def along(base, at, p, m, part=part):
            return Line(
                remote("req"), ssem, rsem, base,
                [(part(*at(0), "all"), part(*at(3), "all"), p), (part(*at(0), "all"), part(*at(1), "all"), m)],
                [(part(*at(3), "a"), part(*at(2), "a"), p), (part(*at(1), "b"), part(*at(2), "b"), m)],
            )

        these = [along(which * 20, lambda k: (k, 0), plus, minus)]
        for i in range(4):
            these.append(along(which * 20 + 4 + 4 * i, lambda k, i=i: (i, k), plus2, minus2))
        lines.append(these)
    return lines


def gather_steps(lines):
    def both(*steps):
        for one in lines:
            for index, name in steps:
                getattr(one[index], name)()

    return [
        lambda: both((0, "out"), (1, "out")),
        lambda: both((0, "forward"), (4, "out"), (2, "out")),
        lambda: both((1, "forward")),
        lambda: both((0, "finish"), (3, "out")),
        lambda: both((4, "forward"), (2, "forward")),
        lambda: both((1, "finish")),
        lambda: both((3, "forward")),
        lambda: both((4, "finish"), (2, "finish")),
        lambda: both((3, "finish")),
        lambda: [line.drain() for one in lines for line in one],
    ]


def finish_kernel(
    attn_ref, wout_ref, hidden_ref, gain_ref, kvx_ref, place_ref, wgu_hbm, wd_hbm,
    out_ref, cache_hbm,
    wgu, wd, part, pin, head_half, head_full, kept, resid, kvall, rows_in, sums, red_half, red_full,
    gates, ranks, picked, acts, outs, staged,
    wsem, csem, hssem, hrsem, kssem, krsem, assem, arsem, rssem, rrsem,
):
    width = hidden_ref.shape[1]
    r = lax.axis_index("req")
    x, z = r // 4, r % 4
    xp, xm = ((x + 1) % 4) * 4 + z, ((x + 3) % 4) * 4 + z
    zp, zm = x * 4 + (z + 1) % 4, x * 4 + (z + 3) % 4
    ring = ((xp, xm), (zp, zm))
    y, c, partner, up, down = head_neighbours()
    wait_all = greet(
        [("head", partner), ("head", up), ("head", down), ("req", xp), ("req", xm), ("req", zp), ("req", zm)]
    )
    loads = [
        pltpu.make_async_copy(wgu_hbm, wgu, wsem.at[0]),
        pltpu.make_async_copy(wd_hbm, wd, wsem.at[1]),
        pltpu.make_async_copy(kvx_ref, kvall.at[pl.ds(0, KV_ROWS), :], wsem.at[2]),
    ]
    loads[2].start()
    for one in loads[:2]:
        one.start()
    kvall[pl.ds(16 * KV_ROWS, 512), :] = jnp.zeros((512, 128), BF16)
    loads[2].wait()
    wait_all()

    kv_lines = gather_lines(
        lambda slot, row, count: kvall.at[pl.ds(slot * KV_ROWS + row, count), :], KV_ROWS, kssem, krsem, ring
    )
    kv_steps = gather_steps(kv_lines)
    row_lines = gather_lines(
        lambda slot, row, count: rows_in.at[slot, pl.ds(row, count), :], 128, assem, arsem, ring
    )
    row_steps = gather_steps(row_lines)
    kv_steps[0]()

    def project(dy, dc, store):
        target = ((y + dy) % 4) * 2 + (c + dc) % 2
        own = attn_ref[pl.ds(pl.multiple_of(target * 128, 128), 128), :]

        @pl.loop(0, width // 256)
        def _(n):
            cols = pl.ds(pl.multiple_of(n * 256, 256), 256)
            store(cols, jnp.dot(own, wout_ref[:, cols], preferred_element_type=F32))

    make = remote("head")
    low, high = pl.ds(0, 64), pl.ds(64, 64)
    to_partner = [
        make(part.at[2 * dy + 1], pin.at[dy], hssem.at[dy], hrsem.at[dy], partner) for dy in range(4)
    ]

    def ring_copy(i, src, dst, to):
        return make(src, dst, hssem.at[4 + i], hrsem.at[4 + i], to)

    far = (
        ring_copy(0, part.at[4, low], head_half.at[0], up),
        ring_copy(1, part.at[4, high], head_half.at[1], down),
    )
    free = (
        ring_copy(2, part.at[2, high], head_full.at[0, high], up),
        ring_copy(3, part.at[6, low], head_full.at[1, low], down),
    )
    bound = (
        ring_copy(4, part.at[2, low], head_full.at[0, low], up),
        ring_copy(5, part.at[6, high], head_full.at[1, high], down),
    )

    def give(dy):
        def store(cols, total):
            part[2 * dy + 1, :, cols] = total.astype(BF16)

        project(dy, 1, store)
        to_partner[dy].start()

    def keep(k, dy):
        def store(cols, total):
            kept[k, :, cols] = total + hidden_ref[:, cols].astype(F32) if dy == 0 else total

        project(dy, 0, store)

    def sum_rows(k, dy, index, first, half=None):
        @pl.loop(0, 4)
        def _(n):
            at = pl.ds(pl.multiple_of(first + n * 16, 16), 16)
            total = kept[k, at, :] + pin[dy, at, :].astype(F32)
            if half is not None:
                total = total + head_half[half, pl.ds(pl.multiple_of(n * 16, 16), 16), :].astype(F32)
            part[index, at, :] = total.astype(BF16)

    give(2)
    give(1)
    give(3)
    to_partner[2].wait_recv()

    def store_far(cols, total):
        part[4, :, cols] = (total + pin[2, :, cols].astype(F32)).astype(BF16)

    project(2, 0, store_far)
    far[0].start()
    far[1].start()
    keep(0, 1)
    to_partner[1].wait_recv()
    sum_rows(0, 1, 2, 64)
    free[0].start()
    keep(1, 3)
    to_partner[3].wait_recv()
    sum_rows(1, 3, 6, 0)
    free[1].start()
    give(0)
    keep(2, 0)
    kv_steps[1]()
    far[0].wait_recv()
    sum_rows(0, 1, 2, 0, 0)
    bound[0].start()
    far[1].wait_recv()
    sum_rows(1, 3, 6, 64, 1)
    bound[1].start()
    kv_steps[2]()
    kv_steps[3]()
    kv_steps[4]()
    to_partner[0].wait_recv()
    for one in free + bound:
        one.wait_recv()

    @pl.loop(0, 8, unroll=2)
    def _(n):
        at = pl.ds(pl.multiple_of(n * 16, 16), 16)
        total = kept[2, at, :] + pin[0, at, :].astype(F32)
        total = total + head_full[0, at, :].astype(F32) + head_full[1, at, :].astype(F32)
        resid[at, :] = total
        rows_in[0, at, :] = rms(total, gain_ref[...].reshape(1, -1)).astype(BF16)

    row_steps[0]()
    kv_steps[5]()
    kv_steps[6]()
    expert = lax.broadcasted_iota(jnp.int32, (32, 128), 0)
    before = lax.broadcasted_iota(jnp.int32, (128, 128), 0) < lax.broadcasted_iota(jnp.int32, (128, 128), 1)
    order = jnp.where(before, 1.0, 0.0).astype(BF16)

    def read_gates(slots):
        for slot in slots:
            table = kvall[slot * KV_ROWS + GATE_ROW : slot * KV_ROWS + GATE_ROW + 32, :].astype(F32)
            for j in range(2):
                mine = jnp.sum(jnp.where(expert == r * 2 + j, table, 0.0), axis=0, keepdims=True)
                gates[slot * 2 + j : slot * 2 + j + 1, :] = mine
        hits = jnp.where(gates[...] > 0.0, 1.0, 0.0).astype(BF16)
        ranks[...] = jnp.dot(hits, order, preferred_element_type=F32)

    def chosen(slot, weighted):
        place = lax.broadcasted_iota(jnp.int32, (CAP, 128), 0).astype(F32)
        maps = []
        for j in range(2):
            gate = gates[slot * 2 + j : slot * 2 + j + 1, :]
            value = gate if weighted else 1.0
            hit = (ranks[slot * 2 + j : slot * 2 + j + 1, :] == place) & (gate > 0.0)
            maps.append(jnp.where(hit, value, 0.0))
        return jnp.concatenate(maps, axis=0).astype(BF16)

    def experts(group):
        count = len(group) * CAP
        for k, (a, b) in enumerate(group):
            slot = a * 4 + b
            select = chosen(slot, False)

            @pl.loop(0, width // 512, unroll=width // 512)
            def _(n, k=k, slot=slot, select=select):
                cols = pl.ds(pl.multiple_of(n * 512, 512), 512)
                got = jnp.dot(select, rows_in[slot, :, cols], preferred_element_type=F32).astype(BF16)
                picked[0, pl.ds(k * CAP, CAP), cols] = got[:CAP]
                picked[1, pl.ds(k * CAP, CAP), cols] = got[CAP:]

        @pl.loop(0, 2)
        def _(e):
            @pl.loop(0, 2)
            def _(n):
                cols = pl.ds(pl.multiple_of(n * 256, 256), 256)
                later = pl.ds(pl.multiple_of(n * 256 + 512, 256), 256)
                own = picked[e, pl.ds(0, count), :]
                gate = jnp.dot(own, wgu[e, :, cols], preferred_element_type=F32)
                lift = jnp.dot(own, wgu[e, :, later], preferred_element_type=F32)
                acts[pl.ds(0, count), cols] = (gate / (1.0 + jnp.exp(-gate)) * lift).astype(BF16)

            @pl.loop(0, width // 256, unroll=2)
            def _(n):
                cols = pl.ds(pl.multiple_of(n * 256, 256), 256)
                outs[e, pl.ds(0, count), cols] = jnp.dot(
                    acts[pl.ds(0, count), :], wd[e, :, cols], preferred_element_type=F32
                ).astype(BF16)

        for k, (a, b) in enumerate(group):
            slot = a * 4 + b
            spread = chosen(slot, True)

            @pl.loop(0, width // 512, unroll=width // 512)
            def _(n, k=k, slot=slot, spread=spread):
                cols = pl.ds(pl.multiple_of(n * 512, 512), 512)
                given = jnp.concatenate(
                    [outs[0, pl.ds(k * CAP, CAP), cols], outs[1, pl.ds(k * CAP, CAP), cols]], axis=0
                )
                sums[slot, :, cols] = lax.dot_general(
                    spread, given, (((0,), (0,)), ((), ())), preferred_element_type=F32
                ).astype(BF16)

    store = pltpu.make_async_copy(staged, cache_hbm, csem.at[0])

    def fill_cache():
        @pl.loop(0, 18)
        def _(s):
            start, length = place_ref[0, s], place_ref[1, s]
            for i in range(4):
                rows = kvall[pl.ds(start * 16 + i * 128, 128), :].astype(F32)
                at = lax.broadcasted_iota(jnp.int32, (128, 128), 0) + i * 128
                staged[s, pl.ds(i * 128, 128), :] = jnp.where(at < length, rows, 0.0).astype(BF16)

        store.start()

    def add(dst, row, src, count):
        @pl.loop(0, count // 16)
        def _(i):
            to = pl.ds(pl.multiple_of(row + i * 16, 16), 16)
            at = pl.ds(pl.multiple_of(i * 16, 16), 16)
            total = sums[dst, to, :].astype(F32)
            for one in src:
                total = total + one[at, :].astype(F32)
            sums[dst, to, :] = total.astype(BF16)

    def reduce_line(n, which, at, plus, minus):
        base = which * 64
        send = remote("req")

        def piece(k, row, count):
            return sums.at[at(k), pl.ds(base + row, count), :]

        def copy(i, src, dst, to):
            return send(src, dst, rssem.at[6 * n + i], rrsem.at[6 * n + i], to)

        first, second = pl.ds(0, 32), pl.ds(32, 32)
        copies = [
            copy(0, piece(2, 0, 32), red_half.at[n, 0], plus),
            copy(1, piece(2, 32, 32), red_half.at[n, 1], minus),
            copy(2, piece(1, 32, 32), red_full.at[n, 0, second], plus),
            copy(3, piece(3, 0, 32), red_full.at[n, 1, first], minus),
            copy(4, piece(1, 0, 32), red_full.at[n, 0, first], plus),
            copy(5, piece(3, 32, 32), red_full.at[n, 1, second], minus),
        ]

        def far():
            copies[0].start()
            copies[1].start()

        def near():
            copies[2].start()
            copies[3].start()

        def middle():
            copies[0].wait_recv()
            add(at(1), base, [red_half.at[n, 0]], 32)
            copies[4].start()
            copies[1].wait_recv()
            add(at(3), base + 32, [red_half.at[n, 1]], 32)
            copies[5].start()

        def last():
            for one in copies[2:]:
                one.wait_recv()

        def fold():
            last()
            add(at(0), base, [red_full.at[n, 0], red_full.at[n, 1]], 64)

        def drain():
            for one in copies:
                one.wait_send()

        return {"far": far, "near": near, "middle": middle, "fold": fold, "last": last, "drain": drain}

    back = []
    for which in (0, 1):
        plus, minus = ring[which]
        plus2, minus2 = ring[1 - which]
        these = [
            reduce_line(which * 5 + i, which, lambda k, i=i, w=which: slot_of(w, i, k), plus2, minus2)
            for i in range(4)
        ]
        these.append(reduce_line(which * 5 + 4, which, lambda k, w=which: slot_of(w, k, 0), plus, minus))
        back.append(these)

    def go(line, step):
        for these in back:
            these[line][step]()

    near = [a * 4 + b for a, b in GROUPS[0]]
    gates[...] = jnp.zeros_like(gates)
    read_gates(near)
    for one in loads[:2]:
        one.wait()
    row_steps[1]()
    row_steps[2]()
    experts(GROUPS[0])
    kv_steps[7]()
    kv_steps[8]()
    row_steps[3]()
    row_steps[4]()
    read_gates([slot for slot in range(16) if slot not in near])

    experts(GROUPS[1])
    row_steps[5]()
    row_steps[6]()
    experts(GROUPS[2])
    row_steps[7]()
    go(0, "far")
    go(0, "near")
    row_steps[8]()
    experts(GROUPS[3])
    go(0, "middle")
    for line, step in (
        (2, "far"), (2, "near"), (1, "far"), (1, "near"), (3, "far"), (3, "near"), (0, "fold"), (2, "middle"),
        (1, "middle"), (3, "middle"),
    ):
        go(line, step)
    fill_cache()
    for line, step in (
        (2, "fold"), (4, "far"), (1, "fold"), (3, "fold"), (4, "near"), (4, "middle"), (4, "last"),
    ):
        go(line, step)
    for which, n in ((0, 4), (1, 9)):
        @pl.loop(0, 4)
        def _(i, which=which, n=n):
            to = pl.ds(pl.multiple_of(which * 64 + i * 16, 16), 16)
            at = pl.ds(pl.multiple_of(i * 16, 16), 16)
            total = resid[to, :] + sums[0, to, :].astype(F32)
            total = total + red_full[n, 0, at, :].astype(F32) + red_full[n, 1, at, :].astype(F32)
            out_ref[to, :] = total.astype(BF16)

    for one in (*to_partner, *far, *free, *bound):
        one.wait_send()
    kv_steps[9]()
    row_steps[9]()
    for line in range(5):
        go(line, "drain")
    store.wait()


def finish(attn, w_out, hidden, gain, kvx, place_rows, w_gate_up, w_down):
    rows, width = hidden.shape
    most = max(len(group) for group in GROUPS) * CAP
    return pl.pallas_call(
        finish_kernel,
        name="finish",
        out_shape=(
            jax.ShapeDtypeStruct((rows, width), BF16),
            jax.ShapeDtypeStruct((18, 512, 128), BF16),
        ),
        in_specs=[vmem()] * 5 + [smem()] + [anyspace()] * 2,
        out_specs=(vmem(), anyspace()),
        scratch_shapes=[
            pltpu.VMEM(w_gate_up.shape, BF16),
            pltpu.VMEM(w_down.shape, BF16),
            pltpu.VMEM((8, rows, width), BF16),
            pltpu.VMEM((4, rows, width), BF16),
            pltpu.VMEM((2, rows // 2, width), BF16),
            pltpu.VMEM((2, rows, width), BF16),
            pltpu.VMEM((3, rows, width), F32),
            pltpu.VMEM((rows, width), F32),
            pltpu.VMEM((16 * KV_ROWS + 512, 128), BF16),
            pltpu.VMEM((16, rows, width), BF16),
            pltpu.VMEM((16, rows, width), BF16),
            pltpu.VMEM((10, 2, rows // 4, width), BF16),
            pltpu.VMEM((10, 2, rows // 2, width), BF16),
            pltpu.VMEM((32, 128), F32),
            pltpu.VMEM((32, 128), F32),
            pltpu.VMEM((2, most, width), BF16),
            pltpu.VMEM((most, w_down.shape[1]), BF16),
            pltpu.VMEM((2, most, width), BF16),
            pltpu.VMEM((18, 512, 128), BF16),
            pltpu.SemaphoreType.DMA((3,)),
            pltpu.SemaphoreType.DMA((1,)),
            pltpu.SemaphoreType.DMA((10,)),
            pltpu.SemaphoreType.DMA((10,)),
            pltpu.SemaphoreType.DMA((40,)),
            pltpu.SemaphoreType.DMA((40,)),
            pltpu.SemaphoreType.DMA((40,)),
            pltpu.SemaphoreType.DMA((40,)),
            pltpu.SemaphoreType.DMA((60,)),
            pltpu.SemaphoreType.DMA((60,)),
        ],
        compiler_params=pltpu.CompilerParams(
            collective_id=1, has_side_effects=True, vmem_limit_bytes=VMEM_BYTES
        ),
    )(attn, w_out, hidden, gain, kvx, place_rows, w_gate_up, w_down)


def emit_kernel(rows_hbm, cache_hbm, rows_out, cache_out, rows_buf, cache_buf, rsem, wsem):
    ways = [(rows_hbm, rows_buf, rows_out)]
    for i in range(6):
        some = pl.ds(3 * i, 3)
        ways.append((cache_hbm.at[some], cache_buf.at[some], cache_out.at[some]))
    reads = [pltpu.make_async_copy(a, b, rsem.at[i]) for i, (a, b, _) in enumerate(ways)]
    writes = [pltpu.make_async_copy(b, c, wsem.at[i]) for i, (_, b, c) in enumerate(ways)]
    for one in reads:
        one.start()
    for read, write in zip(reads, writes):
        read.wait()
        write.start()
    for one in writes:
        one.wait()


def emit(rows, cache):
    return pl.pallas_call(
        emit_kernel,
        name="emit",
        out_shape=(jax.ShapeDtypeStruct(rows.shape, BF16), jax.ShapeDtypeStruct(cache.shape, BF16)),
        in_specs=[anyspace()] * 2,
        out_specs=(anyspace(), anyspace()),
        scratch_shapes=[
            pltpu.VMEM(rows.shape, BF16),
            pltpu.VMEM(cache.shape, BF16),
            pltpu.SemaphoreType.DMA((7,)),
            pltpu.SemaphoreType.DMA((7,)),
        ],
        compiler_params=pltpu.CompilerParams(vmem_limit_bytes=16 * 1024 * 1024),
    )(rows, cache)


def body(
    hidden_in, attn_gain, w_query, keyvalue_weight, w_out, cache_kv, ctx_len, span_len,
    ffn_gain, routes, gate_weights, w_gate_up, w_down, req_prompt, cache_slot,
):
    width = hidden_in.shape[1]
    prompts_dev = cache_kv.shape[0]
    span_t = span_len.T
    freq = (ROPE_BASE ** (-2.0 * (np.arange(128) % 32) / 64.0)).astype(np.float32)[None, :]
    q, kv = project_tokens(
        hidden_in, attn_gain, w_query.T, keyvalue_weight.reshape(width, 128), freq, span_t, ctx_len
    )
    attn, kvx, place_rows = attend(
        q, kv, cache_kv.reshape(prompts_dev, -1, 128), routes.T, gate_weights.T, span_t, ctx_len,
        req_prompt, cache_slot,
    )
    layer_out, cache = finish(
        attn, w_out, hidden_in, ffn_gain, kvx, place_rows, w_gate_up, w_down
    )
    layer_out, cache = emit(layer_out, cache)
    return (layer_out, cache.reshape(18, 512, 1, 128))


def solution(mesh):
    placed = (
        P(("req", "head"), None),
        P(),
        P(None, "head"),
        P(None, "head", None),
        P("head", None),
        P("req", None, "head", None),
        P(),
        P(),
        P(),
        P(("req", "head"), None),
        P(("req", "head"), None),
        P("req", None, None),
        P("req", None, None),
        P("req"),
        P("req"),
    )
    return jax.shard_map(
        body,
        mesh=mesh,
        in_specs=placed,
        out_specs=(P(("req", "head"), None), P("req", None, "head", None)),
        check_vma=False,
    )
```

```python
import functools

import jax
import jax.numpy as jnp
import numpy as np
from jax import lax
from jax.experimental import pallas as pl
from jax.experimental.pallas import tpu as pltpu
from jax.sharding import PartitionSpec as P

CAP = 48
EPSILON = 1e-05
ROPE_BASE = 10000.0
LOG2E = 1.4426950408889634
MESH = pl.DeviceIdType.MESH
F32 = jnp.float32
BF16 = jnp.bfloat16
VMEM_BYTES = 60 * 1024 * 1024
KV_ROWS = 1152
GATE_ROW = 1088


def vmem():
    return pl.BlockSpec(memory_space=pltpu.VMEM)


def smem():
    return pl.BlockSpec(memory_space=pltpu.SMEM)


def anyspace():
    return pl.BlockSpec(memory_space=pl.ANY)


def rms(values, gain):
    mean_sq = jnp.mean(values * values, axis=-1, keepdims=True)
    return values * lax.rsqrt(mean_sq + EPSILON) * gain


def head_neighbours():
    hd = lax.axis_index("head")
    y, c = hd // 2, hd % 2
    partner = y * 2 + (1 - c)
    up = ((y + 1) % 4) * 2 + c
    down = ((y + 3) % 4) * 2 + c
    return y, c, partner, up, down


def greet(neighbours):
    barrier = pltpu.get_barrier_semaphore()
    for axis, where in neighbours:
        pl.semaphore_signal(barrier, inc=1, device_id={axis: where}, device_id_type=MESH)
    return lambda: pl.semaphore_wait(barrier, len(neighbours))


def project_kernel(
    hidden_ref, gain_ref, wq_ref, wkv_ref, freq_ref, span_ref, ctx_ref,
    q_ref, kv_ref,
    tok, wq_wide, cos_tab, sin_tab, ssem, rsem,
):
    rows = hidden_ref.shape[0]
    half = rows // 2
    group = lax.axis_index("req")
    y, c, partner, up, down = head_neighbours()
    wait_all = greet([("head", partner), ("head", up), ("head", down)])
    tok[0] = rms(hidden_ref[...].astype(F32), gain_ref[...].reshape(1, -1)).astype(BF16)
    wait_all()

    def copy(i, src, dst, to):
        return pltpu.make_async_remote_copy(
            src_ref=src, dst_ref=dst, send_sem=ssem.at[i], recv_sem=rsem.at[i],
            device_id={"head": to}, device_id_type=MESH,
        )

    low, high = pl.ds(0, half), pl.ds(half, half)
    copies = [
        copy(0, tok.at[0, low], tok.at[6, low], up),
        copy(1, tok.at[0, high], tok.at[2, high], down),
        copy(2, tok.at[0], tok.at[1], partner),
        copy(3, tok.at[6, low], tok.at[4, low], up),
        copy(4, tok.at[6], tok.at[7], partner),
        copy(5, tok.at[2, high], tok.at[4, high], down),
        copy(6, tok.at[2], tok.at[3], partner),
        copy(7, tok.at[4, low], tok.at[5, low], partner),
        copy(8, tok.at[0, high], tok.at[6, high], up),
        copy(9, tok.at[0, low], tok.at[2, low], down),
        copy(10, tok.at[4, high], tok.at[5, high], partner),
    ]
    for i in (0, 1, 8, 9, 2):
        copies[i].start()

    wq_wide[...] = jnp.zeros_like(wq_wide)
    for h in range(3):
        wq_wide[pl.ds(h * 128, 64), :] = wq_ref[pl.ds(h * 64, 64), :]

    lane = lax.broadcasted_iota(jnp.int32, (rows, 128), 1)

    @pl.loop(0, 8)
    def _(block):
        within = lax.broadcasted_iota(jnp.int32, (rows, 128), 0) + block * rows
        position = jnp.zeros((rows, 128), jnp.int32)
        begin = 0
        for j in range(4):
            shift = ctx_ref[group * 4 + j] - begin
            position = jnp.where(within >= begin, within + shift, position)
            begin = begin + span_ref[j, group]
        angles = position.astype(F32) * freq_ref[...]
        where_rows = pl.ds(pl.multiple_of(block * rows, rows), rows)
        cos_tab[where_rows, :] = jnp.where(lane < 64, jnp.cos(angles), 1.0)
        sine = jnp.sin(angles)
        sin_tab[where_rows, :] = jnp.where(lane < 32, -sine, jnp.where(lane < 64, sine, 0.0))

    def project(slot):
        block = ((y + slot // 2) % 4) * 2 + (c + slot % 2) % 2
        at = pl.ds(pl.multiple_of(block * rows, rows), rows)
        cosine, sine = cos_tab[at, :], sin_tab[at, :]

        def turn(values):
            other = jnp.where(lane < 32, pltpu.roll(values, 96, 1), pltpu.roll(values, 32, 1))
            return (values * cosine + other * sine).astype(BF16)

        own = tok[slot]
        wide = lax.dot_general(own, wq_wide[...], (((1,), (1,)), ((), ())), preferred_element_type=F32)
        for h in range(3):
            q_ref[at, h * 128 : (h + 1) * 128] = turn(wide[:, h * 128 : (h + 1) * 128])
        kv_ref[at, :] = turn(jnp.dot(own, wkv_ref[...], preferred_element_type=F32))

    copies[0].wait_recv()
    copies[3].start()
    copies[1].wait_recv()
    copies[5].start()
    project(0)
    copies[2].wait_recv()
    project(1)
    copies[8].wait_recv()
    copies[4].start()
    copies[9].wait_recv()
    copies[6].start()
    project(6)
    project(2)
    copies[3].wait_recv()
    copies[7].start()
    copies[5].wait_recv()
    copies[10].start()
    copies[4].wait_recv()
    project(7)
    copies[6].wait_recv()
    project(3)
    project(4)
    copies[7].wait_recv()
    copies[10].wait_recv()
    project(5)
    for one in copies:
        one.wait_send()


def project_tokens(hidden, gain, wq_t, wkv, freq, span_t, ctx):
    rows, width = hidden.shape
    tokens = rows * 8
    return pl.pallas_call(
        project_kernel,
        name="project_tokens",
        out_shape=(
            jax.ShapeDtypeStruct((tokens, 384), BF16),
            jax.ShapeDtypeStruct((tokens, 128), BF16),
        ),
        in_specs=[vmem()] * 5 + [smem()] * 2,
        out_specs=(vmem(), vmem()),
        scratch_shapes=[
            pltpu.VMEM((8, rows, width), BF16),
            pltpu.VMEM((384, width), BF16),
            pltpu.VMEM((tokens, 128), F32),
            pltpu.VMEM((tokens, 128), F32),
            pltpu.SemaphoreType.DMA((11,)),
            pltpu.SemaphoreType.DMA((11,)),
        ],
        compiler_params=pltpu.CompilerParams(
            collective_id=0, has_side_effects=True, vmem_limit_bytes=VMEM_BYTES
        ),
    )(hidden, gain, wq_t, wkv, freq, span_t, ctx)


KEYS = 256
LONG = 4
TILE = 128


def attend_kernel(
    q_ref, kv_ref, cache_ref, routes_ref, gates_ref, span_ref, ctx_ref, prompt_ref, place_ref,
    attn_ref, kvx_ref, place_rows_ref,
    kv_wide, old_turned, new_turned, attn_turned, near, top, total, mixed, largest,
):
    group = lax.axis_index("req")
    tokens = q_ref.shape[0]
    kv_wide[pl.ds(0, tokens), :] = kv_ref[...].astype(F32)
    scale = LOG2E / 8.0

    def score(queries, keys):
        return lax.dot_general(keys, queries, (((1,), (1,)), ((), ())), preferred_element_type=F32)

    def mix(scores, values):
        probs = jnp.exp2(scores * scale - top[...])
        total[...] += jnp.sum(probs.reshape(-1, 8, probs.shape[1]), axis=0)
        mixed[...] += jnp.dot(values, probs.astype(BF16), preferred_element_type=F32)

    def new_rows(i):
        return kv_ref[pl.ds(pl.multiple_of(i * KEYS, KEYS), KEYS), :]

    @pl.loop(0, tokens // KEYS)
    def _(i):
        new_turned[i] = new_rows(i).T[64:, :]

    def prompt(j, carry, exact):
        begin, packed = carry
        length = span_ref[j, group]
        end = begin + length
        ctx = ctx_ref[group * 4 + j]
        last = (ctx - 1) // KEYS
        long = last // LONG
        new_first = begin // KEYS

        def old_rows(i, count):
            return cache_ref[j, pl.ds(pl.multiple_of(i * KEYS, KEYS), count * KEYS), :]

        @pl.loop(0, last + 1)
        def _(i):
            old_turned[i] = old_rows(i, 1).T[64:, :]

        def tile(t, _):
            first = pl.multiple_of(t * TILE, TILE)
            at = pl.ds(first, TILE)
            queries = jnp.concatenate([q_ref[at, h * 128 : (h + 1) * 128] for h in range(3)], axis=0)
            lane_row = lax.broadcasted_iota(jnp.int32, (1, 3 * TILE), 1) % TILE + first
            own_lane = (lane_row >= begin) & (lane_row < end)
            new_last = (first + TILE - 1) // KEYS

            def new_scores(i):
                scores = score(queries, new_rows(i))
                key = lax.broadcasted_iota(jnp.int32, (KEYS, TILE), 0) + i * KEYS
                row = lax.broadcasted_iota(jnp.int32, (KEYS, TILE), 1) + first
                bias = jnp.where((key >= begin) & (key <= row), 0.0, -1e30)
                return scores + jnp.concatenate([bias] * 3, axis=1)

            def higher(scores):
                return jnp.max(scores, axis=0, keepdims=True)

            scores = score(queries, old_rows(last, 1))
            key = lax.broadcasted_iota(jnp.int32, scores.shape, 0)
            near[pl.ds(KEYS, KEYS), :] = jnp.where(key < ctx - last * KEYS, scores, -1e30)
            near[pl.ds(0, KEYS), :] = new_scores(new_last)
            most = higher(near[...])
            if exact:
                most = lax.fori_loop(new_first, new_last, lambda i, m: jnp.maximum(m, higher(new_scores(i))), most)
                most = lax.fori_loop(
                    0, last, lambda i, m: jnp.maximum(m, higher(score(queries, old_rows(i, 1)))), most
                )
            top[...] = jnp.where(own_lane, most * scale, 1e30)
            total[...] = jnp.zeros_like(total)
            mixed[...] = jnp.zeros_like(mixed)
            mix(near[...], jnp.concatenate([new_turned[new_last], old_turned[last]], axis=1))

            @pl.loop(new_first, new_last)
            def _(i):
                mix(new_scores(i), new_turned[i])

            def mix_old(i, count):
                values = jnp.concatenate([old_turned[i + k] for k in range(count)], axis=1)
                mix(score(queries, old_rows(i, count)), values)

            @pl.loop(0, long)
            def _(i):
                mix_old(i * LONG, LONG)

            @pl.when(last % LONG == 3)
            def _():
                mix_old(long * LONG, 3)

            @pl.when(last % LONG == 2)
            def _():
                mix_old(long * LONG, 2)

            @pl.when(last % LONG == 1)
            def _():
                mix_old(long * LONG, 1)

            weight = jnp.sum(total[...], axis=0, keepdims=True)
            largest[...] = jnp.maximum(largest[...], jnp.where(own_lane, weight, 0.0))
            out = mixed[...] / weight
            side = jnp.concatenate([out[:, h * TILE : (h + 1) * TILE] for h in range(3)], axis=0)
            row = lax.broadcasted_iota(jnp.int32, side.shape, 1) + first
            mine = (row >= begin) & (row < end)
            attn_turned[t] = jnp.where(mine, side, attn_turned[t])
            return 0

        lax.fori_loop(begin // TILE, (end + TILE - 1) // TILE, tile, 0)
        if exact:
            return end, packed

        def pack(i, _):
            dst = pl.ds(pl.multiple_of(packed + i * 16, 16), 16)
            kvx_ref[dst, :] = kv_wide[pl.ds(begin + i * 16, 16), :].astype(BF16)
            return 0

        chunks = (length + 15) // 16
        lax.fori_loop(0, chunks, pack, 0)
        return end, packed + chunks * 16

    kv_wide[pl.ds(tokens, 16), :] = jnp.zeros((16, 128), F32)
    kvx_ref[...] = jnp.zeros_like(kvx_ref)
    attn_turned[...] = jnp.zeros_like(attn_turned)
    largest[...] = jnp.zeros_like(largest)
    lax.fori_loop(0, 4, functools.partial(prompt, exact=False), (0, 0))

    @pl.when(jnp.logical_not(jnp.max(largest[...]) < 2.0**64))
    def _():
        lax.fori_loop(0, 4, functools.partial(prompt, exact=True), (0, 0))

    @pl.loop(0, tokens // TILE)
    def _(t):
        attn_ref[pl.ds(pl.multiple_of(t * TILE, TILE), TILE), :] = attn_turned[t].T.astype(BF16)

    expert = lax.broadcasted_iota(jnp.int32, (32, 128), 0)
    gates = jnp.zeros((32, 128), F32)
    for k in range(8):
        hit = routes_ref[k : k + 1, :] == expert
        gates = gates + jnp.where(hit, gates_ref[k : k + 1, :].astype(F32), 0.0)
    kvx_ref[pl.ds(GATE_ROW, 32), :] = gates.astype(BF16)

    x, z = group // 4, group % 4

    for i in range(18):
        asked, member = prompt_ref[i] // 4, prompt_ref[i] % 4
        first = ((asked // 4 - x + 4) % 4 * 4 + (asked % 4 - z + 4) % 4) * KV_ROWS
        for j in range(3):
            first = first + jnp.where(j < member, (span_ref[j, asked] + 15) // 16 * 16, 0)
        place_rows_ref[0, place_ref[i]] = first // 16
        place_rows_ref[1, place_ref[i]] = span_ref[member, asked]


def attend(q, kv, cache, routes_t, gates_t, span_t, ctx, req_prompt, cache_slot):
    tokens = q.shape[0]
    return pl.pallas_call(
        attend_kernel,
        name="attend",
        out_shape=(
            jax.ShapeDtypeStruct((tokens, 192), BF16),
            jax.ShapeDtypeStruct((KV_ROWS, 128), BF16),
            jax.ShapeDtypeStruct((2, 18), jnp.int32),
        ),
        in_specs=[vmem()] * 5 + [smem()] * 4,
        out_specs=(vmem(), vmem(), smem()),
        scratch_shapes=[
            pltpu.VMEM((tokens + 16, 128), F32),
            pltpu.VMEM((cache.shape[1] // KEYS, 64, KEYS), BF16),
            pltpu.VMEM((tokens // KEYS, 64, KEYS), BF16),
            pltpu.VMEM((tokens // TILE, 192, TILE), F32),
            pltpu.VMEM((2 * KEYS, 3 * TILE), F32),
            pltpu.VMEM((1, 3 * TILE), F32),
            pltpu.VMEM((8, 3 * TILE), F32),
            pltpu.VMEM((64, 3 * TILE), F32),
            pltpu.VMEM((1, 3 * TILE), F32),
        ],
        compiler_params=pltpu.CompilerParams(vmem_limit_bytes=VMEM_BYTES),
    )(q, kv, cache, routes_t, gates_t, span_t, ctx, req_prompt, cache_slot)


GROUPS = (
    ((0, 0), (0, 1), (0, 3), (1, 0), (3, 0)),
    ((1, 1), (1, 3), (3, 1), (3, 3)),
    ((0, 2), (2, 0)),
    ((2, 2), (2, 1), (2, 3), (1, 2), (3, 2)),
)


def slot_of(which, first, second):
    return first * 4 + second if which == 0 else second * 4 + first


class Line:
    def __init__(self, make, ssem, rsem, base, outs, passes):
        self.copies = [
            make(src, dst, ssem.at[base + i], rsem.at[base + i], to)
            for i, (src, dst, to) in enumerate(outs + passes)
        ]

    def out(self):
        self.copies[0].start()
        self.copies[1].start()

    def forward(self):
        self.copies[0].wait_recv()
        self.copies[2].start()
        self.copies[1].wait_recv()
        self.copies[3].start()

    def finish(self):
        self.copies[2].wait_recv()
        self.copies[3].wait_recv()

    def drain(self):
        for one in self.copies:
            one.wait_send()


def remote(axis):
    def make(src, dst, send, recv, to):
        return pltpu.make_async_remote_copy(
            src_ref=src, dst_ref=dst, send_sem=send, recv_sem=recv, device_id={axis: to}, device_id_type=MESH
        )

    return make


def gather_lines(buf, rows, ssem, rsem, ring):
    half, quarter = rows // 2, rows // 4
    lines = []
    for which in (0, 1):
        plus, minus = ring[which]
        plus2, minus2 = ring[1 - which]
        low = which * half

        def part(first, second, piece, which=which, low=low):
            row, count = {"all": (low, half), "a": (low, quarter), "b": (low + quarter, quarter)}[piece]
            return buf(slot_of(which, first, second), row, count)

        def along(base, at, p, m, part=part):
            return Line(
                remote("req"), ssem, rsem, base,
                [(part(*at(0), "all"), part(*at(3), "all"), p), (part(*at(0), "all"), part(*at(1), "all"), m)],
                [(part(*at(3), "a"), part(*at(2), "a"), p), (part(*at(1), "b"), part(*at(2), "b"), m)],
            )

        these = [along(which * 20, lambda k: (k, 0), plus, minus)]
        for i in range(4):
            these.append(along(which * 20 + 4 + 4 * i, lambda k, i=i: (i, k), plus2, minus2))
        lines.append(these)
    return lines


def gather_steps(lines):
    def both(*steps):
        for one in lines:
            for index, name in steps:
                getattr(one[index], name)()

    return [
        lambda: both((0, "out"), (1, "out")),
        lambda: both((0, "forward"), (4, "out"), (2, "out")),
        lambda: both((1, "forward")),
        lambda: both((0, "finish"), (3, "out")),
        lambda: both((4, "forward"), (2, "forward")),
        lambda: both((1, "finish")),
        lambda: both((3, "forward")),
        lambda: both((4, "finish"), (2, "finish")),
        lambda: both((3, "finish")),
        lambda: [line.drain() for one in lines for line in one],
    ]


def finish_kernel(
    attn_ref, wout_ref, hidden_ref, gain_ref, kvx_ref, place_ref, wgu_hbm, wd_hbm,
    out_ref, cache_hbm,
    wgu, wd, part, pin, head_half, head_full, kept, resid, kvall, rows_in, sums, red_half, red_full,
    gates, ranks, picked, acts, outs, staged,
    wsem, csem, hssem, hrsem, kssem, krsem, assem, arsem, rssem, rrsem,
):
    width = hidden_ref.shape[1]
    r = lax.axis_index("req")
    x, z = r // 4, r % 4
    xp, xm = ((x + 1) % 4) * 4 + z, ((x + 3) % 4) * 4 + z
    zp, zm = x * 4 + (z + 1) % 4, x * 4 + (z + 3) % 4
    ring = ((xp, xm), (zp, zm))
    y, c, partner, up, down = head_neighbours()
    wait_all = greet(
        [("head", partner), ("head", up), ("head", down), ("req", xp), ("req", xm), ("req", zp), ("req", zm)]
    )
    loads = [
        pltpu.make_async_copy(wgu_hbm, wgu, wsem.at[0]),
        pltpu.make_async_copy(wd_hbm, wd, wsem.at[1]),
        pltpu.make_async_copy(kvx_ref, kvall.at[pl.ds(0, KV_ROWS), :], wsem.at[2]),
    ]
    loads[2].start()
    for one in loads[:2]:
        one.start()
    kvall[pl.ds(16 * KV_ROWS, 512), :] = jnp.zeros((512, 128), BF16)
    loads[2].wait()
    wait_all()

    kv_lines = gather_lines(
        lambda slot, row, count: kvall.at[pl.ds(slot * KV_ROWS + row, count), :], KV_ROWS, kssem, krsem, ring
    )
    kv_steps = gather_steps(kv_lines)
    row_lines = gather_lines(
        lambda slot, row, count: rows_in.at[slot, pl.ds(row, count), :], 128, assem, arsem, ring
    )
    row_steps = gather_steps(row_lines)
    kv_steps[0]()

    def project(dy, dc, store):
        target = ((y + dy) % 4) * 2 + (c + dc) % 2
        own = attn_ref[pl.ds(pl.multiple_of(target * 128, 128), 128), :]

        @pl.loop(0, width // 256)
        def _(n):
            cols = pl.ds(pl.multiple_of(n * 256, 256), 256)
            store(cols, jnp.dot(own, wout_ref[:, cols], preferred_element_type=F32))

    make = remote("head")
    low, high = pl.ds(0, 64), pl.ds(64, 64)
    to_partner = [
        make(part.at[2 * dy + 1], pin.at[dy], hssem.at[dy], hrsem.at[dy], partner) for dy in range(4)
    ]

    def ring_copy(i, src, dst, to):
        return make(src, dst, hssem.at[4 + i], hrsem.at[4 + i], to)

    far = (
        ring_copy(0, part.at[4, low], head_half.at[0], up),
        ring_copy(1, part.at[4, high], head_half.at[1], down),
    )
    free = (
        ring_copy(2, part.at[2, high], head_full.at[0, high], up),
        ring_copy(3, part.at[6, low], head_full.at[1, low], down),
    )
    bound = (
        ring_copy(4, part.at[2, low], head_full.at[0, low], up),
        ring_copy(5, part.at[6, high], head_full.at[1, high], down),
    )

    def give(dy):
        def store(cols, total):
            part[2 * dy + 1, :, cols] = total.astype(BF16)

        project(dy, 1, store)
        to_partner[dy].start()

    def keep(k, dy):
        def store(cols, total):
            kept[k, :, cols] = total + hidden_ref[:, cols].astype(F32) if dy == 0 else total

        project(dy, 0, store)

    def sum_rows(k, dy, index, first, half=None):
        @pl.loop(0, 4)
        def _(n):
            at = pl.ds(pl.multiple_of(first + n * 16, 16), 16)
            total = kept[k, at, :] + pin[dy, at, :].astype(F32)
            if half is not None:
                total = total + head_half[half, pl.ds(pl.multiple_of(n * 16, 16), 16), :].astype(F32)
            part[index, at, :] = total.astype(BF16)

    give(2)
    give(1)
    give(3)
    to_partner[2].wait_recv()

    def store_far(cols, total):
        part[4, :, cols] = (total + pin[2, :, cols].astype(F32)).astype(BF16)

    project(2, 0, store_far)
    far[0].start()
    far[1].start()
    keep(0, 1)
    to_partner[1].wait_recv()
    sum_rows(0, 1, 2, 64)
    free[0].start()
    keep(1, 3)
    to_partner[3].wait_recv()
    sum_rows(1, 3, 6, 0)
    free[1].start()
    give(0)
    keep(2, 0)
    kv_steps[1]()
    far[0].wait_recv()
    sum_rows(0, 1, 2, 0, 0)
    bound[0].start()
    far[1].wait_recv()
    sum_rows(1, 3, 6, 64, 1)
    bound[1].start()
    kv_steps[2]()
    kv_steps[3]()
    kv_steps[4]()
    to_partner[0].wait_recv()
    for one in free + bound:
        one.wait_recv()

    @pl.loop(0, 8, unroll=2)
    def _(n):
        at = pl.ds(pl.multiple_of(n * 16, 16), 16)
        total = kept[2, at, :] + pin[0, at, :].astype(F32)
        total = total + head_full[0, at, :].astype(F32) + head_full[1, at, :].astype(F32)
        resid[at, :] = total
        rows_in[0, at, :] = rms(total, gain_ref[...].reshape(1, -1)).astype(BF16)

    row_steps[0]()
    kv_steps[5]()
    kv_steps[6]()
    expert = lax.broadcasted_iota(jnp.int32, (32, 128), 0)
    before = lax.broadcasted_iota(jnp.int32, (128, 128), 0) < lax.broadcasted_iota(jnp.int32, (128, 128), 1)
    order = jnp.where(before, 1.0, 0.0).astype(BF16)

    def read_gates(slots):
        for slot in slots:
            table = kvall[slot * KV_ROWS + GATE_ROW : slot * KV_ROWS + GATE_ROW + 32, :].astype(F32)
            for j in range(2):
                mine = jnp.sum(jnp.where(expert == r * 2 + j, table, 0.0), axis=0, keepdims=True)
                gates[slot * 2 + j : slot * 2 + j + 1, :] = mine
        hits = jnp.where(gates[...] > 0.0, 1.0, 0.0).astype(BF16)
        ranks[...] = jnp.dot(hits, order, preferred_element_type=F32)

    def chosen(slot, weighted):
        place = lax.broadcasted_iota(jnp.int32, (CAP, 128), 0).astype(F32)
        maps = []
        for j in range(2):
            gate = gates[slot * 2 + j : slot * 2 + j + 1, :]
            value = gate if weighted else 1.0
            hit = (ranks[slot * 2 + j : slot * 2 + j + 1, :] == place) & (gate > 0.0)
            maps.append(jnp.where(hit, value, 0.0))
        return jnp.concatenate(maps, axis=0).astype(BF16)

    def experts(group):
        count = len(group) * CAP
        for k, (a, b) in enumerate(group):
            slot = a * 4 + b
            select = chosen(slot, False)

            @pl.loop(0, width // 512, unroll=width // 512)
            def _(n, k=k, slot=slot, select=select):
                cols = pl.ds(pl.multiple_of(n * 512, 512), 512)
                got = jnp.dot(select, rows_in[slot, :, cols], preferred_element_type=F32).astype(BF16)
                picked[0, pl.ds(k * CAP, CAP), cols] = got[:CAP]
                picked[1, pl.ds(k * CAP, CAP), cols] = got[CAP:]

        @pl.loop(0, 2)
        def _(e):
            @pl.loop(0, 2)
            def _(n):
                cols = pl.ds(pl.multiple_of(n * 256, 256), 256)
                later = pl.ds(pl.multiple_of(n * 256 + 512, 256), 256)
                own = picked[e, pl.ds(0, count), :]
                gate = jnp.dot(own, wgu[e, :, cols], preferred_element_type=F32)
                lift = jnp.dot(own, wgu[e, :, later], preferred_element_type=F32)
                acts[pl.ds(0, count), cols] = (gate / (1.0 + jnp.exp(-gate)) * lift).astype(BF16)

            @pl.loop(0, width // 256, unroll=2)
            def _(n):
                cols = pl.ds(pl.multiple_of(n * 256, 256), 256)
                outs[e, pl.ds(0, count), cols] = jnp.dot(
                    acts[pl.ds(0, count), :], wd[e, :, cols], preferred_element_type=F32
                ).astype(BF16)

        for k, (a, b) in enumerate(group):
            slot = a * 4 + b
            spread = chosen(slot, True)

            @pl.loop(0, width // 512, unroll=width // 512)
            def _(n, k=k, slot=slot, spread=spread):
                cols = pl.ds(pl.multiple_of(n * 512, 512), 512)
                given = jnp.concatenate(
                    [outs[0, pl.ds(k * CAP, CAP), cols], outs[1, pl.ds(k * CAP, CAP), cols]], axis=0
                )
                sums[slot, :, cols] = lax.dot_general(
                    spread, given, (((0,), (0,)), ((), ())), preferred_element_type=F32
                ).astype(BF16)

    store = pltpu.make_async_copy(staged, cache_hbm, csem.at[0])

    def fill_cache():
        @pl.loop(0, 18)
        def _(s):
            start, length = place_ref[0, s], place_ref[1, s]
            for i in range(4):
                rows = kvall[pl.ds(start * 16 + i * 128, 128), :].astype(F32)
                at = lax.broadcasted_iota(jnp.int32, (128, 128), 0) + i * 128
                staged[s, pl.ds(i * 128, 128), :] = jnp.where(at < length, rows, 0.0).astype(BF16)

        store.start()

    def add(dst, row, src, count):
        @pl.loop(0, count // 16)
        def _(i):
            to = pl.ds(pl.multiple_of(row + i * 16, 16), 16)
            at = pl.ds(pl.multiple_of(i * 16, 16), 16)
            total = sums[dst, to, :].astype(F32)
            for one in src:
                total = total + one[at, :].astype(F32)
            sums[dst, to, :] = total.astype(BF16)

    def reduce_line(n, which, at, plus, minus):
        base = which * 64
        send = remote("req")

        def piece(k, row, count):
            return sums.at[at(k), pl.ds(base + row, count), :]

        def copy(i, src, dst, to):
            return send(src, dst, rssem.at[6 * n + i], rrsem.at[6 * n + i], to)

        first, second = pl.ds(0, 32), pl.ds(32, 32)
        copies = [
            copy(0, piece(2, 0, 32), red_half.at[n, 0], plus),
            copy(1, piece(2, 32, 32), red_half.at[n, 1], minus),
            copy(2, piece(1, 32, 32), red_full.at[n, 0, second], plus),
            copy(3, piece(3, 0, 32), red_full.at[n, 1, first], minus),
            copy(4, piece(1, 0, 32), red_full.at[n, 0, first], plus),
            copy(5, piece(3, 32, 32), red_full.at[n, 1, second], minus),
        ]

        def far():
            copies[0].start()
            copies[1].start()

        def near():
            copies[2].start()
            copies[3].start()

        def middle():
            copies[0].wait_recv()
            add(at(1), base, [red_half.at[n, 0]], 32)
            copies[4].start()
            copies[1].wait_recv()
            add(at(3), base + 32, [red_half.at[n, 1]], 32)
            copies[5].start()

        def last():
            for one in copies[2:]:
                one.wait_recv()

        def fold():
            last()
            add(at(0), base, [red_full.at[n, 0], red_full.at[n, 1]], 64)

        def drain():
            for one in copies:
                one.wait_send()

        return {"far": far, "near": near, "middle": middle, "fold": fold, "last": last, "drain": drain}

    back = []
    for which in (0, 1):
        plus, minus = ring[which]
        plus2, minus2 = ring[1 - which]
        these = [
            reduce_line(which * 5 + i, which, lambda k, i=i, w=which: slot_of(w, i, k), plus2, minus2)
            for i in range(4)
        ]
        these.append(reduce_line(which * 5 + 4, which, lambda k, w=which: slot_of(w, k, 0), plus, minus))
        back.append(these)

    def go(line, step):
        for these in back:
            these[line][step]()

    near = [a * 4 + b for a, b in GROUPS[0]]
    gates[...] = jnp.zeros_like(gates)
    read_gates(near)
    for one in loads[:2]:
        one.wait()
    row_steps[1]()
    row_steps[2]()
    experts(GROUPS[0])
    kv_steps[7]()
    kv_steps[8]()
    row_steps[3]()
    row_steps[4]()
    read_gates([slot for slot in range(16) if slot not in near])

    experts(GROUPS[1])
    row_steps[5]()
    row_steps[6]()
    experts(GROUPS[2])
    row_steps[7]()
    go(0, "far")
    go(0, "near")
    row_steps[8]()
    experts(GROUPS[3])
    go(0, "middle")
    for line, step in (
        (2, "far"), (2, "near"), (1, "far"), (1, "near"), (3, "far"), (3, "near"), (0, "fold"), (2, "middle"),
        (1, "middle"), (3, "middle"),
    ):
        go(line, step)
    fill_cache()
    for line, step in (
        (2, "fold"), (4, "far"), (1, "fold"), (3, "fold"), (4, "near"), (4, "middle"), (4, "last"),
    ):
        go(line, step)
    for which, n in ((0, 4), (1, 9)):
        @pl.loop(0, 4)
        def _(i, which=which, n=n):
            to = pl.ds(pl.multiple_of(which * 64 + i * 16, 16), 16)
            at = pl.ds(pl.multiple_of(i * 16, 16), 16)
            total = resid[to, :] + sums[0, to, :].astype(F32)
            total = total + red_full[n, 0, at, :].astype(F32) + red_full[n, 1, at, :].astype(F32)
            out_ref[to, :] = total.astype(BF16)

    for one in (*to_partner, *far, *free, *bound):
        one.wait_send()
    kv_steps[9]()
    row_steps[9]()
    for line in range(5):
        go(line, "drain")
    store.wait()


def finish(attn, w_out, hidden, gain, kvx, place_rows, w_gate_up, w_down):
    rows, width = hidden.shape
    most = max(len(group) for group in GROUPS) * CAP
    return pl.pallas_call(
        finish_kernel,
        name="finish",
        out_shape=(
            jax.ShapeDtypeStruct((rows, width), BF16),
            jax.ShapeDtypeStruct((18, 512, 128), BF16),
        ),
        in_specs=[vmem()] * 5 + [smem()] + [anyspace()] * 2,
        out_specs=(vmem(), anyspace()),
        scratch_shapes=[
            pltpu.VMEM(w_gate_up.shape, BF16),
            pltpu.VMEM(w_down.shape, BF16),
            pltpu.VMEM((8, rows, width), BF16),
            pltpu.VMEM((4, rows, width), BF16),
            pltpu.VMEM((2, rows // 2, width), BF16),
            pltpu.VMEM((2, rows, width), BF16),
            pltpu.VMEM((3, rows, width), F32),
            pltpu.VMEM((rows, width), F32),
            pltpu.VMEM((16 * KV_ROWS + 512, 128), BF16),
            pltpu.VMEM((16, rows, width), BF16),
            pltpu.VMEM((16, rows, width), BF16),
            pltpu.VMEM((10, 2, rows // 4, width), BF16),
            pltpu.VMEM((10, 2, rows // 2, width), BF16),
            pltpu.VMEM((32, 128), F32),
            pltpu.VMEM((32, 128), F32),
            pltpu.VMEM((2, most, width), BF16),
            pltpu.VMEM((most, w_down.shape[1]), BF16),
            pltpu.VMEM((2, most, width), BF16),
            pltpu.VMEM((18, 512, 128), BF16),
            pltpu.SemaphoreType.DMA((3,)),
            pltpu.SemaphoreType.DMA((1,)),
            pltpu.SemaphoreType.DMA((10,)),
            pltpu.SemaphoreType.DMA((10,)),
            pltpu.SemaphoreType.DMA((40,)),
            pltpu.SemaphoreType.DMA((40,)),
            pltpu.SemaphoreType.DMA((40,)),
            pltpu.SemaphoreType.DMA((40,)),
            pltpu.SemaphoreType.DMA((60,)),
            pltpu.SemaphoreType.DMA((60,)),
        ],
        compiler_params=pltpu.CompilerParams(
            collective_id=1, has_side_effects=True, vmem_limit_bytes=VMEM_BYTES
        ),
    )(attn, w_out, hidden, gain, kvx, place_rows, w_gate_up, w_down)


def emit_kernel(rows_hbm, cache_hbm, rows_out, cache_out, rows_buf, cache_buf, rsem, wsem):
    ways = [(rows_hbm, rows_buf, rows_out)]
    for i in range(6):
        some = pl.ds(3 * i, 3)
        ways.append((cache_hbm.at[some], cache_buf.at[some], cache_out.at[some]))
    reads = [pltpu.make_async_copy(a, b, rsem.at[i]) for i, (a, b, _) in enumerate(ways)]
    writes = [pltpu.make_async_copy(b, c, wsem.at[i]) for i, (_, b, c) in enumerate(ways)]
    for one in reads:
        one.start()
    for read, write in zip(reads, writes):
        read.wait()
        write.start()
    for one in writes:
        one.wait()


def emit(rows, cache):
    return pl.pallas_call(
        emit_kernel,
        name="emit",
        out_shape=(jax.ShapeDtypeStruct(rows.shape, BF16), jax.ShapeDtypeStruct(cache.shape, BF16)),
        in_specs=[anyspace()] * 2,
        out_specs=(anyspace(), anyspace()),
        scratch_shapes=[
            pltpu.VMEM(rows.shape, BF16),
            pltpu.VMEM(cache.shape, BF16),
            pltpu.SemaphoreType.DMA((7,)),
            pltpu.SemaphoreType.DMA((7,)),
        ],
        compiler_params=pltpu.CompilerParams(vmem_limit_bytes=VMEM_BYTES),
    )(rows, cache)


def body(
    hidden_in, attn_gain, w_query, keyvalue_weight, w_out, cache_kv, ctx_len, span_len,
    ffn_gain, routes, gate_weights, w_gate_up, w_down, req_prompt, cache_slot,
):
    width = hidden_in.shape[1]
    prompts_dev = cache_kv.shape[0]
    span_t = span_len.T
    freq = (ROPE_BASE ** (-2.0 * (np.arange(128) % 32) / 64.0)).astype(np.float32)[None, :]
    q, kv = project_tokens(
        hidden_in, attn_gain, w_query.T, keyvalue_weight.reshape(width, 128), freq, span_t, ctx_len
    )
    attn, kvx, place_rows = attend(
        q, kv, cache_kv.reshape(prompts_dev, -1, 128), routes.T, gate_weights.T, span_t, ctx_len,
        req_prompt, cache_slot,
    )
    layer_out, cache = finish(
        attn, w_out, hidden_in, ffn_gain, kvx, place_rows, w_gate_up, w_down
    )
    layer_out, cache = emit(layer_out, cache)
    return (layer_out, cache.reshape(18, 512, 1, 128))


def solution(mesh):
    placed = (
        P(("req", "head"), None),
        P(),
        P(None, "head"),
        P(None, "head", None),
        P("head", None),
        P("req", None, "head", None),
        P(),
        P(),
        P(),
        P(("req", "head"), None),
        P(("req", "head"), None),
        P("req", None, None),
        P("req", None, None),
        P("req"),
        P("req"),
    )
    return jax.shard_map(
        body,
        mesh=mesh,
        in_specs=placed,
        out_specs=(P(("req", "head"), None), P("req", None, "head", None)),
        check_vma=False,
    )
```
